32 devices in a mesh: groups: 2 (over x), seq: 16 (over z, y, core).
Axes of the slice: x: 2, y: 2, z: 4, core: 2. Of those that a mesh axis runs over, the one named last changes fastest.
Arguments:
- query_in: bfloat16 [4096, 4096], P(('groups', 'seq')), parts along dimension 0, may hold values from -6 to 6
- key_in: bfloat16 [4096, 4096], P(('groups', 'seq')), parts along dimension 0, may hold values from -6 to 6
- value_in: bfloat16 [4096, 4096], P(('groups', 'seq')), parts along dimension 0, may hold values from -6 to 6
- long_filter: bfloat16 [2048, 4096], P('seq'), may hold values from -0.4 to 0.4
- short_weight: float32 [3, 3, 4096], replicated, may hold values from -3 to 3
- skip_gain: float32 [4096], replicated, may hold values from 0.5 to 1.5
Outputs:
- gated_out: bfloat16 [4096, 4096], P(('groups', 'seq')), parts along dimension 0
The draws below stay inside these ranges and needn't reach their ends.
There are 2 independent parts, one for each index of `groups`. The reference program is written for one: setup_inputs(seed, part) draws one part's arguments, and reference() takes and returns one part's arrays. A program takes and returns all parts, laid end to end along the dimension named above; an argument that names none is the same for every part. Nothing has to cross between parts.
All inputs are finite; a program needn't handle non-finite values.
Results may differ from the reference program's by a relative error of at most 0.0052.
Values may be sent and summed in bfloat16 or wider, within the bound.
No kernel may reach another device: no remote copies, remote signals or barrier semaphores. Data moves between devices by JAX's collectives and lax.ppermute only.
A program may use at most 128 MiB of HBM per device.

```python
import math
import jax
import jax.numpy as jnp
from jax import lax

CONV_CHANNELS = 4096
TAPS = 3
SEQUENCE_LENGTH = 2048


def draw_long_filter(key, part):
    random_subkeys = jax.random.split(key, 9)
    filter_position = jnp.arange(SEQUENCE_LENGTH, dtype=jnp.float32)[:, None]
    fast_share = 0.5
    fast_mask = jax.random.bernoulli(random_subkeys[0], fast_share, (1, CONV_CHANNELS))
    slow_length = jnp.exp(jax.random.uniform(random_subkeys[1], (1, CONV_CHANNELS), jnp.float32, math.log(0.5 * SEQUENCE_LENGTH), math.log(4.0 * SEQUENCE_LENGTH)))
    fast_length = jnp.exp(jax.random.uniform(random_subkeys[2], (1, CONV_CHANNELS), jnp.float32, math.log(20.0), math.log(200.0)))
    slow_signs = jnp.where(jax.random.bernoulli(random_subkeys[3], 0.5, (1, CONV_CHANNELS)), 1.0, -1.0)
    fast_signs = jnp.where(jax.random.bernoulli(random_subkeys[7], 0.5, (1, CONV_CHANNELS)), 1.0, -1.0)
    slow_weight = jax.random.uniform(random_subkeys[8], (1, CONV_CHANNELS), jnp.float32, 0.4, 1.0)
    slow_part = slow_signs * slow_weight / jnp.sqrt(slow_length) * jnp.exp(-filter_position / slow_length)
    fast_part = jnp.where(fast_mask, fast_signs / jnp.sqrt(fast_length), 0.0) * jnp.exp(-filter_position / fast_length)
    filter_jaggedness = 1.0 + 0.25 * jnp.clip(jax.random.normal(random_subkeys[4], (SEQUENCE_LENGTH, CONV_CHANNELS), jnp.float32), -2.0, 2.0)
    spike_position = jax.random.uniform(random_subkeys[5], (3, 1, CONV_CHANNELS), jnp.float32) * SEQUENCE_LENGTH
    spike_depth = jax.random.uniform(random_subkeys[6], (3, 1, CONV_CHANNELS), jnp.float32, 0.2, 0.5)
    spike_factor = jnp.ones((SEQUENCE_LENGTH, CONV_CHANNELS), jnp.float32)
    for sudden_spike in range(3):
        spike_factor = spike_factor * jnp.where(filter_position >= spike_position[sudden_spike], 1.0 - spike_depth[sudden_spike], 1.0)
    filter_values = (slow_part + fast_part) * spike_factor * filter_jaggedness
    return filter_values.astype(jnp.float32).astype(jnp.bfloat16)


def levels(stream_key, extent, cuts, low, high):
    gain = 1.0
    for position, parts in cuts:
        steps = jax.random.uniform(jax.random.fold_in(jax.random.fold_in(stream_key, 6), position), (parts,), jnp.float32, low / len(cuts), high / len(cuts))
        gain = gain * jnp.repeat(jnp.exp(steps), extent[position] // parts).reshape((-1,) + (1,) * (len(extent) - 1 - position))
    return gain


def gaussian(own_key, shape, deviation, bound, cuts=(), kind=jnp.bfloat16):
    array = deviation * jax.random.normal(own_key, shape, jnp.float32)
    if cuts:
        array = array * levels(own_key, shape, cuts, -0.22, 0.18)
    return jnp.clip(array, -bound, bound).astype(kind)


def setup_inputs(seed: int = 0, part: int = 0) -> dict:
    seeds = jax.random.split(jax.random.key(seed), 7)
    part_keys = jax.random.split(jax.random.fold_in(seeds[6], part), 7)
    return {
        "query_in": gaussian(part_keys[0], (SEQUENCE_LENGTH, CONV_CHANNELS), 1.0, 6.0, ((0, 16),)),
        "key_in": gaussian(part_keys[1], (SEQUENCE_LENGTH, CONV_CHANNELS), 1.0, 6.0, ((0, 16),)),
        "value_in": gaussian(part_keys[2], (SEQUENCE_LENGTH, CONV_CHANNELS), 1.0, 6.0, ((0, 16),)),
        "long_filter": draw_long_filter(jax.random.fold_in(seeds[6], 71), part),
        "short_weight": gaussian(seeds[4], (3, TAPS, CONV_CHANNELS), 0.6, 3.0, (), jnp.float32),
        "skip_gain": jnp.clip(jax.random.uniform(seeds[5], (CONV_CHANNELS,), jnp.float32, 0.5, 1.5), 0.5, 1.5),
    }


def featurize(stream, taps_weight):
    rim_rows = taps_weight.shape[0] - 1
    row_count = stream.shape[0]
    padded = jnp.pad(stream.astype(jnp.float32), ((rim_rows, 0), (0, 0)))
    result = jnp.zeros(stream.shape, jnp.float32)
    for offset in range(rim_rows + 1):
        result = result + taps_weight[offset] * padded[rim_rows - offset: rim_rows - offset + row_count]
    return result


def causal_conv(signal, kernel):
    length = signal.shape[0]
    padded_length = 2 * length
    spectrum = jnp.fft.rfft(signal, n=padded_length, axis=0) * jnp.fft.rfft(kernel, n=padded_length, axis=0)
    return jnp.fft.irfft(spectrum, n=padded_length, axis=0)[:length]


def reference(query_in, key_in, value_in, long_filter, short_weight, skip_gain):
    q_short = featurize(query_in, short_weight[0])
    k_short = featurize(key_in, short_weight[1])
    v_short = featurize(value_in, short_weight[2])
    product = (k_short * v_short).astype(jnp.bfloat16)
    product_wide = lax.optimization_barrier(product).astype(jnp.float32)
    filter_wide = long_filter.astype(jnp.float32)
    channels = product.shape[1]
    block_width = min(512, channels)
    pieces = []
    for start_column in range(0, channels, block_width):
        pieces.append(causal_conv(product_wide[:, start_column:start_column + block_width],
                                  filter_wide[:, start_column:start_column + block_width]))
    convolved = jnp.concatenate(pieces, axis=1).astype(jnp.float32).astype(jnp.bfloat16)
    convolved_wide = lax.optimization_barrier(convolved).astype(jnp.float32)
    gated_out = q_short * (convolved_wide + skip_gain * product_wide)
    return gated_out.astype(jnp.bfloat16)
```

```python
import functools

import jax
import jax.numpy as jnp
import ml_dtypes
import numpy as np
from jax import lax
from jax.experimental import pallas as pl
from jax.experimental.pallas import tpu as pltpu
from jax.sharding import PartitionSpec as P

LANES = 128
BLOCK = 256
UNROLLED = 8
MIB = 1 << 20


def from_behind(value, axis):
    count = lax.axis_size(axis)
    return lax.ppermute(value, axis, [(source, source + 1) for source in range(count - 1)])


def transform_tables(block):
    numbers = np.concatenate([np.arange(0, block, 2), np.arange(1, block, 2)])
    quarter = (2 * numbers[:, None] + 1) * np.arange(block)[None, :] % (4 * block)
    angle = quarter.astype(np.float64) * (2.0 * np.pi / (4 * block))
    table = np.concatenate([np.cos(angle), -np.sin(angle)], axis=0)

    def split(values):
        high = values.astype(ml_dtypes.bfloat16)
        low = (values - high.astype(np.float64)).astype(ml_dtypes.bfloat16)
        return np.concatenate([high, low], axis=0)

    return split(table), split(table.T / block)


def shifted(values, edge, steps):
    rolled = pltpu.roll(values, steps, 0)
    row = lax.broadcasted_iota(jnp.int32, values.shape, 0)
    for place in range(steps):
        source = edge[edge.shape[0] - steps + place : edge.shape[0] - steps + place + 1]
        rolled = jnp.where(row == place, jnp.broadcast_to(source, values.shape), rolled)
    return rolled


def featurize(own, edge, taps):
    own = own.astype(jnp.float32)
    edge = edge.astype(jnp.float32)
    result = taps[0:1] * own
    for offset in range(1, taps.shape[0]):
        result = result + taps[offset : offset + 1] * shifted(own, edge, offset)
    return result


def product_kernel(width, key_ref, value_ref, edge_ref, taps_ref, out_ref):
    for part in range(key_ref.shape[1] // width):
        span = slice(part * width, (part + 1) * width)
        k_short = featurize(key_ref[:, span], edge_ref[1, :, span], taps_ref[1, :, span])
        v_short = featurize(value_ref[:, span], edge_ref[2, :, span], taps_ref[2, :, span])
        out_ref[part] = (k_short * v_short).astype(out_ref.dtype)


def products(key_in, value_in, edges, short_weight, width):
    rows, channels = key_in.shape
    span = max(width, min(channels, 1024))
    taps = short_weight.shape[1]
    return pl.pallas_call(
        functools.partial(product_kernel, width),
        out_shape=jax.ShapeDtypeStruct((channels // width, rows, width), jnp.bfloat16),
        grid=(channels // span,),
        in_specs=[
            pl.BlockSpec((rows, span), lambda i: (0, i)),
            pl.BlockSpec((rows, span), lambda i: (0, i)),
            pl.BlockSpec((3, taps - 1, span), lambda i: (0, 0, i)),
            pl.BlockSpec((3, taps, span), lambda i: (0, 0, i)),
        ],
        out_specs=pl.BlockSpec((span // width, rows, width), lambda i: (i, 0, 0)),
        cost_estimate=pl.CostEstimate(
            flops=12 * rows * channels, bytes_accessed=6 * rows * channels, transcendentals=0
        ),
    )(key_in, value_in, edges, short_weight)


def gate_kernel(width, conv_ref, product_ref, query_ref, edge_ref, taps_ref, gain_ref, out_ref):
    for part in range(query_ref.shape[1] // width):
        span = slice(part * width, (part + 1) * width)
        q_short = featurize(query_ref[:, span], edge_ref[0, :, span], taps_ref[0, :, span])
        mixed = conv_ref[part].astype(jnp.float32) + gain_ref[:, span] * product_ref[part].astype(
            jnp.float32
        )
        out_ref[:, span] = (q_short * mixed).astype(out_ref.dtype)


def gate(convolved, product, query_in, edges, short_weight, skip_gain):
    rows, channels = query_in.shape
    width = product.shape[2]
    span = max(width, min(channels, 1024))
    taps = short_weight.shape[1]
    parts = pl.BlockSpec((span // width, rows, width), lambda i: (i, 0, 0))
    return pl.pallas_call(
        functools.partial(gate_kernel, width),
        out_shape=jax.ShapeDtypeStruct((rows, channels), jnp.bfloat16),
        grid=(channels // span,),
        in_specs=[
            parts,
            parts,
            pl.BlockSpec((rows, span), lambda i: (0, i)),
            pl.BlockSpec((3, taps - 1, span), lambda i: (0, 0, i)),
            pl.BlockSpec((3, taps, span), lambda i: (0, 0, i)),
            pl.BlockSpec((1, span), lambda i: (0, i)),
        ],
        out_specs=pl.BlockSpec((rows, span), lambda i: (0, i)),
        cost_estimate=pl.CostEstimate(
            flops=9 * rows * channels, bytes_accessed=8 * rows * channels, transcendentals=0
        ),
    )(convolved, product, query_in, edges, short_weight, skip_gain.reshape(1, channels))


def spread_kernel(parts, width, group_ref, filter_ref, out_ref, sems):
    group = group_ref[0]
    copies = []
    for place in range(out_ref.shape[0]):
        start = pl.multiple_of((place * parts + group) * width, width)
        copies.append(
            pltpu.make_async_copy(
                filter_ref.at[:, pl.ds(start, width)], out_ref.at[place], sems.at[place]
            )
        )
    for copy in copies:
        copy.start()
    for copy in copies:
        copy.wait()


def spread_filter(long_filter, group, places, parts):
    rows, channels = long_filter.shape
    width = channels // (places * parts)
    return pl.pallas_call(
        functools.partial(spread_kernel, parts, width),
        out_shape=jax.ShapeDtypeStruct((places, rows, width), long_filter.dtype),
        in_specs=[
            pl.BlockSpec(memory_space=pltpu.SMEM),
            pl.BlockSpec(memory_space=pl.ANY),
        ],
        out_specs=pl.BlockSpec(memory_space=pl.ANY),
        scratch_shapes=[pltpu.SemaphoreType.DMA((places,))],
        cost_estimate=pl.CostEstimate(
            flops=0, bytes_accessed=4 * rows * places * width, transcendentals=0
        ),
    )(group.reshape(1), long_filter)


def transform(table, values):
    both = jnp.dot(table, values, preferred_element_type=jnp.float32)
    half = table.shape[0] // 2
    return both[:half] + both[half:]


def over(count, body):
    if count <= UNROLLED:
        for step in range(count):
            body(step)
    else:

        @pl.loop(0, count)
        def _(step):
            body(step)


def filter_kernel(pieces, *refs):
    group_ref, table_ref = refs[:2]
    filter_refs = refs[2 : 2 + pieces]
    out_ref = refs[2 + pieces]
    count, double, _ = out_ref.shape
    block = double // 2

    def body(step):
        start = step * block
        if not isinstance(step, int):
            start = pl.multiple_of(start, block)
        values = [ref[pl.ds(start, block), :] for ref in filter_refs]
        if pieces == 2:
            own, other = values
            first = group_ref[0] == 0
            values = [jnp.where(first, own, other), jnp.where(first, other, own)]
        joined = values[0] if pieces == 1 else jnp.concatenate(values, axis=1)
        out_ref[step] = transform(table_ref[...], joined)

    over(count, body)


def filter_spectra(pieces, group, table):
    length = pieces[0].shape[0]
    width = sum(piece.shape[1] for piece in pieces)
    block = table.shape[1]
    return pl.pallas_call(
        functools.partial(filter_kernel, len(pieces)),
        out_shape=jax.ShapeDtypeStruct((length // block, 2 * block, width), jnp.float32),
        in_specs=[pl.BlockSpec(memory_space=pltpu.SMEM)]
        + [pl.BlockSpec(memory_space=pltpu.VMEM)] * (1 + len(pieces)),
        out_specs=pl.BlockSpec(memory_space=pltpu.VMEM),
        compiler_params=pltpu.CompilerParams(vmem_limit_bytes=40 * MIB),
        cost_estimate=pl.CostEstimate(
            flops=8 * length * block * width, bytes_accessed=10 * length * width, transcendentals=0
        ),
    )(group.reshape(1), table, *pieces)


def conv_kernel(forward_ref, inverse_ref, product_ref, filter_ref, out_ref, data, mixed, last):
    count, double, width = filter_ref.shape
    block = double // 2
    tile = 8

    def piece(step):
        start = step * block
        return pl.ds(start if isinstance(step, int) else pl.multiple_of(start, block), block)

    def forward(step):
        data[step] = transform(forward_ref[...], product_ref[piece(step), :])

    def inverse(slot, step):
        values = mixed[slot]
        high = values.astype(jnp.bfloat16)
        low = (values - high.astype(jnp.float32)).astype(jnp.bfloat16)
        result = transform(inverse_ref[...], high) + jnp.dot(
            inverse_ref[:block], low, preferred_element_type=jnp.float32
        )
        out_ref[piece(step), :] = result.astype(out_ref.dtype)

    over(count, forward)
    lane_step = min(width, LANES)
    strips = [
        (sign, column)
        for sign in (1.0, -1.0)
        for column in range(0, width, lane_step)
    ]
    if count <= UNROLLED:
        for half, (sign, column) in enumerate(strips):
            base = 0 if sign > 0 else block // 2
            lanes = slice(column, column + lane_step)

            @pl.loop(0, block // 2 // tile)
            def _(index):
                real = pl.ds(pl.multiple_of(base + index * tile, tile), tile)
                imag = pl.ds(pl.multiple_of(block + base + index * tile, tile), tile)
                data_parts = [
                    (data[step, real, lanes], data[step, imag, lanes]) for step in range(count)
                ]
                filter_parts = [
                    (filter_ref[step, real, lanes], filter_ref[step, imag, lanes])
                    for step in range(count)
                ]
                before = None
                for total in range(count):
                    sum_real = sum_imag = None
                    for step in range(total + 1):
                        a, b = data_parts[step]
                        c, d = filter_parts[total - step]
                        term_real = a * c - b * d
                        term_imag = a * d + b * c
                        sum_real = term_real if step == 0 else sum_real + term_real
                        sum_imag = term_imag if step == 0 else sum_imag + term_imag
                    if before is None:
                        mixed[total, real, lanes] = sum_real
                        mixed[total, imag, lanes] = sum_imag
                    elif sign > 0:
                        mixed[total, real, lanes] = sum_real - before[1]
                        mixed[total, imag, lanes] = sum_imag + before[0]
                    else:
                        mixed[total, real, lanes] = sum_real + before[1]
                        mixed[total, imag, lanes] = sum_imag - before[0]
                    before = (sum_real, sum_imag)

        for step in range(count):
            inverse(step, step)
    else:
        last[...] = jnp.zeros_like(last)

        @pl.loop(0, count)
        def _(total):
            for sign, column in strips:
                base = 0 if sign > 0 else block // 2
                lanes = slice(column, column + lane_step)

                @pl.loop(0, block // 2 // tile)
                def _(index):
                    real = pl.ds(pl.multiple_of(base + index * tile, tile), tile)
                    imag = pl.ds(pl.multiple_of(block + base + index * tile, tile), tile)

                    def add(step, sums):
                        a, b = data[step, real, lanes], data[step, imag, lanes]
                        c = filter_ref[total - step, real, lanes]
                        d = filter_ref[total - step, imag, lanes]
                        return sums[0] + (a * c - b * d), sums[1] + (a * d + b * c)

                    zero = jnp.zeros((tile, lane_step), jnp.float32)
                    sum_real, sum_imag = lax.fori_loop(0, total + 1, add, (zero, zero))
                    mixed[0, real, lanes] = sum_real - sign * last[imag, lanes]
                    mixed[0, imag, lanes] = sum_imag + sign * last[real, lanes]
                    last[real, lanes] = sum_real
                    last[imag, lanes] = sum_imag

            inverse(0, total)


def convolve(product, spectra, forward_table, inverse_table):
    length, width = product.shape
    count, double, _ = spectra.shape
    small = count <= UNROLLED
    return pl.pallas_call(
        conv_kernel,
        out_shape=jax.ShapeDtypeStruct((length, width), jnp.bfloat16),
        in_specs=[pl.BlockSpec(memory_space=pltpu.VMEM)] * 4,
        out_specs=pl.BlockSpec(memory_space=pltpu.VMEM),
        scratch_shapes=[
            pltpu.VMEM((count, double, width), jnp.float32),
            pltpu.VMEM((count if small else 1, double, width), jnp.float32),
            pltpu.VMEM((8, width) if small else (double, width), jnp.float32),
        ],
        compiler_params=pltpu.CompilerParams(vmem_limit_bytes=(32 if small else 56) * MIB),
        cost_estimate=pl.CostEstimate(
            flops=16 * length * double * width,
            bytes_accessed=12 * length * width,
            transcendentals=0,
        ),
    )(forward_table, inverse_table, product, spectra)


def exchange(value):
    return lax.all_to_all(value, "seq", split_axis=0, concat_axis=0, tiled=True)


def on_device(query_in, key_in, value_in, long_filter, short_weight, skip_gain):
    places = lax.axis_size("seq")
    parts = lax.axis_size("groups")
    group = lax.axis_index("groups").astype(jnp.int32)
    rows, channels = key_in.shape
    width = channels // places
    length = places * rows
    block = BLOCK if length % BLOCK == 0 else rows
    forward_table, inverse_table = transform_tables(block)
    forward_table = jnp.asarray(forward_table)
    inverse_table = jnp.asarray(inverse_table)
    rim = short_weight.shape[1] - 1
    aligned = width % (parts * LANES) == 0 and parts == 2

    if aligned:
        sent = spread_filter(long_filter, group, places, parts)
        own = exchange(sent).reshape(length, width // parts)
        other = lax.ppermute(own, "groups", [(0, 1), (1, 0)])
        filter_pieces = [own, other]
    else:
        sent = long_filter.reshape(rows, places, width).transpose(1, 0, 2)
        filter_pieces = [exchange(sent).reshape(length, width)]

    edges = from_behind(jnp.stack([query_in[-rim:], key_in[-rim:], value_in[-rim:]]), "seq")
    if aligned:
        product = products(key_in, value_in, edges, short_weight, width)
        sent = product
    else:
        product = products(key_in, value_in, edges, short_weight, channels)
        sent = product.reshape(rows, places, width).transpose(1, 0, 2)
    received = exchange(sent).reshape(length, width)
    spectra = filter_spectra(filter_pieces, group, forward_table)
    convolved = convolve(received, spectra, forward_table, inverse_table)
    convolved = exchange(convolved.reshape(places, rows, width))
    if not aligned:
        convolved = convolved.transpose(1, 0, 2).reshape(1, rows, channels)
    return gate(convolved, product, query_in, edges, short_weight, skip_gain)


def solution(mesh):
    placed = (
        P(("groups", "seq"), None),
        P(("groups", "seq"), None),
        P(("groups", "seq"), None),
        P("seq", None),
        P(),
        P(),
    )
    return jax.shard_map(
        on_device, mesh=mesh, in_specs=placed, out_specs=P(("groups", "seq"), None), check_vma=False
    )
```

```python
import functools

import jax
import jax.numpy as jnp
import ml_dtypes
import numpy as np
from jax import lax
from jax.experimental import pallas as pl
from jax.experimental.pallas import tpu as pltpu
from jax.sharding import PartitionSpec as P

LANES = 128
SUBLANES = 8
BLOCK = 256
UNROLLED = 8
MIB = 1 << 20


def from_behind(value, axis):
    count = lax.axis_size(axis)
    return lax.ppermute(value, axis, [(source, source + 1) for source in range(count - 1)])


def transform_tables(block):
    numbers = np.concatenate([np.arange(0, block, 2), np.arange(1, block, 2)])
    quarter = (2 * numbers[:, None] + 1) * np.arange(block)[None, :] % (4 * block)
    angle = quarter.astype(np.float64) * (2.0 * np.pi / (4 * block))
    table = np.concatenate([np.cos(angle), -np.sin(angle)], axis=0)

    def split(values):
        high = values.astype(ml_dtypes.bfloat16)
        low = (values - high.astype(np.float64)).astype(ml_dtypes.bfloat16)
        return np.concatenate([high, low], axis=0)

    return split(table), split(table.T / block)


def shifted(values, edge, steps):
    rolled = pltpu.roll(values, steps, 0)
    row = lax.broadcasted_iota(jnp.int32, values.shape, 0)
    for place in range(steps):
        source = edge[edge.shape[0] - steps + place : edge.shape[0] - steps + place + 1]
        rolled = jnp.where(row == place, jnp.broadcast_to(source, values.shape), rolled)
    return rolled


def featurize_inside(own, taps):
    result = taps[0:1] * own
    for offset in range(1, taps.shape[0]):
        result = result + taps[offset : offset + 1] * pltpu.roll(own, offset, 0)
    return result


def featurize(own, edge, taps):
    own = own.astype(jnp.float32)
    edge = edge.astype(jnp.float32)
    top = own[:SUBLANES]
    first = taps[0:1] * top
    for offset in range(1, taps.shape[0]):
        first = first + taps[offset : offset + 1] * shifted(top, edge, offset)
    return jnp.concatenate([first, featurize_inside(own, taps)[SUBLANES:]], axis=0)


def product_kernel(key_ref, value_ref, edge_ref, taps_ref, out_ref):
    for start in range(0, key_ref.shape[1], LANES):
        span = slice(start, start + LANES)
        k_short = featurize(key_ref[:, span], edge_ref[1, :, span], taps_ref[1, :, span])
        v_short = featurize(value_ref[:, span], edge_ref[2, :, span], taps_ref[2, :, span])
        out_ref[:, span] = (k_short * v_short).astype(out_ref.dtype)


def products(key_in, value_in, edges, short_weight):
    rows, channels = key_in.shape
    span = min(channels, 1024)
    taps = short_weight.shape[1]
    return pl.pallas_call(
        product_kernel,
        out_shape=jax.ShapeDtypeStruct((rows, channels), jnp.bfloat16),
        grid=(channels // span,),
        in_specs=[
            pl.BlockSpec((rows, span), lambda i: (0, i)),
            pl.BlockSpec((rows, span), lambda i: (0, i)),
            pl.BlockSpec((3, taps - 1, span), lambda i: (0, 0, i)),
            pl.BlockSpec((3, taps, span), lambda i: (0, 0, i)),
        ],
        out_specs=pl.BlockSpec((rows, span), lambda i: (0, i)),
        cost_estimate=pl.CostEstimate(
            flops=12 * rows * channels, bytes_accessed=6 * rows * channels, transcendentals=0
        ),
    )(key_in, value_in, edges, short_weight)


def gate_kernel(conv_ref, product_ref, query_ref, edge_ref, taps_ref, gain_ref, out_ref):
    for part in range(conv_ref.shape[0]):
        span = slice(part * LANES, (part + 1) * LANES)
        q_short = featurize(query_ref[:, span], edge_ref[0, :, span], taps_ref[0, :, span])
        mixed = conv_ref[part].astype(jnp.float32) + gain_ref[:, span] * product_ref[
            :, span
        ].astype(jnp.float32)
        out_ref[:, span] = (q_short * mixed).astype(out_ref.dtype)


def gate(convolved, product, query_in, edges, short_weight, skip_gain):
    rows, channels = query_in.shape
    span = min(channels, 1024)
    taps = short_weight.shape[1]
    across = pl.BlockSpec((rows, span), lambda i: (0, i))
    return pl.pallas_call(
        gate_kernel,
        out_shape=jax.ShapeDtypeStruct((rows, channels), jnp.bfloat16),
        grid=(channels // span,),
        in_specs=[
            pl.BlockSpec((span // LANES, rows, LANES), lambda i: (i, 0, 0)),
            across,
            across,
            pl.BlockSpec((3, taps - 1, span), lambda i: (0, 0, i)),
            pl.BlockSpec((3, taps, span), lambda i: (0, 0, i)),
            pl.BlockSpec((1, span), lambda i: (0, i)),
        ],
        out_specs=across,
        cost_estimate=pl.CostEstimate(
            flops=9 * rows * channels, bytes_accessed=8 * rows * channels, transcendentals=0
        ),
    )(convolved, product, query_in, edges, short_weight, skip_gain.reshape(1, channels))


def pack_kernel(group_ref, key_ref, value_ref, filter_ref, taps_ref, out_ref):
    del group_ref
    rows = key_ref.shape[0]
    share = filter_ref.shape[0]
    row = lax.broadcasted_iota(jnp.int32, (SUBLANES, LANES), 0)
    for part in range(out_ref.shape[0]):
        span = slice(part * LANES, (part + 1) * LANES)
        key = key_ref[:, span].astype(jnp.float32)
        value = value_ref[:, span].astype(jnp.float32)
        k_short = featurize_inside(key, taps_ref[1, :, span])
        v_short = featurize_inside(value, taps_ref[2, :, span])
        out_ref[part, :rows] = (k_short * v_short).astype(out_ref.dtype)
        out_ref[part, rows : rows + share] = filter_ref[:, span]
        key_tile = jnp.where(
            row < 2,
            pltpu.roll(key[rows - SUBLANES :], 2, 0),
            pltpu.roll(key[:SUBLANES], 2, 0),
        )
        value_tile = jnp.where(
            row < 6,
            pltpu.roll(value[rows - SUBLANES :], 6, 0),
            pltpu.roll(value[:SUBLANES], 6, 0),
        )
        edge = jnp.where(row < 4, key_tile, value_tile)
        out_ref[part, rows + share :] = edge.astype(out_ref.dtype)


def pack(key_in, value_in, long_filter, short_weight, group, owners, parts):
    rows, channels = key_in.shape
    span = min(channels, 1024)
    taps = short_weight.shape[1]
    height = rows + rows // parts + SUBLANES
    return pl.pallas_call(
        pack_kernel,
        out_shape=jax.ShapeDtypeStruct((owners, height, LANES), jnp.bfloat16),
        grid_spec=pltpu.PrefetchScalarGridSpec(
            num_scalar_prefetch=1,
            grid=(channels // span,),
            in_specs=[
                pl.BlockSpec((rows, span), lambda i, g: (0, i)),
                pl.BlockSpec((rows, span), lambda i, g: (0, i)),
                pl.BlockSpec((rows // parts, span), lambda i, g: (g[0], i)),
                pl.BlockSpec((3, taps, span), lambda i, g: (0, 0, i)),
            ],
            out_specs=pl.BlockSpec((span // LANES, height, LANES), lambda i, g: (i, 0, 0)),
        ),
        cost_estimate=pl.CostEstimate(
            flops=12 * rows * channels, bytes_accessed=8 * rows * channels, transcendentals=0
        ),
    )(group.reshape(1), key_in, value_in, long_filter, short_weight)


def transform(table, values):
    both = jnp.dot(table, values, preferred_element_type=jnp.float32)
    half = table.shape[0] // 2
    return both[:half] + both[half:]


def over(count, body):
    if count <= UNROLLED:
        for step in range(count):
            body(step)
    else:

        @pl.loop(0, count)
        def _(step):
            body(step)


def filter_kernel(table_ref, filter_ref, out_ref):
    count, double, _ = out_ref.shape
    block = double // 2

    def body(step):
        start = step * block
        if not isinstance(step, int):
            start = pl.multiple_of(start, block)
        out_ref[step] = transform(table_ref[...], filter_ref[pl.ds(start, block), :])

    over(count, body)


def filter_spectra(long_filter, table):
    length, width = long_filter.shape
    block = table.shape[1]
    return pl.pallas_call(
        filter_kernel,
        out_shape=jax.ShapeDtypeStruct((length // block, 2 * block, width), jnp.float32),
        in_specs=[pl.BlockSpec(memory_space=pltpu.VMEM)] * 2,
        out_specs=pl.BlockSpec(memory_space=pltpu.VMEM),
        compiler_params=pltpu.CompilerParams(vmem_limit_bytes=40 * MIB),
        cost_estimate=pl.CostEstimate(
            flops=8 * length * block * width, bytes_accessed=10 * length * width, transcendentals=0
        ),
    )(table, long_filter)


def inverse(table_ref, values, block):
    high = values.astype(jnp.bfloat16)
    low = (values - high.astype(jnp.float32)).astype(jnp.bfloat16)
    return transform(table_ref[...], high) + jnp.dot(
        table_ref[:block], low, preferred_element_type=jnp.float32
    )


def conv_kernel(forward_ref, inverse_ref, product_ref, filter_ref, out_ref, data, mixed, last):
    count, double, width = filter_ref.shape
    block = double // 2
    lane_step = min(width, LANES)

    def piece(step):
        start = step * block
        return pl.ds(start if isinstance(step, int) else pl.multiple_of(start, block), block)

    def forward(step):
        data[step] = transform(forward_ref[...], product_ref[piece(step), :])

    over(count, forward)
    last[...] = jnp.zeros_like(last)

    @pl.loop(0, count)
    def _(total):
        for sign, base in ((1.0, 0), (-1.0, block // 2)):
            for column in range(0, width, lane_step):
                lanes = slice(column, column + lane_step)

                @pl.loop(0, block // 2 // SUBLANES)
                def _(index):
                    start = pl.multiple_of(base + index * SUBLANES, SUBLANES)
                    real = pl.ds(start, SUBLANES)
                    imag = pl.ds(pl.multiple_of(block + start, SUBLANES), SUBLANES)

                    def add(step, sums):
                        a, b = data[step, real, lanes], data[step, imag, lanes]
                        c = filter_ref[total - step, real, lanes]
                        d = filter_ref[total - step, imag, lanes]
                        return sums[0] + (a * c - b * d), sums[1] + (a * d + b * c)

                    zero = jnp.zeros((SUBLANES, lane_step), jnp.float32)
                    sum_real, sum_imag = lax.fori_loop(0, total + 1, add, (zero, zero))
                    mixed[real, lanes] = sum_real - sign * last[imag, lanes]
                    mixed[imag, lanes] = sum_imag + sign * last[real, lanes]
                    last[real, lanes] = sum_real
                    last[imag, lanes] = sum_imag

        out_ref[piece(total), :] = inverse(inverse_ref, mixed[...], block).astype(out_ref.dtype)


def convolve(product, spectra, forward_table, inverse_table):
    length, width = product.shape
    count, double, _ = spectra.shape
    return pl.pallas_call(
        conv_kernel,
        out_shape=jax.ShapeDtypeStruct((length, width), jnp.bfloat16),
        in_specs=[pl.BlockSpec(memory_space=pltpu.VMEM)] * 4,
        out_specs=pl.BlockSpec(memory_space=pltpu.VMEM),
        scratch_shapes=[
            pltpu.VMEM((count, double, width), jnp.float32),
            pltpu.VMEM((double, width), jnp.float32),
            pltpu.VMEM((double, width), jnp.float32),
        ],
        compiler_params=pltpu.CompilerParams(vmem_limit_bytes=56 * MIB),
        cost_estimate=pl.CostEstimate(
            flops=16 * length * double * width,
            bytes_accessed=12 * length * width,
            transcendentals=0,
        ),
    )(forward_table, inverse_table, product, spectra)


def whole_kernel(
    owner_ref, forward_ref, inverse_ref, taps_ref, sent_ref, out_ref,
    arrived, product, filters, data, mixed, ready, in_sems, out_sems,
):
    del owner_ref
    senders, height, _ = sent_ref.shape
    _, rows, _ = out_ref.shape
    places = senders // 2
    share = rows // 2
    count, double, _ = data.shape
    block = double // 2
    near = block // rows

    copies = []
    for step in range(count):
        for part in range(2):
            span = pl.ds(part * places + step * near, near)
            copies.append(
                pltpu.make_async_copy(sent_ref.at[span], arrived.at[span], in_sems.at[step, part])
            )
    for copy in copies:
        copy.start()

    row = lax.broadcasted_iota(jnp.int32, (SUBLANES, LANES), 0)
    weights = [
        jnp.where(row < 4, taps_ref[1, tap : tap + 1], taps_ref[2, tap : tap + 1])
        for tap in range(taps_ref.shape[1])
    ]
    own_rows = (row % 4) >= 2
    behind = [jnp.zeros((SUBLANES, LANES), jnp.float32)] * 2
    for step in range(count):
        for part in range(2):
            copies[2 * step + part].wait()
            lanes = slice(part * LANES, (part + 1) * LANES)
            for offset in range(near):
                sender = part * places + step * near + offset
                edge = arrived[sender, rows + share :].astype(jnp.float32)
                joined = jnp.where(own_rows, edge, behind[part])
                behind[part] = edge
                short = weights[0] * joined
                for tap in range(1, len(weights)):
                    short = short + weights[tap] * pltpu.roll(joined, tap, 0)
                first = pltpu.roll(short * pltpu.roll(short, 4, 0), 6, 0)
                values = arrived[sender, :rows].astype(jnp.float32)
                top = jnp.where(row < 2, first, values[:SUBLANES])
                values = jnp.concatenate([top, values[SUBLANES:]], axis=0)
                product[step, offset * rows : (offset + 1) * rows, lanes] = values.astype(
                    product.dtype
                )
                start = offset * rows + part * share
                half = (step % 2) * LANES
                filters[start : start + share, half : half + LANES] = arrived[
                    sender, rows : rows + share
                ]
        data[step, :, : 2 * LANES] = transform(forward_ref[...], product[step])
        if step % 2:
            both = transform(forward_ref[...], filters[...])
            data[step - 1, :, 2 * LANES :] = both[:, :LANES]
            data[step, :, 2 * LANES :] = both[:, LANES:]

    for sign, base in ((1, 0), (-1, block // 2)):

        @pl.loop(0, block // 2 // SUBLANES)
        def _(index):
            start = pl.multiple_of(base + index * SUBLANES, SUBLANES)
            real = pl.ds(start, SUBLANES)
            imag = pl.ds(pl.multiple_of(block + start, SUBLANES), SUBLANES)
            third = slice(2 * LANES, 3 * LANES)
            filter_parts = [
                (data[step, real, third], data[step, imag, third]) for step in range(count)
            ]
            for part in range(2):
                lanes = slice(part * LANES, (part + 1) * LANES)
                data_parts = [
                    (data[step, real, lanes], data[step, imag, lanes]) for step in range(count)
                ]
                before = None
                for total in range(count):
                    sums = None
                    for step in range(total + 1):
                        a, b = data_parts[step]
                        c, d = filter_parts[total - step]
                        term = (a * c - b * d, a * d + b * c)
                        sums = term if sums is None else (sums[0] + term[0], sums[1] + term[1])
                    if before is None:
                        both = sums
                    elif sign > 0:
                        both = (sums[0] - before[1], sums[1] + before[0])
                    else:
                        both = (sums[0] + before[1], sums[1] - before[0])
                    mixed[total, real, lanes] = both[0]
                    mixed[total, imag, lanes] = both[1]
                    before = sums

    copies = []
    for step in range(count):
        result = inverse(inverse_ref, mixed[step], block).astype(ready.dtype)
        for part in range(2):
            for offset in range(near):
                ready[part * places + step * near + offset] = result[
                    offset * rows : (offset + 1) * rows, part * LANES : (part + 1) * LANES
                ]
            span = pl.ds(part * places + step * near, near)
            copies.append(
                pltpu.make_async_copy(ready.at[span], out_ref.at[span], out_sems.at[step, part])
            )
            copies[-1].start()
    for copy in copies:
        copy.wait()


def convolve_whole(sent, short_weight, owner, rows, forward_table, inverse_table):
    senders, height, _ = sent.shape
    block = forward_table.shape[1]
    length = senders // 2 * rows
    count = length // block
    taps = short_weight.shape[1]
    whole = pl.BlockSpec(memory_space=pltpu.HBM)
    return pl.pallas_call(
        whole_kernel,
        out_shape=jax.ShapeDtypeStruct((senders, rows, LANES), jnp.bfloat16),
        grid_spec=pltpu.PrefetchScalarGridSpec(
            num_scalar_prefetch=1,
            grid=(1,),
            in_specs=[
                pl.BlockSpec(memory_space=pltpu.VMEM),
                pl.BlockSpec(memory_space=pltpu.VMEM),
                pl.BlockSpec((3, taps, LANES), lambda i, owner: (0, 0, owner[0])),
                whole,
            ],
            out_specs=whole,
            scratch_shapes=[
                pltpu.VMEM((senders, height, LANES), jnp.bfloat16),
                pltpu.VMEM((count, block, 2 * LANES), jnp.bfloat16),
                pltpu.VMEM((block, 2 * LANES), jnp.bfloat16),
                pltpu.VMEM((count, 2 * block, 3 * LANES), jnp.float32),
                pltpu.VMEM((count, 2 * block, 2 * LANES), jnp.float32),
                pltpu.VMEM((senders, rows, LANES), jnp.bfloat16),
                pltpu.SemaphoreType.DMA((count, 2)),
                pltpu.SemaphoreType.DMA((count, 2)),
            ],
        ),
        compiler_params=pltpu.CompilerParams(vmem_limit_bytes=32 * MIB),
        cost_estimate=pl.CostEstimate(
            flops=40 * length * block * LANES,
            bytes_accessed=2 * senders * (height + rows) * LANES,
            transcendentals=0,
        ),
    )(owner.reshape(1), forward_table, inverse_table, short_weight, sent)


def exchange(value, axes):
    return lax.all_to_all(value, axes, split_axis=0, concat_axis=0, tiled=True)


def on_device(query_in, key_in, value_in, long_filter, short_weight, skip_gain):
    places = lax.axis_size("seq")
    parts = lax.axis_size("groups")
    group = lax.axis_index("groups").astype(jnp.int32)
    place = lax.axis_index("seq").astype(jnp.int32)
    rows, channels = key_in.shape
    length = places * rows
    block = BLOCK if length % BLOCK == 0 else rows
    forward_table, inverse_table = transform_tables(block)
    forward_table = jnp.asarray(forward_table)
    inverse_table = jnp.asarray(inverse_table)
    rim = short_weight.shape[1] - 1
    owners = parts * places
    count = length // block
    aligned = (
        parts == 2
        and rim == 2
        and channels == owners * LANES
        and rows % 32 == 0
        and block % rows == 0
        and count % 2 == 0
        and count <= UNROLLED
    )
    edges = jnp.stack([query_in[-rim:], key_in[-rim:], value_in[-rim:]])

    if aligned:
        sent = pack(key_in, value_in, long_filter, short_weight, group, owners, parts)
        edges, sent = lax.optimization_barrier((edges, sent))
        received = exchange(sent, ("groups", "seq"))
        edges = from_behind(edges, "seq")
        product = products(key_in, value_in, edges, short_weight)
        owner = group * places + place
        convolved = convolve_whole(
            received, short_weight, owner, rows, forward_table, inverse_table
        )
        convolved = exchange(convolved, ("groups", "seq"))
    else:
        width = channels // places
        sent = long_filter.reshape(rows, places, width).transpose(1, 0, 2)
        spectra = filter_spectra(exchange(sent, "seq").reshape(length, width), forward_table)
        edges = from_behind(edges, "seq")
        product = products(key_in, value_in, edges, short_weight)
        sent = product.reshape(rows, places, width).transpose(1, 0, 2)
        received = exchange(sent, "seq").reshape(length, width)
        convolved = convolve(received, spectra, forward_table, inverse_table)
        convolved = exchange(convolved.reshape(places, rows, width), "seq")
        convolved = convolved.transpose(1, 0, 2).reshape(rows, channels // LANES, LANES)
        convolved = convolved.transpose(1, 0, 2)
    return gate(convolved, product, query_in, edges, short_weight, skip_gain)


def solution(mesh):
    placed = (
        P(("groups", "seq"), None),
        P(("groups", "seq"), None),
        P(("groups", "seq"), None),
        P("seq", None),
        P(),
        P(),
    )
    return jax.shard_map(
        on_device, mesh=mesh, in_specs=placed, out_specs=P(("groups", "seq"), None), check_vma=False
    )
```

```python
import functools

import jax
import jax.numpy as jnp
import ml_dtypes
import numpy as np
from jax import lax
from jax.experimental import pallas as pl
from jax.experimental.pallas import tpu as pltpu
from jax.sharding import PartitionSpec as P

LANES = 128
SUBLANES = 8
BLOCK = 256
UNROLLED = 8
MIB = 1 << 20


def from_behind(value, axis):
    count = lax.axis_size(axis)
    return lax.ppermute(value, axis, [(source, source + 1) for source in range(count - 1)])


def transform_tables(block):
    numbers = np.concatenate([np.arange(0, block, 2), np.arange(1, block, 2)])
    quarter = (2 * numbers[:, None] + 1) * np.arange(block)[None, :] % (4 * block)
    angle = quarter.astype(np.float64) * (2.0 * np.pi / (4 * block))
    table = np.concatenate([np.cos(angle), -np.sin(angle)], axis=0)

    def split(values):
        high = values.astype(ml_dtypes.bfloat16)
        low = (values - high.astype(np.float64)).astype(ml_dtypes.bfloat16)
        return np.concatenate([high, low], axis=0)

    return split(table), split(table.T / block)


def shifted(values, edge, steps):
    rolled = pltpu.roll(values, steps, 0)
    row = lax.broadcasted_iota(jnp.int32, values.shape, 0)
    for place in range(steps):
        source = edge[edge.shape[0] - steps + place : edge.shape[0] - steps + place + 1]
        rolled = jnp.where(row == place, jnp.broadcast_to(source, values.shape), rolled)
    return rolled


def featurize_inside(own, taps):
    result = taps[0:1] * own
    for offset in range(1, taps.shape[0]):
        result = result + taps[offset : offset + 1] * pltpu.roll(own, offset, 0)
    return result


def featurize(own, edge, taps):
    own = own.astype(jnp.float32)
    edge = edge.astype(jnp.float32)
    top = own[:SUBLANES]
    first = taps[0:1] * top
    for offset in range(1, taps.shape[0]):
        first = first + taps[offset : offset + 1] * shifted(top, edge, offset)
    return jnp.concatenate([first, featurize_inside(own, taps)[SUBLANES:]], axis=0)


def product_kernel(key_ref, value_ref, edge_ref, taps_ref, out_ref):
    for start in range(0, key_ref.shape[1], LANES):
        span = slice(start, start + LANES)
        k_short = featurize(key_ref[:, span], edge_ref[1, :, span], taps_ref[1, :, span])
        v_short = featurize(value_ref[:, span], edge_ref[2, :, span], taps_ref[2, :, span])
        out_ref[:, span] = (k_short * v_short).astype(out_ref.dtype)


def products(key_in, value_in, edges, short_weight):
    rows, channels = key_in.shape
    span = min(channels, 1024)
    taps = short_weight.shape[1]
    return pl.pallas_call(
        product_kernel,
        out_shape=jax.ShapeDtypeStruct((rows, channels), jnp.bfloat16),
        grid=(channels // span,),
        in_specs=[
            pl.BlockSpec((rows, span), lambda i: (0, i)),
            pl.BlockSpec((rows, span), lambda i: (0, i)),
            pl.BlockSpec((3, taps - 1, span), lambda i: (0, 0, i)),
            pl.BlockSpec((3, taps, span), lambda i: (0, 0, i)),
        ],
        out_specs=pl.BlockSpec((rows, span), lambda i: (0, i)),
        cost_estimate=pl.CostEstimate(
            flops=12 * rows * channels, bytes_accessed=6 * rows * channels, transcendentals=0
        ),
    )(key_in, value_in, edges, short_weight)


def gate_kernel(conv_ref, product_ref, query_ref, edge_ref, taps_ref, gain_ref, out_ref):
    for part in range(conv_ref.shape[0]):
        span = slice(part * LANES, (part + 1) * LANES)
        q_short = featurize(query_ref[:, span], edge_ref[0, :, span], taps_ref[0, :, span])
        mixed = conv_ref[part].astype(jnp.float32) + gain_ref[:, span] * product_ref[
            :, span
        ].astype(jnp.float32)
        out_ref[:, span] = (q_short * mixed).astype(out_ref.dtype)


def gate(convolved, product, query_in, edges, short_weight, skip_gain):
    rows, channels = query_in.shape
    span = min(channels, 1024)
    taps = short_weight.shape[1]
    across = pl.BlockSpec((rows, span), lambda i: (0, i))
    return pl.pallas_call(
        gate_kernel,
        out_shape=jax.ShapeDtypeStruct((rows, channels), jnp.bfloat16),
        grid=(channels // span,),
        in_specs=[
            pl.BlockSpec((span // LANES, rows, LANES), lambda i: (i, 0, 0)),
            across,
            across,
            pl.BlockSpec((3, taps - 1, span), lambda i: (0, 0, i)),
            pl.BlockSpec((3, taps, span), lambda i: (0, 0, i)),
            pl.BlockSpec((1, span), lambda i: (0, i)),
        ],
        out_specs=across,
        cost_estimate=pl.CostEstimate(
            flops=9 * rows * channels, bytes_accessed=8 * rows * channels, transcendentals=0
        ),
    )(convolved, product, query_in, edges, short_weight, skip_gain.reshape(1, channels))


def finish_kernel(
    conv_ref, product_ref, query_ref, edge_ref, taps_ref, gain_ref, out_ref, ready, sems
):
    channels = ready.shape[1]
    chunks = sems.shape[0]
    span = channels // chunks
    near = span // LANES

    def departure(chunk):
        columns = pl.ds(pl.multiple_of(chunk * span, span), span)
        return pltpu.make_async_copy(ready.at[:, columns], out_ref.at[:, columns], sems.at[chunk])

    @pl.loop(0, chunks)
    def _(chunk):
        for part in range(near):
            lanes = pl.ds(pl.multiple_of(chunk * span + part * LANES, LANES), LANES)
            q_short = featurize(query_ref[:, lanes], edge_ref[0, :, lanes], taps_ref[0, :, lanes])
            mixed = conv_ref[chunk * near + part].astype(jnp.float32) + gain_ref[
                :, lanes
            ] * product_ref[:, lanes].astype(jnp.float32)
            ready[:, lanes] = (q_short * mixed).astype(ready.dtype)
        departure(chunk).start()

    for chunk in range(chunks):
        departure(chunk).wait()


def finish(convolved, product, query_in, edges, short_weight, skip_gain):
    rows, channels = query_in.shape
    chunks = max(1, channels // 512)
    here = pl.BlockSpec(memory_space=pltpu.VMEM)
    return pl.pallas_call(
        finish_kernel,
        out_shape=jax.ShapeDtypeStruct((rows, channels), jnp.bfloat16),
        in_specs=[here] * 6,
        out_specs=pl.BlockSpec(memory_space=pltpu.HBM),
        scratch_shapes=[
            pltpu.VMEM((rows, channels), jnp.bfloat16),
            pltpu.SemaphoreType.DMA((chunks,)),
        ],
        compiler_params=pltpu.CompilerParams(vmem_limit_bytes=8 * MIB),
        cost_estimate=pl.CostEstimate(
            flops=9 * rows * channels, bytes_accessed=8 * rows * channels, transcendentals=0
        ),
    )(convolved, product, query_in, edges, short_weight, skip_gain.reshape(1, channels))


def pack_kernel(
    group_ref, query_ref, key_ref, value_ref, filter_ref, taps_ref, out_ref, edges_ref,
    query, key, value, filters, taps, packed, edges, in_sems, one_sems, out_sems,
):
    rows, channels = key.shape
    share = filters.shape[0]
    rim = edges.shape[1]
    chunks = out_sems.shape[0]
    span = channels // chunks
    near = span // LANES
    start = pl.multiple_of(group_ref[0] * share, share)
    whole = [
        pltpu.make_async_copy(taps_ref, taps, one_sems.at[0]),
        pltpu.make_async_copy(query_ref.at[pl.ds(rows - SUBLANES, SUBLANES)], query, one_sems.at[1]),
    ]

    def arrivals(chunk):
        columns = pl.ds(pl.multiple_of(chunk * span, span), span)
        return [
            pltpu.make_async_copy(key_ref.at[:, columns], key.at[:, columns], in_sems.at[0, chunk]),
            pltpu.make_async_copy(
                value_ref.at[:, columns], value.at[:, columns], in_sems.at[1, chunk]
            ),
            pltpu.make_async_copy(
                filter_ref.at[pl.ds(start, share), columns],
                filters.at[:, columns],
                in_sems.at[2, chunk],
            ),
        ]

    def departure(chunk):
        owners = pl.ds(chunk * near, near)
        return pltpu.make_async_copy(packed.at[owners], out_ref.at[owners], out_sems.at[chunk])

    for copy in whole:
        copy.start()
    for chunk in range(chunks):
        for copy in arrivals(chunk):
            copy.start()
    for copy in whole:
        copy.wait()
    row = lax.broadcasted_iota(jnp.int32, (SUBLANES, LANES), 0)

    @pl.loop(0, chunks)
    def _(chunk):
        for copy in arrivals(chunk):
            copy.wait()
        for part in range(near):
            span_here = pl.ds(pl.multiple_of(chunk * span + part * LANES, LANES), LANES)
            owner = chunk * near + part
            key_here = key[:, span_here].astype(jnp.float32)
            value_here = value[:, span_here].astype(jnp.float32)
            k_short = featurize_inside(key_here, taps[1, :, span_here])
            v_short = featurize_inside(value_here, taps[2, :, span_here])
            packed[owner, :rows] = (k_short * v_short).astype(packed.dtype)
            packed[owner, rows : rows + share] = filters[:, span_here]
            query_last = pltpu.roll(query[:, span_here].astype(jnp.float32), rim, 0)
            key_last = pltpu.roll(key_here[rows - SUBLANES :], rim, 0)
            value_last = pltpu.roll(value_here[rows - SUBLANES :], rim, 0)
            key_tile = jnp.where(row < 2, key_last, pltpu.roll(key_here[:SUBLANES], 2, 0))
            value_tile = jnp.where(
                row < 6, pltpu.roll(value_last, 4, 0), pltpu.roll(value_here[:SUBLANES], 6, 0)
            )
            edge = jnp.where(row < 4, key_tile, value_tile)
            packed[owner, rows + share :] = edge.astype(packed.dtype)
            for stream, last in enumerate((query_last, key_last, value_last)):
                edges[stream, :, span_here] = last[:rim].astype(edges.dtype)
        departure(chunk).start()

    last = pltpu.make_async_copy(edges, edges_ref, one_sems.at[0])
    last.start()
    for chunk in range(chunks):
        departure(chunk).wait()
    last.wait()


def pack(query_in, key_in, value_in, long_filter, short_weight, group, owners, parts):
    rows, channels = key_in.shape
    chunks = max(1, channels // 512)
    taps = short_weight.shape[1]
    share = rows // parts
    height = rows + share + SUBLANES
    here = pl.BlockSpec(memory_space=pltpu.HBM)
    return pl.pallas_call(
        pack_kernel,
        out_shape=(
            jax.ShapeDtypeStruct((owners, height, LANES), jnp.bfloat16),
            jax.ShapeDtypeStruct((3, taps - 1, channels), jnp.bfloat16),
        ),
        in_specs=[pl.BlockSpec(memory_space=pltpu.SMEM)] + [here] * 5,
        out_specs=(here, here),
        scratch_shapes=[
            pltpu.VMEM((SUBLANES, channels), jnp.bfloat16),
            pltpu.VMEM((rows, channels), jnp.bfloat16),
            pltpu.VMEM((rows, channels), jnp.bfloat16),
            pltpu.VMEM((share, channels), jnp.bfloat16),
            pltpu.VMEM((3, taps, channels), jnp.float32),
            pltpu.VMEM((owners, height, LANES), jnp.bfloat16),
            pltpu.VMEM((3, taps - 1, channels), jnp.bfloat16),
            pltpu.SemaphoreType.DMA((3, chunks)),
            pltpu.SemaphoreType.DMA((2,)),
            pltpu.SemaphoreType.DMA((chunks,)),
        ],
        cost_estimate=pl.CostEstimate(
            flops=12 * rows * channels, bytes_accessed=8 * rows * channels, transcendentals=0
        ),
    )(group.reshape(1), query_in, key_in, value_in, long_filter, short_weight)


def transform(table, values):
    both = jnp.dot(table, values, preferred_element_type=jnp.float32)
    half = table.shape[0] // 2
    return both[:half] + both[half:]


def over(count, body):
    if count <= UNROLLED:
        for step in range(count):
            body(step)
    else:

        @pl.loop(0, count)
        def _(step):
            body(step)


def filter_kernel(table_ref, filter_ref, out_ref):
    count, double, _ = out_ref.shape
    block = double // 2

    def body(step):
        start = step * block
        if not isinstance(step, int):
            start = pl.multiple_of(start, block)
        out_ref[step] = transform(table_ref[...], filter_ref[pl.ds(start, block), :])

    over(count, body)


def filter_spectra(long_filter, table):
    length, width = long_filter.shape
    block = table.shape[1]
    return pl.pallas_call(
        filter_kernel,
        out_shape=jax.ShapeDtypeStruct((length // block, 2 * block, width), jnp.float32),
        in_specs=[pl.BlockSpec(memory_space=pltpu.VMEM)] * 2,
        out_specs=pl.BlockSpec(memory_space=pltpu.VMEM),
        compiler_params=pltpu.CompilerParams(vmem_limit_bytes=40 * MIB),
        cost_estimate=pl.CostEstimate(
            flops=8 * length * block * width, bytes_accessed=10 * length * width, transcendentals=0
        ),
    )(table, long_filter)


def inverse(table_ref, values, block):
    high = values.astype(jnp.bfloat16)
    low = (values - high.astype(jnp.float32)).astype(jnp.bfloat16)
    return transform(table_ref[...], high) + jnp.dot(
        table_ref[:block], low, preferred_element_type=jnp.float32
    )


def conv_kernel(forward_ref, inverse_ref, product_ref, filter_ref, out_ref, data, mixed, last):
    count, double, width = filter_ref.shape
    block = double // 2
    lane_step = min(width, LANES)

    def piece(step):
        start = step * block
        return pl.ds(start if isinstance(step, int) else pl.multiple_of(start, block), block)

    def forward(step):
        data[step] = transform(forward_ref[...], product_ref[piece(step), :])

    over(count, forward)
    last[...] = jnp.zeros_like(last)

    @pl.loop(0, count)
    def _(total):
        for sign, base in ((1.0, 0), (-1.0, block // 2)):
            for column in range(0, width, lane_step):
                lanes = slice(column, column + lane_step)

                @pl.loop(0, block // 2 // SUBLANES)
                def _(index):
                    start = pl.multiple_of(base + index * SUBLANES, SUBLANES)
                    real = pl.ds(start, SUBLANES)
                    imag = pl.ds(pl.multiple_of(block + start, SUBLANES), SUBLANES)

                    def add(step, sums):
                        a, b = data[step, real, lanes], data[step, imag, lanes]
                        c = filter_ref[total - step, real, lanes]
                        d = filter_ref[total - step, imag, lanes]
                        return sums[0] + (a * c - b * d), sums[1] + (a * d + b * c)

                    zero = jnp.zeros((SUBLANES, lane_step), jnp.float32)
                    sum_real, sum_imag = lax.fori_loop(0, total + 1, add, (zero, zero))
                    mixed[real, lanes] = sum_real - sign * last[imag, lanes]
                    mixed[imag, lanes] = sum_imag + sign * last[real, lanes]
                    last[real, lanes] = sum_real
                    last[imag, lanes] = sum_imag

        out_ref[piece(total), :] = inverse(inverse_ref, mixed[...], block).astype(out_ref.dtype)


def convolve(product, spectra, forward_table, inverse_table):
    length, width = product.shape
    count, double, _ = spectra.shape
    return pl.pallas_call(
        conv_kernel,
        out_shape=jax.ShapeDtypeStruct((length, width), jnp.bfloat16),
        in_specs=[pl.BlockSpec(memory_space=pltpu.VMEM)] * 4,
        out_specs=pl.BlockSpec(memory_space=pltpu.VMEM),
        scratch_shapes=[
            pltpu.VMEM((count, double, width), jnp.float32),
            pltpu.VMEM((double, width), jnp.float32),
            pltpu.VMEM((double, width), jnp.float32),
        ],
        compiler_params=pltpu.CompilerParams(vmem_limit_bytes=56 * MIB),
        cost_estimate=pl.CostEstimate(
            flops=16 * length * double * width,
            bytes_accessed=12 * length * width,
            transcendentals=0,
        ),
    )(forward_table, inverse_table, product, spectra)


def whole_kernel(
    owner_ref, forward_ref, inverse_ref, taps_ref, arrived, out_ref,
    product, filters, data, mixed, ready, out_sems,
):
    del owner_ref
    senders, rows, _ = ready.shape
    places = senders // 2
    share = rows // 2
    count, double, _ = data.shape
    block = double // 2
    near = block // rows

    row = lax.broadcasted_iota(jnp.int32, (SUBLANES, LANES), 0)
    weights = [
        jnp.where(row < 4, taps_ref[1, tap : tap + 1], taps_ref[2, tap : tap + 1])
        for tap in range(taps_ref.shape[1])
    ]
    own_rows = (row % 4) >= 2
    behind = [jnp.zeros((SUBLANES, LANES), jnp.float32)] * 2
    for step in range(count):
        for part in range(2):
            lanes = slice(part * LANES, (part + 1) * LANES)
            for offset in range(near):
                sender = part * places + step * near + offset
                edge = arrived[sender, rows + share :].astype(jnp.float32)
                joined = jnp.where(own_rows, edge, behind[part])
                behind[part] = edge
                short = weights[0] * joined
                for tap in range(1, len(weights)):
                    short = short + weights[tap] * pltpu.roll(joined, tap, 0)
                first = pltpu.roll(short * pltpu.roll(short, 4, 0), 6, 0)
                values = arrived[sender, :rows].astype(jnp.float32)
                top = jnp.where(row < 2, first, values[:SUBLANES])
                values = jnp.concatenate([top, values[SUBLANES:]], axis=0)
                product[step, offset * rows : (offset + 1) * rows, lanes] = values.astype(
                    product.dtype
                )
                start = offset * rows + part * share
                half = (step % 2) * LANES
                filters[start : start + share, half : half + LANES] = arrived[
                    sender, rows : rows + share
                ]
        data[step, :, : 2 * LANES] = transform(forward_ref[...], product[step])
        if step % 2:
            both = transform(forward_ref[...], filters[...])
            data[step - 1, :, 2 * LANES :] = both[:, :LANES]
            data[step, :, 2 * LANES :] = both[:, LANES:]

    for sign, base in ((1, 0), (-1, block // 2)):

        @pl.loop(0, block // 2 // SUBLANES)
        def _(index):
            start = pl.multiple_of(base + index * SUBLANES, SUBLANES)
            real = pl.ds(start, SUBLANES)
            imag = pl.ds(pl.multiple_of(block + start, SUBLANES), SUBLANES)
            third = slice(2 * LANES, 3 * LANES)
            filter_parts = [
                (data[step, real, third], data[step, imag, third]) for step in range(count)
            ]
            for part in range(2):
                lanes = slice(part * LANES, (part + 1) * LANES)
                data_parts = [
                    (data[step, real, lanes], data[step, imag, lanes]) for step in range(count)
                ]
                before = None
                for total in range(count):
                    sums = None
                    for step in range(total + 1):
                        a, b = data_parts[step]
                        c, d = filter_parts[total - step]
                        term = (a * c - b * d, a * d + b * c)
                        sums = term if sums is None else (sums[0] + term[0], sums[1] + term[1])
                    if before is None:
                        both = sums
                    elif sign > 0:
                        both = (sums[0] - before[1], sums[1] + before[0])
                    else:
                        both = (sums[0] + before[1], sums[1] - before[0])
                    mixed[total, real, lanes] = both[0]
                    mixed[total, imag, lanes] = both[1]
                    before = sums

    copies = []
    for step in range(count):
        result = inverse(inverse_ref, mixed[step], block).astype(ready.dtype)
        for part in range(2):
            for offset in range(near):
                ready[part * places + step * near + offset] = result[
                    offset * rows : (offset + 1) * rows, part * LANES : (part + 1) * LANES
                ]
            span = pl.ds(part * places + step * near, near)
            copies.append(
                pltpu.make_async_copy(ready.at[span], out_ref.at[span], out_sems.at[step, part])
            )
            copies[-1].start()
    for copy in copies:
        copy.wait()


def convolve_whole(sent, short_weight, owner, rows, forward_table, inverse_table):
    senders, height, _ = sent.shape
    block = forward_table.shape[1]
    length = senders // 2 * rows
    count = length // block
    taps = short_weight.shape[1]
    return pl.pallas_call(
        whole_kernel,
        out_shape=jax.ShapeDtypeStruct((senders, rows, LANES), jnp.bfloat16),
        grid_spec=pltpu.PrefetchScalarGridSpec(
            num_scalar_prefetch=1,
            grid=(1,),
            in_specs=[
                pl.BlockSpec(memory_space=pltpu.VMEM),
                pl.BlockSpec(memory_space=pltpu.VMEM),
                pl.BlockSpec((3, taps, LANES), lambda i, owner: (0, 0, owner[0])),
                pl.BlockSpec(memory_space=pltpu.VMEM),
            ],
            out_specs=pl.BlockSpec(memory_space=pltpu.HBM),
            scratch_shapes=[
                pltpu.VMEM((count, block, 2 * LANES), jnp.bfloat16),
                pltpu.VMEM((block, 2 * LANES), jnp.bfloat16),
                pltpu.VMEM((count, 2 * block, 3 * LANES), jnp.float32),
                pltpu.VMEM((count, 2 * block, 2 * LANES), jnp.float32),
                pltpu.VMEM((senders, rows, LANES), jnp.bfloat16),
                pltpu.SemaphoreType.DMA((count, 2)),
            ],
        ),
        compiler_params=pltpu.CompilerParams(vmem_limit_bytes=32 * MIB),
        cost_estimate=pl.CostEstimate(
            flops=40 * length * block * LANES,
            bytes_accessed=2 * senders * (height + rows) * LANES,
            transcendentals=0,
        ),
    )(owner.reshape(1), forward_table, inverse_table, short_weight, sent)


def exchange(value, axes):
    return lax.all_to_all(value, axes, split_axis=0, concat_axis=0, tiled=True)


def on_device(query_in, key_in, value_in, long_filter, short_weight, skip_gain):
    places = lax.axis_size("seq")
    parts = lax.axis_size("groups")
    group = lax.axis_index("groups").astype(jnp.int32)
    place = lax.axis_index("seq").astype(jnp.int32)
    rows, channels = key_in.shape
    length = places * rows
    block = BLOCK if length % BLOCK == 0 else rows
    forward_table, inverse_table = transform_tables(block)
    forward_table = jnp.asarray(forward_table)
    inverse_table = jnp.asarray(inverse_table)
    rim = short_weight.shape[1] - 1
    owners = parts * places
    count = length // block
    aligned = (
        parts == 2
        and rim == 2
        and channels == owners * LANES
        and rows % 32 == 0
        and block % rows == 0
        and count % 2 == 0
        and count <= UNROLLED
    )
    if aligned:
        sent, edges = pack(
            query_in, key_in, value_in, long_filter, short_weight, group, owners, parts
        )
        received = exchange(sent, ("groups", "seq"))
        edges = from_behind(edges, "seq")
        product = products(key_in, value_in, edges, short_weight)
        received, product, edges = lax.optimization_barrier((received, product, edges))
        owner = group * places + place
        convolved = convolve_whole(
            received, short_weight, owner, rows, forward_table, inverse_table
        )
        convolved = exchange(convolved, ("groups", "seq"))
        return finish(convolved, product, query_in, edges, short_weight, skip_gain)
    else:
        width = channels // places
        edges = jnp.stack([query_in[-rim:], key_in[-rim:], value_in[-rim:]])
        sent = long_filter.reshape(rows, places, width).transpose(1, 0, 2)
        spectra = filter_spectra(exchange(sent, "seq").reshape(length, width), forward_table)
        edges = from_behind(edges, "seq")
        product = products(key_in, value_in, edges, short_weight)
        sent = product.reshape(rows, places, width).transpose(1, 0, 2)
        received = exchange(sent, "seq").reshape(length, width)
        convolved = convolve(received, spectra, forward_table, inverse_table)
        convolved = exchange(convolved.reshape(places, rows, width), "seq")
        convolved = convolved.transpose(1, 0, 2).reshape(rows, channels // LANES, LANES)
        convolved = convolved.transpose(1, 0, 2)
        return gate(convolved, product, query_in, edges, short_weight, skip_gain)


def solution(mesh):
    placed = (
        P(("groups", "seq"), None),
        P(("groups", "seq"), None),
        P(("groups", "seq"), None),
        P("seq", None),
        P(),
        P(),
    )
    return jax.shard_map(
        on_device, mesh=mesh, in_specs=placed, out_specs=P(("groups", "seq"), None), check_vma=False
    )
```

```python
import functools

import jax
import jax.numpy as jnp
import ml_dtypes
import numpy as np
from jax import lax
from jax.experimental import pallas as pl
from jax.experimental.pallas import tpu as pltpu
from jax.sharding import PartitionSpec as P

LANES = 128
SUBLANES = 8
BLOCK = 256
UNROLLED = 8
MIB = 1 << 20


def from_behind(value, axis):
    count = lax.axis_size(axis)
    return lax.ppermute(value, axis, [(source, source + 1) for source in range(count - 1)])


def transform_tables(block):
    numbers = np.concatenate([np.arange(0, block, 2), np.arange(1, block, 2)])
    quarter = (2 * numbers[:, None] + 1) * np.arange(block)[None, :] % (4 * block)
    angle = quarter.astype(np.float64) * (2.0 * np.pi / (4 * block))
    table = np.concatenate([np.cos(angle), -np.sin(angle)], axis=0)

    def split(values):
        high = values.astype(ml_dtypes.bfloat16)
        low = (values - high.astype(np.float64)).astype(ml_dtypes.bfloat16)
        return np.concatenate([high, low], axis=0)

    return split(table), split(table.T / block)


def shifted(values, edge, steps):
    rolled = pltpu.roll(values, steps, 0)
    row = lax.broadcasted_iota(jnp.int32, values.shape, 0)
    for place in range(steps):
        source = edge[edge.shape[0] - steps + place : edge.shape[0] - steps + place + 1]
        rolled = jnp.where(row == place, jnp.broadcast_to(source, values.shape), rolled)
    return rolled


def featurize_inside(own, taps):
    result = taps[0:1] * own
    for offset in range(1, taps.shape[0]):
        result = result + taps[offset : offset + 1] * pltpu.roll(own, offset, 0)
    return result


def featurize(own, edge, taps):
    own = own.astype(jnp.float32)
    edge = edge.astype(jnp.float32)
    top = own[:SUBLANES]
    first = taps[0:1] * top
    for offset in range(1, taps.shape[0]):
        first = first + taps[offset : offset + 1] * shifted(top, edge, offset)
    return jnp.concatenate([first, featurize_inside(own, taps)[SUBLANES:]], axis=0)


def product_kernel(key_ref, value_ref, edge_ref, taps_ref, out_ref):
    for start in range(0, key_ref.shape[1], LANES):
        span = slice(start, start + LANES)
        k_short = featurize(key_ref[:, span], edge_ref[1, :, span], taps_ref[1, :, span])
        v_short = featurize(value_ref[:, span], edge_ref[2, :, span], taps_ref[2, :, span])
        out_ref[:, span] = (k_short * v_short).astype(out_ref.dtype)


def products(key_in, value_in, edges, short_weight):
    rows, channels = key_in.shape
    span = min(channels, 1024)
    taps = short_weight.shape[1]
    return pl.pallas_call(
        product_kernel,
        out_shape=jax.ShapeDtypeStruct((rows, channels), jnp.bfloat16),
        grid=(channels // span,),
        in_specs=[
            pl.BlockSpec((rows, span), lambda i: (0, i)),
            pl.BlockSpec((rows, span), lambda i: (0, i)),
            pl.BlockSpec((3, taps - 1, span), lambda i: (0, 0, i)),
            pl.BlockSpec((3, taps, span), lambda i: (0, 0, i)),
        ],
        out_specs=pl.BlockSpec((rows, span), lambda i: (0, i)),
        cost_estimate=pl.CostEstimate(
            flops=12 * rows * channels, bytes_accessed=6 * rows * channels, transcendentals=0
        ),
    )(key_in, value_in, edges, short_weight)


def gate_kernel(conv_ref, product_ref, query_ref, edge_ref, taps_ref, gain_ref, out_ref):
    for part in range(conv_ref.shape[0]):
        span = slice(part * LANES, (part + 1) * LANES)
        q_short = featurize(query_ref[:, span], edge_ref[0, :, span], taps_ref[0, :, span])
        mixed = conv_ref[part].astype(jnp.float32) + gain_ref[:, span] * product_ref[
            :, span
        ].astype(jnp.float32)
        out_ref[:, span] = (q_short * mixed).astype(out_ref.dtype)


def gate(convolved, product, query_in, edges, short_weight, skip_gain):
    rows, channels = query_in.shape
    span = min(channels, 1024)
    taps = short_weight.shape[1]
    across = pl.BlockSpec((rows, span), lambda i: (0, i))
    return pl.pallas_call(
        gate_kernel,
        out_shape=jax.ShapeDtypeStruct((rows, channels), jnp.bfloat16),
        grid=(channels // span,),
        in_specs=[
            pl.BlockSpec((span // LANES, rows, LANES), lambda i: (i, 0, 0)),
            across,
            across,
            pl.BlockSpec((3, taps - 1, span), lambda i: (0, 0, i)),
            pl.BlockSpec((3, taps, span), lambda i: (0, 0, i)),
            pl.BlockSpec((1, span), lambda i: (0, i)),
        ],
        out_specs=across,
        cost_estimate=pl.CostEstimate(
            flops=9 * rows * channels, bytes_accessed=8 * rows * channels, transcendentals=0
        ),
    )(convolved, product, query_in, edges, short_weight, skip_gain.reshape(1, channels))


def finish_kernel(
    conv_ref, sent_ref, query_ref, edge_ref, taps_ref, gain_ref, out_ref, ready, sems
):
    rows, channels = ready.shape
    tail = sent_ref.shape[1] - SUBLANES
    chunks = sems.shape[0]
    span = channels // chunks
    near = span // LANES
    row = lax.broadcasted_iota(jnp.int32, (SUBLANES, LANES), 0)

    def departure(chunk):
        columns = pl.ds(pl.multiple_of(chunk * span, span), span)
        return pltpu.make_async_copy(ready.at[:, columns], out_ref.at[:, columns], sems.at[chunk])

    @pl.loop(0, chunks)
    def _(chunk):
        for part in range(near):
            owner = chunk * near + part
            lanes = pl.ds(pl.multiple_of(owner * LANES, LANES), LANES)
            behind = edge_ref[:, lanes].astype(jnp.float32)
            own = sent_ref[owner, tail:].astype(jnp.float32)
            first = first_products(own, behind, tap_tiles(taps_ref, lanes))
            first = first.astype(jnp.bfloat16).astype(jnp.float32)
            product = sent_ref[owner, :rows].astype(jnp.float32)
            top = jnp.where(row < 2, first, product[:SUBLANES])
            product = jnp.concatenate([top, product[SUBLANES:]], axis=0)

            query = query_ref[:, lanes].astype(jnp.float32)
            weights = taps_ref[0, :, lanes]
            top = query[:SUBLANES]
            one = jnp.where(row < 1, pltpu.roll(behind, 5, 0), pltpu.roll(top, 1, 0))
            two = jnp.where(row < 2, pltpu.roll(behind, 6, 0), pltpu.roll(top, 2, 0))
            top = weights[0:1] * top + weights[1:2] * one + weights[2:3] * two
            inside = featurize_inside(query, weights)
            q_short = jnp.concatenate([top, inside[SUBLANES:]], axis=0)

            mixed = conv_ref[owner].astype(jnp.float32) + gain_ref[:, lanes] * product
            ready[:, lanes] = (q_short * mixed).astype(ready.dtype)
        departure(chunk).start()

    for chunk in range(chunks):
        departure(chunk).wait()


def finish(convolved, sent, query_in, edges, short_weight, skip_gain):
    rows, channels = query_in.shape
    chunks = max(1, channels // 512)
    here = pl.BlockSpec(memory_space=pltpu.VMEM)
    return pl.pallas_call(
        finish_kernel,
        out_shape=jax.ShapeDtypeStruct((rows, channels), jnp.bfloat16),
        in_specs=[here] * 6,
        out_specs=pl.BlockSpec(memory_space=pltpu.HBM),
        scratch_shapes=[
            pltpu.VMEM((rows, channels), jnp.bfloat16),
            pltpu.SemaphoreType.DMA((chunks,)),
        ],
        compiler_params=pltpu.CompilerParams(vmem_limit_bytes=8 * MIB),
        cost_estimate=pl.CostEstimate(
            flops=9 * rows * channels, bytes_accessed=8 * rows * channels, transcendentals=0
        ),
    )(convolved, sent, query_in, edges, short_weight, skip_gain.reshape(1, channels))


def tap_tiles(taps_ref, lanes):
    row = lax.broadcasted_iota(jnp.int32, (SUBLANES, LANES), 0)
    return [
        jnp.where(row < 4, taps_ref[1, tap : tap + 1, lanes], taps_ref[2, tap : tap + 1, lanes])
        for tap in range(taps_ref.shape[1])
    ]


def first_products(tile, behind, weights):
    row = lax.broadcasted_iota(jnp.int32, (SUBLANES, LANES), 0)
    joined = jnp.where(row % 4 >= 2, tile, behind)
    short = weights[0] * joined
    for tap in range(1, len(weights)):
        short = short + weights[tap] * pltpu.roll(joined, tap, 0)
    return pltpu.roll(short * pltpu.roll(short, 4, 0), 6, 0)


def pack_kernel(
    group_ref, query_ref, key_ref, value_ref, filter_ref, taps_ref, out_ref, edges_ref,
    query, key, value, filters, taps, packed, edges, in_sems, one_sems, out_sems,
):
    rows, channels = key.shape
    share = filters.shape[0]
    chunks = out_sems.shape[0]
    span = channels // chunks
    near = span // LANES
    start = pl.multiple_of(group_ref[0] * share, share)
    whole = [
        pltpu.make_async_copy(taps_ref, taps, one_sems.at[0]),
        pltpu.make_async_copy(query_ref.at[pl.ds(rows - SUBLANES, SUBLANES)], query, one_sems.at[1]),
    ]

    def arrivals(chunk):
        columns = pl.ds(pl.multiple_of(chunk * span, span), span)
        return [
            pltpu.make_async_copy(key_ref.at[:, columns], key.at[:, columns], in_sems.at[0, chunk]),
            pltpu.make_async_copy(
                value_ref.at[:, columns], value.at[:, columns], in_sems.at[1, chunk]
            ),
            pltpu.make_async_copy(
                filter_ref.at[pl.ds(start, share), columns],
                filters.at[:, columns],
                in_sems.at[2, chunk],
            ),
        ]

    def departure(chunk):
        owners = pl.ds(chunk * near, near)
        return pltpu.make_async_copy(packed.at[owners], out_ref.at[owners], out_sems.at[chunk])

    for copy in whole:
        copy.start()
    for chunk in range(chunks):
        for copy in arrivals(chunk):
            copy.start()
    for copy in whole:
        copy.wait()
    row = lax.broadcasted_iota(jnp.int32, (SUBLANES, LANES), 0)

    @pl.loop(0, chunks)
    def _(chunk):
        for copy in arrivals(chunk):
            copy.wait()
        for part in range(near):
            span_here = pl.ds(pl.multiple_of(chunk * span + part * LANES, LANES), LANES)
            owner = chunk * near + part
            key_here = key[:, span_here].astype(jnp.float32)
            value_here = value[:, span_here].astype(jnp.float32)
            k_short = featurize_inside(key_here, taps[1, :, span_here])
            v_short = featurize_inside(value_here, taps[2, :, span_here])
            packed[owner, :rows] = (k_short * v_short).astype(packed.dtype)
            packed[owner, rows : rows + share] = filters[:, span_here]
            query_last = pltpu.roll(query[:, span_here].astype(jnp.float32), 4, 0)
            key_tile = jnp.where(
                row < 2,
                pltpu.roll(key_here[rows - SUBLANES :], 2, 0),
                pltpu.roll(key_here[:SUBLANES], 2, 0),
            )
            value_tile = jnp.where(
                row < 6,
                pltpu.roll(value_here[rows - SUBLANES :], 6, 0),
                pltpu.roll(value_here[:SUBLANES], 6, 0),
            )
            edge = jnp.where(row < 4, key_tile, value_tile)
            packed[owner, rows + share :] = edge.astype(packed.dtype)
            edge = jnp.where((row == 2) | (row == 3), query_last, edge)
            edges[:, span_here] = edge.astype(edges.dtype)
        departure(chunk).start()

    last = pltpu.make_async_copy(edges, edges_ref, one_sems.at[0])
    last.start()
    for chunk in range(chunks):
        departure(chunk).wait()
    last.wait()


def pack(query_in, key_in, value_in, long_filter, short_weight, group, owners, parts):
    rows, channels = key_in.shape
    chunks = max(1, channels // 512)
    taps = short_weight.shape[1]
    share = rows // parts
    height = rows + share + SUBLANES
    here = pl.BlockSpec(memory_space=pltpu.HBM)
    return pl.pallas_call(
        pack_kernel,
        out_shape=(
            jax.ShapeDtypeStruct((owners, height, LANES), jnp.bfloat16),
            jax.ShapeDtypeStruct((SUBLANES, channels), jnp.bfloat16),
        ),
        in_specs=[pl.BlockSpec(memory_space=pltpu.SMEM)] + [here] * 5,
        out_specs=(here, here),
        scratch_shapes=[
            pltpu.VMEM((SUBLANES, channels), jnp.bfloat16),
            pltpu.VMEM((rows, channels), jnp.bfloat16),
            pltpu.VMEM((rows, channels), jnp.bfloat16),
            pltpu.VMEM((share, channels), jnp.bfloat16),
            pltpu.VMEM((3, taps, channels), jnp.float32),
            pltpu.VMEM((owners, height, LANES), jnp.bfloat16),
            pltpu.VMEM((SUBLANES, channels), jnp.bfloat16),
            pltpu.SemaphoreType.DMA((3, chunks)),
            pltpu.SemaphoreType.DMA((2,)),
            pltpu.SemaphoreType.DMA((chunks,)),
        ],
        cost_estimate=pl.CostEstimate(
            flops=12 * rows * channels, bytes_accessed=8 * rows * channels, transcendentals=0
        ),
    )(group.reshape(1), query_in, key_in, value_in, long_filter, short_weight)


def transform(table, values):
    both = jnp.dot(table, values, preferred_element_type=jnp.float32)
    half = table.shape[0] // 2
    return both[:half] + both[half:]


def over(count, body):
    if count <= UNROLLED:
        for step in range(count):
            body(step)
    else:

        @pl.loop(0, count)
        def _(step):
            body(step)


def filter_kernel(table_ref, filter_ref, out_ref):
    count, double, _ = out_ref.shape
    block = double // 2

    def body(step):
        start = step * block
        if not isinstance(step, int):
            start = pl.multiple_of(start, block)
        out_ref[step] = transform(table_ref[...], filter_ref[pl.ds(start, block), :])

    over(count, body)


def filter_spectra(long_filter, table):
    length, width = long_filter.shape
    block = table.shape[1]
    return pl.pallas_call(
        filter_kernel,
        out_shape=jax.ShapeDtypeStruct((length // block, 2 * block, width), jnp.float32),
        in_specs=[pl.BlockSpec(memory_space=pltpu.VMEM)] * 2,
        out_specs=pl.BlockSpec(memory_space=pltpu.VMEM),
        compiler_params=pltpu.CompilerParams(vmem_limit_bytes=40 * MIB),
        cost_estimate=pl.CostEstimate(
            flops=8 * length * block * width, bytes_accessed=10 * length * width, transcendentals=0
        ),
    )(table, long_filter)


def inverse(table_ref, values, block):
    high = values.astype(jnp.bfloat16)
    low = (values - high.astype(jnp.float32)).astype(jnp.bfloat16)
    return transform(table_ref[...], high) + jnp.dot(
        table_ref[:block], low, preferred_element_type=jnp.float32
    )


def conv_kernel(forward_ref, inverse_ref, product_ref, filter_ref, out_ref, data, mixed, last):
    count, double, width = filter_ref.shape
    block = double // 2
    lane_step = min(width, LANES)

    def piece(step):
        start = step * block
        return pl.ds(start if isinstance(step, int) else pl.multiple_of(start, block), block)

    def forward(step):
        data[step] = transform(forward_ref[...], product_ref[piece(step), :])

    over(count, forward)
    last[...] = jnp.zeros_like(last)

    @pl.loop(0, count)
    def _(total):
        for sign, base in ((1.0, 0), (-1.0, block // 2)):
            for column in range(0, width, lane_step):
                lanes = slice(column, column + lane_step)

                @pl.loop(0, block // 2 // SUBLANES)
                def _(index):
                    start = pl.multiple_of(base + index * SUBLANES, SUBLANES)
                    real = pl.ds(start, SUBLANES)
                    imag = pl.ds(pl.multiple_of(block + start, SUBLANES), SUBLANES)

                    def add(step, sums):
                        a, b = data[step, real, lanes], data[step, imag, lanes]
                        c = filter_ref[total - step, real, lanes]
                        d = filter_ref[total - step, imag, lanes]
                        return sums[0] + (a * c - b * d), sums[1] + (a * d + b * c)

                    zero = jnp.zeros((SUBLANES, lane_step), jnp.float32)
                    sum_real, sum_imag = lax.fori_loop(0, total + 1, add, (zero, zero))
                    mixed[real, lanes] = sum_real - sign * last[imag, lanes]
                    mixed[imag, lanes] = sum_imag + sign * last[real, lanes]
                    last[real, lanes] = sum_real
                    last[imag, lanes] = sum_imag

        out_ref[piece(total), :] = inverse(inverse_ref, mixed[...], block).astype(out_ref.dtype)


def convolve(product, spectra, forward_table, inverse_table):
    length, width = product.shape
    count, double, _ = spectra.shape
    return pl.pallas_call(
        conv_kernel,
        out_shape=jax.ShapeDtypeStruct((length, width), jnp.bfloat16),
        in_specs=[pl.BlockSpec(memory_space=pltpu.VMEM)] * 4,
        out_specs=pl.BlockSpec(memory_space=pltpu.VMEM),
        scratch_shapes=[
            pltpu.VMEM((count, double, width), jnp.float32),
            pltpu.VMEM((double, width), jnp.float32),
            pltpu.VMEM((double, width), jnp.float32),
        ],
        compiler_params=pltpu.CompilerParams(vmem_limit_bytes=56 * MIB),
        cost_estimate=pl.CostEstimate(
            flops=16 * length * double * width,
            bytes_accessed=12 * length * width,
            transcendentals=0,
        ),
    )(forward_table, inverse_table, product, spectra)


def whole_kernel(
    owner_ref, forward_ref, inverse_ref, taps_ref, arrived, ready,
    product, filters, data, mixed,
):
    del owner_ref
    senders, rows, _ = ready.shape
    places = senders // 2
    share = rows // 2
    count, double, _ = data.shape
    block = double // 2
    near = block // rows

    row = lax.broadcasted_iota(jnp.int32, (SUBLANES, LANES), 0)
    weights = tap_tiles(taps_ref, slice(None))
    behind = [jnp.zeros((SUBLANES, LANES), jnp.float32)] * 2
    for step in range(count):
        for part in range(2):
            lanes = slice(part * LANES, (part + 1) * LANES)
            for offset in range(near):
                sender = part * places + step * near + offset
                edge = arrived[sender, rows + share :].astype(jnp.float32)
                first = first_products(edge, behind[part], weights)
                behind[part] = edge
                values = arrived[sender, :rows].astype(jnp.float32)
                top = jnp.where(row < 2, first, values[:SUBLANES])
                values = jnp.concatenate([top, values[SUBLANES:]], axis=0)
                product[step, offset * rows : (offset + 1) * rows, lanes] = values.astype(
                    product.dtype
                )
                start = offset * rows + part * share
                half = (step % 2) * LANES
                filters[start : start + share, half : half + LANES] = arrived[
                    sender, rows : rows + share
                ]
        data[step, :, : 2 * LANES] = transform(forward_ref[...], product[step])
        if step % 2:
            both = transform(forward_ref[...], filters[...])
            data[step - 1, :, 2 * LANES :] = both[:, :LANES]
            data[step, :, 2 * LANES :] = both[:, LANES:]

    for sign, base in ((1, 0), (-1, block // 2)):

        @pl.loop(0, block // 2 // SUBLANES)
        def _(index):
            start = pl.multiple_of(base + index * SUBLANES, SUBLANES)
            real = pl.ds(start, SUBLANES)
            imag = pl.ds(pl.multiple_of(block + start, SUBLANES), SUBLANES)
            third = slice(2 * LANES, 3 * LANES)
            filter_parts = [
                (data[step, real, third], data[step, imag, third]) for step in range(count)
            ]
            for part in range(2):
                lanes = slice(part * LANES, (part + 1) * LANES)
                data_parts = [
                    (data[step, real, lanes], data[step, imag, lanes]) for step in range(count)
                ]
                before = None
                for total in range(count):
                    sums = None
                    for step in range(total + 1):
                        a, b = data_parts[step]
                        c, d = filter_parts[total - step]
                        term = (a * c - b * d, a * d + b * c)
                        sums = term if sums is None else (sums[0] + term[0], sums[1] + term[1])
                    if before is None:
                        both = sums
                    elif sign > 0:
                        both = (sums[0] - before[1], sums[1] + before[0])
                    else:
                        both = (sums[0] + before[1], sums[1] - before[0])
                    mixed[total, real, lanes] = both[0]
                    mixed[total, imag, lanes] = both[1]
                    before = sums

    for step in range(count):
        result = inverse(inverse_ref, mixed[step], block).astype(ready.dtype)
        for part in range(2):
            for offset in range(near):
                ready[part * places + step * near + offset] = result[
                    offset * rows : (offset + 1) * rows, part * LANES : (part + 1) * LANES
                ]


def convolve_whole(sent, short_weight, owner, rows, forward_table, inverse_table):
    senders, height, _ = sent.shape
    block = forward_table.shape[1]
    length = senders // 2 * rows
    count = length // block
    taps = short_weight.shape[1]
    return pl.pallas_call(
        whole_kernel,
        out_shape=jax.ShapeDtypeStruct((senders, rows, LANES), jnp.bfloat16),
        grid_spec=pltpu.PrefetchScalarGridSpec(
            num_scalar_prefetch=1,
            grid=(1,),
            in_specs=[
                pl.BlockSpec(memory_space=pltpu.VMEM),
                pl.BlockSpec(memory_space=pltpu.VMEM),
                pl.BlockSpec((3, taps, LANES), lambda i, owner: (0, 0, owner[0])),
                pl.BlockSpec(memory_space=pltpu.VMEM),
            ],
            out_specs=pl.BlockSpec(memory_space=pltpu.VMEM),
            scratch_shapes=[
                pltpu.VMEM((count, block, 2 * LANES), jnp.bfloat16),
                pltpu.VMEM((block, 2 * LANES), jnp.bfloat16),
                pltpu.VMEM((count, 2 * block, 3 * LANES), jnp.float32),
                pltpu.VMEM((count, 2 * block, 2 * LANES), jnp.float32),
            ],
        ),
        compiler_params=pltpu.CompilerParams(vmem_limit_bytes=32 * MIB),
        cost_estimate=pl.CostEstimate(
            flops=40 * length * block * LANES,
            bytes_accessed=2 * senders * (height + rows) * LANES,
            transcendentals=0,
        ),
    )(owner.reshape(1), forward_table, inverse_table, short_weight, sent)


def exchange(value, axes):
    return lax.all_to_all(value, axes, split_axis=0, concat_axis=0, tiled=True)


def on_device(query_in, key_in, value_in, long_filter, short_weight, skip_gain):
    places = lax.axis_size("seq")
    parts = lax.axis_size("groups")
    group = lax.axis_index("groups").astype(jnp.int32)
    place = lax.axis_index("seq").astype(jnp.int32)
    rows, channels = key_in.shape
    length = places * rows
    block = BLOCK if length % BLOCK == 0 else rows
    forward_table, inverse_table = transform_tables(block)
    forward_table = jnp.asarray(forward_table)
    inverse_table = jnp.asarray(inverse_table)
    rim = short_weight.shape[1] - 1
    owners = parts * places
    count = length // block
    aligned = (
        parts == 2
        and rim == 2
        and channels == owners * LANES
        and rows % 32 == 0
        and block % rows == 0
        and count % 2 == 0
        and count <= UNROLLED
    )
    if aligned:
        sent, edges = pack(
            query_in, key_in, value_in, long_filter, short_weight, group, owners, parts
        )
        received = exchange(sent, ("groups", "seq"))
        edges = from_behind(edges, "seq")
        received, edges = lax.optimization_barrier((received, edges))
        owner = group * places + place
        convolved = convolve_whole(
            received, short_weight, owner, rows, forward_table, inverse_table
        )
        convolved = exchange(convolved, ("groups", "seq"))
        return finish(convolved, sent, query_in, edges, short_weight, skip_gain)
    else:
        width = channels // places
        edges = jnp.stack([query_in[-rim:], key_in[-rim:], value_in[-rim:]])
        sent = long_filter.reshape(rows, places, width).transpose(1, 0, 2)
        spectra = filter_spectra(exchange(sent, "seq").reshape(length, width), forward_table)
        edges = from_behind(edges, "seq")
        product = products(key_in, value_in, edges, short_weight)
        sent = product.reshape(rows, places, width).transpose(1, 0, 2)
        received = exchange(sent, "seq").reshape(length, width)
        convolved = convolve(received, spectra, forward_table, inverse_table)
        convolved = exchange(convolved.reshape(places, rows, width), "seq")
        convolved = convolved.transpose(1, 0, 2).reshape(rows, channels // LANES, LANES)
        convolved = convolved.transpose(1, 0, 2)
        return gate(convolved, product, query_in, edges, short_weight, skip_gain)


def solution(mesh):
    placed = (
        P(("groups", "seq"), None),
        P(("groups", "seq"), None),
        P(("groups", "seq"), None),
        P("seq", None),
        P(),
        P(),
    )
    return jax.shard_map(
        on_device, mesh=mesh, in_specs=placed, out_specs=P(("groups", "seq"), None), check_vma=False
    )
```

```python
import functools

import jax
import jax.numpy as jnp
import ml_dtypes
import numpy as np
from jax import lax
from jax.experimental import pallas as pl
from jax.experimental.pallas import tpu as pltpu
from jax.sharding import PartitionSpec as P

LANES = 128
SUBLANES = 8
BLOCK = 256
UNROLLED = 8
MIB = 1 << 20


def from_behind(value, axis):
    count = lax.axis_size(axis)
    return lax.ppermute(value, axis, [(source, source + 1) for source in range(count - 1)])


def transform_tables(block):
    numbers = np.concatenate([np.arange(0, block, 2), np.arange(1, block, 2)])
    quarter = (2 * numbers[:, None] + 1) * np.arange(block)[None, :] % (4 * block)
    angle = quarter.astype(np.float64) * (2.0 * np.pi / (4 * block))
    table = np.concatenate([np.cos(angle), -np.sin(angle)], axis=0)

    def split(values):
        high = values.astype(ml_dtypes.bfloat16)
        low = (values - high.astype(np.float64)).astype(ml_dtypes.bfloat16)
        return np.concatenate([high, low], axis=0)

    return split(table), split(table.T / block)


def half_tables(block):
    forward, inverse = transform_tables(block)
    half = block // 2
    rows = np.arange(2 * block).reshape(2, 2, half).transpose(1, 0, 2).reshape(2, block)
    forward = forward.reshape(2, 2 * block, block)
    forward = np.stack([forward[:, rows[side]].reshape(2 * block, block) for side in range(2)])
    inverse = np.stack([inverse[:, rows[side]] for side in range(2)])
    return forward, inverse


def shifted(values, edge, steps):
    rolled = pltpu.roll(values, steps, 0)
    row = lax.broadcasted_iota(jnp.int32, values.shape, 0)
    for place in range(steps):
        source = edge[edge.shape[0] - steps + place : edge.shape[0] - steps + place + 1]
        rolled = jnp.where(row == place, jnp.broadcast_to(source, values.shape), rolled)
    return rolled


def featurize_inside(own, taps):
    result = taps[0:1] * own
    for offset in range(1, taps.shape[0]):
        result = result + taps[offset : offset + 1] * pltpu.roll(own, offset, 0)
    return result


def featurize(own, edge, taps):
    own = own.astype(jnp.float32)
    edge = edge.astype(jnp.float32)
    top = own[:SUBLANES]
    first = taps[0:1] * top
    for offset in range(1, taps.shape[0]):
        first = first + taps[offset : offset + 1] * shifted(top, edge, offset)
    return jnp.concatenate([first, featurize_inside(own, taps)[SUBLANES:]], axis=0)


def product_kernel(key_ref, value_ref, edge_ref, taps_ref, out_ref):
    for start in range(0, key_ref.shape[1], LANES):
        span = slice(start, start + LANES)
        k_short = featurize(key_ref[:, span], edge_ref[1, :, span], taps_ref[1, :, span])
        v_short = featurize(value_ref[:, span], edge_ref[2, :, span], taps_ref[2, :, span])
        out_ref[:, span] = (k_short * v_short).astype(out_ref.dtype)


def products(key_in, value_in, edges, short_weight):
    rows, channels = key_in.shape
    span = min(channels, 1024)
    taps = short_weight.shape[1]
    return pl.pallas_call(
        product_kernel,
        out_shape=jax.ShapeDtypeStruct((rows, channels), jnp.bfloat16),
        grid=(channels // span,),
        in_specs=[
            pl.BlockSpec((rows, span), lambda i: (0, i)),
            pl.BlockSpec((rows, span), lambda i: (0, i)),
            pl.BlockSpec((3, taps - 1, span), lambda i: (0, 0, i)),
            pl.BlockSpec((3, taps, span), lambda i: (0, 0, i)),
        ],
        out_specs=pl.BlockSpec((rows, span), lambda i: (0, i)),
        cost_estimate=pl.CostEstimate(
            flops=12 * rows * channels, bytes_accessed=6 * rows * channels, transcendentals=0
        ),
    )(key_in, value_in, edges, short_weight)


def gate_kernel(conv_ref, product_ref, query_ref, edge_ref, taps_ref, gain_ref, out_ref):
    for part in range(conv_ref.shape[0]):
        span = slice(part * LANES, (part + 1) * LANES)
        q_short = featurize(query_ref[:, span], edge_ref[0, :, span], taps_ref[0, :, span])
        mixed = conv_ref[part].astype(jnp.float32) + gain_ref[:, span] * product_ref[
            :, span
        ].astype(jnp.float32)
        out_ref[:, span] = (q_short * mixed).astype(out_ref.dtype)


def gate(convolved, product, query_in, edges, short_weight, skip_gain):
    rows, channels = query_in.shape
    span = min(channels, 1024)
    taps = short_weight.shape[1]
    across = pl.BlockSpec((rows, span), lambda i: (0, i))
    return pl.pallas_call(
        gate_kernel,
        out_shape=jax.ShapeDtypeStruct((rows, channels), jnp.bfloat16),
        grid=(channels // span,),
        in_specs=[
            pl.BlockSpec((span // LANES, rows, LANES), lambda i: (i, 0, 0)),
            across,
            across,
            pl.BlockSpec((3, taps - 1, span), lambda i: (0, 0, i)),
            pl.BlockSpec((3, taps, span), lambda i: (0, 0, i)),
            pl.BlockSpec((1, span), lambda i: (0, i)),
        ],
        out_specs=across,
        cost_estimate=pl.CostEstimate(
            flops=9 * rows * channels, bytes_accessed=8 * rows * channels, transcendentals=0
        ),
    )(convolved, product, query_in, edges, short_weight, skip_gain.reshape(1, channels))


def finish_kernel(
    conv_ref, sent_ref, query_ref, edge_ref, taps_ref, gain_ref, out_ref, ready, sems
):
    rows, channels = ready.shape
    tail = sent_ref.shape[1] - SUBLANES
    chunks = sems.shape[0]
    span = channels // chunks
    near = span // LANES
    row = lax.broadcasted_iota(jnp.int32, (SUBLANES, LANES), 0)

    def departure(chunk):
        columns = pl.ds(pl.multiple_of(chunk * span, span), span)
        return pltpu.make_async_copy(ready.at[:, columns], out_ref.at[:, columns], sems.at[chunk])

    @pl.loop(0, chunks)
    def _(chunk):
        for part in range(near):
            owner = chunk * near + part
            lanes = pl.ds(pl.multiple_of(owner * LANES, LANES), LANES)
            behind = edge_ref[:, lanes].astype(jnp.float32)
            own = sent_ref[owner, tail:].astype(jnp.float32)
            first = first_products(own, behind, tap_tiles(taps_ref, lanes))
            first = first.astype(jnp.bfloat16).astype(jnp.float32)
            product = sent_ref[owner, :rows].astype(jnp.float32)
            top = jnp.where(row < 2, first, product[:SUBLANES])
            product = jnp.concatenate([top, product[SUBLANES:]], axis=0)

            query = query_ref[:, lanes].astype(jnp.float32)
            weights = taps_ref[0, :, lanes]
            top = query[:SUBLANES]
            one = jnp.where(row < 1, pltpu.roll(behind, 5, 0), pltpu.roll(top, 1, 0))
            two = jnp.where(row < 2, pltpu.roll(behind, 6, 0), pltpu.roll(top, 2, 0))
            top = weights[0:1] * top + weights[1:2] * one + weights[2:3] * two
            inside = featurize_inside(query, weights)
            q_short = jnp.concatenate([top, inside[SUBLANES:]], axis=0)

            mixed = conv_ref[owner].astype(jnp.float32) + gain_ref[:, lanes] * product
            ready[:, lanes] = (q_short * mixed).astype(ready.dtype)
        departure(chunk).start()

    for chunk in range(chunks):
        departure(chunk).wait()


def finish(convolved, sent, query_in, edges, short_weight, skip_gain):
    rows, channels = query_in.shape
    chunks = max(1, channels // 512)
    here = pl.BlockSpec(memory_space=pltpu.VMEM)
    return pl.pallas_call(
        finish_kernel,
        out_shape=jax.ShapeDtypeStruct((rows, channels), jnp.bfloat16),
        in_specs=[here] * 6,
        out_specs=pl.BlockSpec(memory_space=pltpu.HBM),
        scratch_shapes=[
            pltpu.VMEM((rows, channels), jnp.bfloat16),
            pltpu.SemaphoreType.DMA((chunks,)),
        ],
        compiler_params=pltpu.CompilerParams(vmem_limit_bytes=8 * MIB),
        cost_estimate=pl.CostEstimate(
            flops=9 * rows * channels, bytes_accessed=8 * rows * channels, transcendentals=0
        ),
    )(convolved, sent, query_in, edges, short_weight, skip_gain.reshape(1, channels))


def tap_tiles(taps_ref, lanes):
    row = lax.broadcasted_iota(jnp.int32, (SUBLANES, LANES), 0)
    return [
        jnp.where(row < 4, taps_ref[1, tap : tap + 1, lanes], taps_ref[2, tap : tap + 1, lanes])
        for tap in range(taps_ref.shape[1])
    ]


def first_products(tile, behind, weights):
    row = lax.broadcasted_iota(jnp.int32, (SUBLANES, LANES), 0)
    joined = jnp.where(row % 4 >= 2, tile, behind)
    short = weights[0] * joined
    for tap in range(1, len(weights)):
        short = short + weights[tap] * pltpu.roll(joined, tap, 0)
    return pltpu.roll(short * pltpu.roll(short, 4, 0), 6, 0)


def pack_kernel(
    group_ref, query_ref, key_ref, value_ref, filter_ref, taps_ref, out_ref, edges_ref,
    query, key, value, filters, taps, packed, edges, in_sems, one_sems, out_sems,
):
    rows, channels = key.shape
    share = filters.shape[0]
    chunks = out_sems.shape[0]
    span = channels // chunks
    near = span // LANES
    start = pl.multiple_of(group_ref[0] * share, share)
    whole = [
        pltpu.make_async_copy(taps_ref, taps, one_sems.at[0]),
        pltpu.make_async_copy(query_ref.at[pl.ds(rows - SUBLANES, SUBLANES)], query, one_sems.at[1]),
    ]

    def arrivals(chunk):
        columns = pl.ds(pl.multiple_of(chunk * span, span), span)
        return [
            pltpu.make_async_copy(key_ref.at[:, columns], key.at[:, columns], in_sems.at[0, chunk]),
            pltpu.make_async_copy(
                value_ref.at[:, columns], value.at[:, columns], in_sems.at[1, chunk]
            ),
            pltpu.make_async_copy(
                filter_ref.at[pl.ds(start, share), columns],
                filters.at[:, columns],
                in_sems.at[2, chunk],
            ),
        ]

    def departure(chunk):
        owners = pl.ds(chunk * near, near)
        return pltpu.make_async_copy(packed.at[owners], out_ref.at[owners], out_sems.at[chunk])

    for copy in whole:
        copy.start()
    for chunk in range(chunks):
        for copy in arrivals(chunk):
            copy.start()
    for copy in whole:
        copy.wait()
    row = lax.broadcasted_iota(jnp.int32, (SUBLANES, LANES), 0)

    @pl.loop(0, chunks)
    def _(chunk):
        for copy in arrivals(chunk):
            copy.wait()
        for part in range(near):
            span_here = pl.ds(pl.multiple_of(chunk * span + part * LANES, LANES), LANES)
            owner = chunk * near + part
            key_here = key[:, span_here].astype(jnp.float32)
            value_here = value[:, span_here].astype(jnp.float32)
            k_short = featurize_inside(key_here, taps[1, :, span_here])
            v_short = featurize_inside(value_here, taps[2, :, span_here])
            packed[owner, :rows] = (k_short * v_short).astype(packed.dtype)
            packed[owner, rows : rows + share] = filters[:, span_here]
            query_last = pltpu.roll(query[:, span_here].astype(jnp.float32), 4, 0)
            key_tile = jnp.where(
                row < 2,
                pltpu.roll(key_here[rows - SUBLANES :], 2, 0),
                pltpu.roll(key_here[:SUBLANES], 2, 0),
            )
            value_tile = jnp.where(
                row < 6,
                pltpu.roll(value_here[rows - SUBLANES :], 6, 0),
                pltpu.roll(value_here[:SUBLANES], 6, 0),
            )
            edge = jnp.where(row < 4, key_tile, value_tile)
            packed[owner, rows + share :] = edge.astype(packed.dtype)
            edge = jnp.where((row == 2) | (row == 3), query_last, edge)
            edges[:, span_here] = edge.astype(edges.dtype)
        departure(chunk).start()

    last = pltpu.make_async_copy(edges, edges_ref, one_sems.at[0])
    last.start()
    for chunk in range(chunks):
        departure(chunk).wait()
    last.wait()


def pack(query_in, key_in, value_in, long_filter, short_weight, group, owners, parts):
    rows, channels = key_in.shape
    chunks = max(1, channels // 1024)
    taps = short_weight.shape[1]
    share = rows // parts
    height = rows + share + SUBLANES
    here = pl.BlockSpec(memory_space=pltpu.HBM)
    return pl.pallas_call(
        pack_kernel,
        out_shape=(
            jax.ShapeDtypeStruct((owners, height, LANES), jnp.bfloat16),
            jax.ShapeDtypeStruct((SUBLANES, channels), jnp.bfloat16),
        ),
        in_specs=[pl.BlockSpec(memory_space=pltpu.SMEM)] + [here] * 5,
        out_specs=(here, here),
        scratch_shapes=[
            pltpu.VMEM((SUBLANES, channels), jnp.bfloat16),
            pltpu.VMEM((rows, channels), jnp.bfloat16),
            pltpu.VMEM((rows, channels), jnp.bfloat16),
            pltpu.VMEM((share, channels), jnp.bfloat16),
            pltpu.VMEM((3, taps, channels), jnp.float32),
            pltpu.VMEM((owners, height, LANES), jnp.bfloat16),
            pltpu.VMEM((SUBLANES, channels), jnp.bfloat16),
            pltpu.SemaphoreType.DMA((3, chunks)),
            pltpu.SemaphoreType.DMA((2,)),
            pltpu.SemaphoreType.DMA((chunks,)),
        ],
        cost_estimate=pl.CostEstimate(
            flops=12 * rows * channels, bytes_accessed=8 * rows * channels, transcendentals=0
        ),
    )(group.reshape(1), query_in, key_in, value_in, long_filter, short_weight)


def transform(table, values):
    both = jnp.dot(table, values, preferred_element_type=jnp.float32)
    half = table.shape[0] // 2
    return both[:half] + both[half:]


def over(count, body):
    if count <= UNROLLED:
        for step in range(count):
            body(step)
    else:

        @pl.loop(0, count)
        def _(step):
            body(step)


def filter_kernel(table_ref, filter_ref, out_ref):
    count, double, _ = out_ref.shape
    block = double // 2

    def body(step):
        start = step * block
        if not isinstance(step, int):
            start = pl.multiple_of(start, block)
        out_ref[step] = transform(table_ref[...], filter_ref[pl.ds(start, block), :])

    over(count, body)


def filter_spectra(long_filter, table):
    length, width = long_filter.shape
    block = table.shape[1]
    return pl.pallas_call(
        filter_kernel,
        out_shape=jax.ShapeDtypeStruct((length // block, 2 * block, width), jnp.float32),
        in_specs=[pl.BlockSpec(memory_space=pltpu.VMEM)] * 2,
        out_specs=pl.BlockSpec(memory_space=pltpu.VMEM),
        compiler_params=pltpu.CompilerParams(vmem_limit_bytes=40 * MIB),
        cost_estimate=pl.CostEstimate(
            flops=8 * length * block * width, bytes_accessed=10 * length * width, transcendentals=0
        ),
    )(table, long_filter)


def inverse(table_ref, values, block):
    high = values.astype(jnp.bfloat16)
    low = (values - high.astype(jnp.float32)).astype(jnp.bfloat16)
    return transform(table_ref[...], high) + jnp.dot(
        table_ref[:block], low, preferred_element_type=jnp.float32
    )


def conv_kernel(forward_ref, inverse_ref, product_ref, filter_ref, out_ref, data, mixed, last):
    count, double, width = filter_ref.shape
    block = double // 2
    lane_step = min(width, LANES)

    def piece(step):
        start = step * block
        return pl.ds(start if isinstance(step, int) else pl.multiple_of(start, block), block)

    def forward(step):
        data[step] = transform(forward_ref[...], product_ref[piece(step), :])

    over(count, forward)
    last[...] = jnp.zeros_like(last)

    @pl.loop(0, count)
    def _(total):
        for sign, base in ((1.0, 0), (-1.0, block // 2)):
            for column in range(0, width, lane_step):
                lanes = slice(column, column + lane_step)

                @pl.loop(0, block // 2 // SUBLANES)
                def _(index):
                    start = pl.multiple_of(base + index * SUBLANES, SUBLANES)
                    real = pl.ds(start, SUBLANES)
                    imag = pl.ds(pl.multiple_of(block + start, SUBLANES), SUBLANES)

                    def add(step, sums):
                        a, b = data[step, real, lanes], data[step, imag, lanes]
                        c = filter_ref[total - step, real, lanes]
                        d = filter_ref[total - step, imag, lanes]
                        return sums[0] + (a * c - b * d), sums[1] + (a * d + b * c)

                    zero = jnp.zeros((SUBLANES, lane_step), jnp.float32)
                    sum_real, sum_imag = lax.fori_loop(0, total + 1, add, (zero, zero))
                    mixed[real, lanes] = sum_real - sign * last[imag, lanes]
                    mixed[imag, lanes] = sum_imag + sign * last[real, lanes]
                    last[real, lanes] = sum_real
                    last[imag, lanes] = sum_imag

        out_ref[piece(total), :] = inverse(inverse_ref, mixed[...], block).astype(out_ref.dtype)


def convolve(product, spectra, forward_table, inverse_table):
    length, width = product.shape
    count, double, _ = spectra.shape
    return pl.pallas_call(
        conv_kernel,
        out_shape=jax.ShapeDtypeStruct((length, width), jnp.bfloat16),
        in_specs=[pl.BlockSpec(memory_space=pltpu.VMEM)] * 4,
        out_specs=pl.BlockSpec(memory_space=pltpu.VMEM),
        scratch_shapes=[
            pltpu.VMEM((count, double, width), jnp.float32),
            pltpu.VMEM((double, width), jnp.float32),
            pltpu.VMEM((double, width), jnp.float32),
        ],
        compiler_params=pltpu.CompilerParams(vmem_limit_bytes=56 * MIB),
        cost_estimate=pl.CostEstimate(
            flops=16 * length * double * width,
            bytes_accessed=12 * length * width,
            transcendentals=0,
        ),
    )(forward_table, inverse_table, product, spectra)


def whole_kernel(
    owner_ref, forward_ref, inverse_ref, taps_ref, arrived, ready,
    product, filters, data, known, mixed, partly,
):
    del owner_ref
    senders, rows, _ = ready.shape
    places = senders // 2
    share = rows // 2
    _, count, block, _ = data.shape
    half = block // 2
    near = block // rows
    tiles = half // SUBLANES // count
    row = lax.broadcasted_iota(jnp.int32, (SUBLANES, LANES), 0)
    weights = tap_tiles(taps_ref, slice(None))

    def forward(side, values):
        return transform(forward_ref[side], values)

    def backward(side, step):
        return inverse(inverse_ref.at[side], mixed[side, step], block)

    def multiply(side, tile):
        start = tile * SUBLANES
        real = slice(start, start + SUBLANES)
        imag = slice(half + start, half + start + SUBLANES)
        filter_parts = []
        for step in range(count):
            c, d = known[side, step, real], known[side, step, imag]
            filter_parts.append((c, d - c, c + d))
        for part in range(2):
            lanes = slice(part * LANES, (part + 1) * LANES)
            data_parts = []
            for step in range(count):
                a, b = data[side, step, real, lanes], data[side, step, imag, lanes]
                data_parts.append((a + b, a, b))
            before = None
            for total in range(count):
                sums = None
                for step in range(total + 1):
                    pairs = zip(data_parts[step], filter_parts[total - step])
                    terms = [x * y for x, y in pairs]
                    sums = terms if sums is None else [x + y for x, y in zip(sums, terms)]
                both = (sums[0] - sums[2], sums[0] + sums[1])
                if before is None:
                    out = both
                elif side == 0:
                    out = (both[0] - before[1], both[1] + before[0])
                else:
                    out = (both[0] + before[1], both[1] - before[0])
                mixed[side, total, real, lanes] = out[0]
                mixed[side, total, imag, lanes] = out[1]
                before = both

    behind = [jnp.zeros((SUBLANES, LANES), jnp.float32)] * 2
    for step in range(count):
        for part in range(2):
            lanes = slice(part * LANES, (part + 1) * LANES)
            for offset in range(near):
                sender = part * places + step * near + offset
                edge = arrived[sender, rows + share :].astype(jnp.float32)
                first = first_products(edge, behind[part], weights)
                behind[part] = edge
                values = arrived[sender, : 2 * SUBLANES].astype(jnp.float32)
                top = jnp.where(row < 2, first, values[:SUBLANES])
                values = jnp.concatenate([top, values[SUBLANES:]], axis=0)
                start = offset * rows
                product[step, start : start + 2 * SUBLANES, lanes] = values.astype(product.dtype)
                product[step, start + 2 * SUBLANES : start + rows, lanes] = arrived[
                    sender, 2 * SUBLANES : rows
                ]
                start = offset * rows + part * share
                place = (step % 2) * LANES
                filters[step // 2, start : start + share, place : place + LANES] = arrived[
                    sender, rows : rows + share
                ]
        data[0, step] = forward(0, product[step])
        if step % 2:
            for side in range(2):
                both = forward(side, filters[step // 2])
                known[side, step - 1] = both[:, :LANES]
                known[side, step] = both[:, LANES:]

    for step in range(count):
        for tile in range(tiles):
            multiply(0, step * tiles + tile)
        data[1, step] = forward(1, product[step])

    for step in range(count):
        for tile in range(tiles):
            multiply(1, step * tiles + tile)
        partly[step] = backward(0, step)

    for step in range(count):
        result = (partly[step] + backward(1, step)).astype(ready.dtype)
        for part in range(2):
            for offset in range(near):
                ready[part * places + step * near + offset] = result[
                    offset * rows : (offset + 1) * rows, part * LANES : (part + 1) * LANES
                ]


def convolve_whole(sent, short_weight, owner, rows, forward_table, inverse_table):
    senders, height, _ = sent.shape
    block = forward_table.shape[2]
    length = senders // 2 * rows
    count = length // block
    taps = short_weight.shape[1]
    return pl.pallas_call(
        whole_kernel,
        out_shape=jax.ShapeDtypeStruct((senders, rows, LANES), jnp.bfloat16),
        grid_spec=pltpu.PrefetchScalarGridSpec(
            num_scalar_prefetch=1,
            grid=(1,),
            in_specs=[
                pl.BlockSpec(memory_space=pltpu.VMEM),
                pl.BlockSpec(memory_space=pltpu.VMEM),
                pl.BlockSpec((3, taps, LANES), lambda i, owner: (0, 0, owner[0])),
                pl.BlockSpec(memory_space=pltpu.VMEM),
            ],
            out_specs=pl.BlockSpec(memory_space=pltpu.VMEM),
            scratch_shapes=[
                pltpu.VMEM((count, block, 2 * LANES), jnp.bfloat16),
                pltpu.VMEM((count // 2, block, 2 * LANES), jnp.bfloat16),
                pltpu.VMEM((2, count, block, 2 * LANES), jnp.float32),
                pltpu.VMEM((2, count, block, LANES), jnp.float32),
                pltpu.VMEM((2, count, block, 2 * LANES), jnp.float32),
                pltpu.VMEM((count, block, 2 * LANES), jnp.float32),
            ],
        ),
        compiler_params=pltpu.CompilerParams(vmem_limit_bytes=32 * MIB),
        cost_estimate=pl.CostEstimate(
            flops=40 * length * block * LANES,
            bytes_accessed=2 * senders * (height + rows) * LANES,
            transcendentals=0,
        ),
    )(owner.reshape(1), forward_table, inverse_table, short_weight, sent)


def exchange(value, axes):
    return lax.all_to_all(value, axes, split_axis=0, concat_axis=0, tiled=True)


def on_device(query_in, key_in, value_in, long_filter, short_weight, skip_gain):
    places = lax.axis_size("seq")
    parts = lax.axis_size("groups")
    group = lax.axis_index("groups").astype(jnp.int32)
    place = lax.axis_index("seq").astype(jnp.int32)
    rows, channels = key_in.shape
    length = places * rows
    block = BLOCK if length % BLOCK == 0 else rows
    rim = short_weight.shape[1] - 1
    owners = parts * places
    count = length // block
    aligned = (
        parts == 2
        and rim == 2
        and channels == owners * LANES
        and rows % 32 == 0
        and block % rows == 0
        and block == BLOCK
        and count in (2, 4, 8)
    )
    forward_table, inverse_table = half_tables(block) if aligned else transform_tables(block)
    forward_table = jnp.asarray(forward_table)
    inverse_table = jnp.asarray(inverse_table)
    if aligned:
        sent, edges = pack(
            query_in, key_in, value_in, long_filter, short_weight, group, owners, parts
        )
        received = exchange(sent, ("groups", "seq"))
        edges = from_behind(edges, "seq")
        received, edges = lax.optimization_barrier((received, edges))
        owner = group * places + place
        convolved = convolve_whole(
            received, short_weight, owner, rows, forward_table, inverse_table
        )
        convolved = exchange(convolved, ("groups", "seq"))
        return finish(convolved, sent, query_in, edges, short_weight, skip_gain)
    else:
        width = channels // places
        edges = jnp.stack([query_in[-rim:], key_in[-rim:], value_in[-rim:]])
        sent = long_filter.reshape(rows, places, width).transpose(1, 0, 2)
        spectra = filter_spectra(exchange(sent, "seq").reshape(length, width), forward_table)
        edges = from_behind(edges, "seq")
        product = products(key_in, value_in, edges, short_weight)
        sent = product.reshape(rows, places, width).transpose(1, 0, 2)
        received = exchange(sent, "seq").reshape(length, width)
        convolved = convolve(received, spectra, forward_table, inverse_table)
        convolved = exchange(convolved.reshape(places, rows, width), "seq")
        convolved = convolved.transpose(1, 0, 2).reshape(rows, channels // LANES, LANES)
        convolved = convolved.transpose(1, 0, 2)
        return gate(convolved, product, query_in, edges, short_weight, skip_gain)


def solution(mesh):
    placed = (
        P(("groups", "seq"), None),
        P(("groups", "seq"), None),
        P(("groups", "seq"), None),
        P("seq", None),
        P(),
        P(),
    )
    return jax.shard_map(
        on_device, mesh=mesh, in_specs=placed, out_specs=P(("groups", "seq"), None), check_vma=False
    )
```

```python
import functools

import jax
import jax.numpy as jnp
import ml_dtypes
import numpy as np
from jax import lax
from jax.experimental import pallas as pl
from jax.experimental.pallas import tpu as pltpu
from jax.sharding import PartitionSpec as P

LANES = 128
SUBLANES = 8
BLOCK = 256
UNROLLED = 8
MIB = 1 << 20


def from_behind(value, axis):
    count = lax.axis_size(axis)
    return lax.ppermute(value, axis, [(source, source + 1) for source in range(count - 1)])


def transform_tables(block):
    numbers = np.concatenate([np.arange(0, block, 2), np.arange(1, block, 2)])
    quarter = (2 * numbers[:, None] + 1) * np.arange(block)[None, :] % (4 * block)
    angle = quarter.astype(np.float64) * (2.0 * np.pi / (4 * block))
    table = np.concatenate([np.cos(angle), -np.sin(angle)], axis=0)

    def split(values):
        high = values.astype(ml_dtypes.bfloat16)
        low = (values - high.astype(np.float64)).astype(ml_dtypes.bfloat16)
        return np.concatenate([high, low], axis=0)

    return split(table), split(table.T / block)


def half_tables(block):
    forward, inverse = transform_tables(block)
    half = block // 2
    rows = np.arange(2 * block).reshape(2, 2, half).transpose(1, 0, 2).reshape(2, block)
    forward = forward.reshape(2, 2 * block, block)
    forward = np.stack([forward[:, rows[side]].reshape(2 * block, block) for side in range(2)])
    inverse = np.stack([inverse[:, rows[side]] for side in range(2)])
    return forward, inverse


def shifted(values, edge, steps):
    rolled = pltpu.roll(values, steps, 0)
    row = lax.broadcasted_iota(jnp.int32, values.shape, 0)
    for place in range(steps):
        source = edge[edge.shape[0] - steps + place : edge.shape[0] - steps + place + 1]
        rolled = jnp.where(row == place, jnp.broadcast_to(source, values.shape), rolled)
    return rolled


def featurize_inside(own, taps):
    result = taps[0:1] * own
    for offset in range(1, taps.shape[0]):
        result = result + taps[offset : offset + 1] * pltpu.roll(own, offset, 0)
    return result


def featurize(own, edge, taps):
    own = own.astype(jnp.float32)
    edge = edge.astype(jnp.float32)
    top = own[:SUBLANES]
    first = taps[0:1] * top
    for offset in range(1, taps.shape[0]):
        first = first + taps[offset : offset + 1] * shifted(top, edge, offset)
    return jnp.concatenate([first, featurize_inside(own, taps)[SUBLANES:]], axis=0)


def product_kernel(key_ref, value_ref, edge_ref, taps_ref, out_ref):
    for start in range(0, key_ref.shape[1], LANES):
        span = slice(start, start + LANES)
        k_short = featurize(key_ref[:, span], edge_ref[1, :, span], taps_ref[1, :, span])
        v_short = featurize(value_ref[:, span], edge_ref[2, :, span], taps_ref[2, :, span])
        out_ref[:, span] = (k_short * v_short).astype(out_ref.dtype)


def products(key_in, value_in, edges, short_weight):
    rows, channels = key_in.shape
    span = min(channels, 1024)
    taps = short_weight.shape[1]
    return pl.pallas_call(
        product_kernel,
        out_shape=jax.ShapeDtypeStruct((rows, channels), jnp.bfloat16),
        grid=(channels // span,),
        in_specs=[
            pl.BlockSpec((rows, span), lambda i: (0, i)),
            pl.BlockSpec((rows, span), lambda i: (0, i)),
            pl.BlockSpec((3, taps - 1, span), lambda i: (0, 0, i)),
            pl.BlockSpec((3, taps, span), lambda i: (0, 0, i)),
        ],
        out_specs=pl.BlockSpec((rows, span), lambda i: (0, i)),
        cost_estimate=pl.CostEstimate(
            flops=12 * rows * channels, bytes_accessed=6 * rows * channels, transcendentals=0
        ),
    )(key_in, value_in, edges, short_weight)


def gate_kernel(conv_ref, product_ref, query_ref, edge_ref, taps_ref, gain_ref, out_ref):
    for part in range(conv_ref.shape[0]):
        span = slice(part * LANES, (part + 1) * LANES)
        q_short = featurize(query_ref[:, span], edge_ref[0, :, span], taps_ref[0, :, span])
        mixed = conv_ref[part].astype(jnp.float32) + gain_ref[:, span] * product_ref[
            :, span
        ].astype(jnp.float32)
        out_ref[:, span] = (q_short * mixed).astype(out_ref.dtype)


def gate(convolved, product, query_in, edges, short_weight, skip_gain):
    rows, channels = query_in.shape
    span = min(channels, 1024)
    taps = short_weight.shape[1]
    across = pl.BlockSpec((rows, span), lambda i: (0, i))
    return pl.pallas_call(
        gate_kernel,
        out_shape=jax.ShapeDtypeStruct((rows, channels), jnp.bfloat16),
        grid=(channels // span,),
        in_specs=[
            pl.BlockSpec((span // LANES, rows, LANES), lambda i: (i, 0, 0)),
            across,
            across,
            pl.BlockSpec((3, taps - 1, span), lambda i: (0, 0, i)),
            pl.BlockSpec((3, taps, span), lambda i: (0, 0, i)),
            pl.BlockSpec((1, span), lambda i: (0, i)),
        ],
        out_specs=across,
        cost_estimate=pl.CostEstimate(
            flops=9 * rows * channels, bytes_accessed=8 * rows * channels, transcendentals=0
        ),
    )(convolved, product, query_in, edges, short_weight, skip_gain.reshape(1, channels))


def prepare_kernel(sent_ref, query_ref, taps_ref, gain_ref, short_ref, direct_ref):
    owners, rows, _ = short_ref.shape
    for owner in range(owners):
        lanes = slice(owner * LANES, (owner + 1) * LANES)
        q_short = featurize_inside(query_ref[:, lanes].astype(jnp.float32), taps_ref[0, :, lanes])
        product = sent_ref[owner, :rows].astype(jnp.float32)
        short_ref[owner] = q_short
        direct_ref[owner] = q_short * (gain_ref[:, lanes] * product)


def prepare(sent, query_in, short_weight, skip_gain):
    rows, channels = query_in.shape
    owners, height, _ = sent.shape
    near = min(owners, 8)
    span = near * LANES
    taps = short_weight.shape[1]
    out = pl.BlockSpec((near, rows, LANES), lambda i: (i, 0, 0))
    return pl.pallas_call(
        prepare_kernel,
        out_shape=(jax.ShapeDtypeStruct((owners, rows, LANES), jnp.float32),) * 2,
        grid=(owners // near,),
        in_specs=[
            pl.BlockSpec((near, height, LANES), lambda i: (i, 0, 0)),
            pl.BlockSpec((rows, span), lambda i: (0, i)),
            pl.BlockSpec((3, taps, span), lambda i: (0, 0, i)),
            pl.BlockSpec((1, span), lambda i: (0, i)),
        ],
        out_specs=(out, out),
        cost_estimate=pl.CostEstimate(
            flops=8 * rows * channels, bytes_accessed=12 * rows * channels, transcendentals=0
        ),
    )(sent, query_in, short_weight, skip_gain.reshape(1, channels))


def finish_kernel(
    conv_ref, short_ref, direct_ref, sent_ref, query_ref, edge_ref, taps_ref, gain_ref, out_ref,
    ready, sems,
):
    rows, channels = ready.shape
    tail = sent_ref.shape[1] - SUBLANES
    chunks = sems.shape[0]
    span = channels // chunks
    near = span // LANES
    row = lax.broadcasted_iota(jnp.int32, (SUBLANES, LANES), 0)

    def departure(chunk):
        columns = pl.ds(pl.multiple_of(chunk * span, span), span)
        return pltpu.make_async_copy(ready.at[:, columns], out_ref.at[:, columns], sems.at[chunk])

    @pl.loop(0, chunks)
    def _(chunk):
        for part in range(near):
            owner = chunk * near + part
            lanes = pl.ds(pl.multiple_of(owner * LANES, LANES), LANES)
            behind = edge_ref[:, lanes].astype(jnp.float32)
            own = sent_ref[owner, tail:].astype(jnp.float32)
            first = first_products(own, behind, tap_tiles(taps_ref, lanes))
            first = first.astype(jnp.bfloat16).astype(jnp.float32)
            product = sent_ref[owner, :SUBLANES].astype(jnp.float32)
            product = jnp.where(row < 2, first, product)

            weights = taps_ref[0, :, lanes]
            top = query_ref[:SUBLANES, lanes].astype(jnp.float32)
            one = jnp.where(row < 1, pltpu.roll(behind, 5, 0), pltpu.roll(top, 1, 0))
            two = jnp.where(row < 2, pltpu.roll(behind, 6, 0), pltpu.roll(top, 2, 0))
            top = weights[0:1] * top + weights[1:2] * one + weights[2:3] * two

            convolved = conv_ref[owner].astype(jnp.float32)
            top = top * convolved[:SUBLANES] + top * (gain_ref[:, lanes] * product)
            result = short_ref[owner] * convolved + direct_ref[owner]
            result = jnp.concatenate([top, result[SUBLANES:]], axis=0)
            ready[:, lanes] = result.astype(ready.dtype)
        departure(chunk).start()

    for chunk in range(chunks):
        departure(chunk).wait()


def finish(convolved, prepared, sent, query_in, edges, short_weight, skip_gain):
    rows, channels = query_in.shape
    chunks = max(1, channels // 512)
    here = pl.BlockSpec(memory_space=pltpu.VMEM)
    return pl.pallas_call(
        finish_kernel,
        out_shape=jax.ShapeDtypeStruct((rows, channels), jnp.bfloat16),
        in_specs=[here] * 8,
        out_specs=pl.BlockSpec(memory_space=pltpu.HBM),
        scratch_shapes=[
            pltpu.VMEM((rows, channels), jnp.bfloat16),
            pltpu.SemaphoreType.DMA((chunks,)),
        ],
        compiler_params=pltpu.CompilerParams(vmem_limit_bytes=8 * MIB),
        cost_estimate=pl.CostEstimate(
            flops=3 * rows * channels, bytes_accessed=12 * rows * channels, transcendentals=0
        ),
    )(
        convolved, *prepared, sent, query_in, edges, short_weight, skip_gain.reshape(1, channels)
    )


def tap_tiles(taps_ref, lanes):
    row = lax.broadcasted_iota(jnp.int32, (SUBLANES, LANES), 0)
    return [
        jnp.where(row < 4, taps_ref[1, tap : tap + 1, lanes], taps_ref[2, tap : tap + 1, lanes])
        for tap in range(taps_ref.shape[1])
    ]


def first_products(tile, behind, weights):
    row = lax.broadcasted_iota(jnp.int32, (SUBLANES, LANES), 0)
    joined = jnp.where(row % 4 >= 2, tile, behind)
    short = weights[0] * joined
    for tap in range(1, len(weights)):
        short = short + weights[tap] * pltpu.roll(joined, tap, 0)
    return pltpu.roll(short * pltpu.roll(short, 4, 0), 6, 0)


def pack_kernel(
    group_ref, query_ref, key_ref, value_ref, filter_ref, taps_ref, out_ref, edges_ref,
    query, key, value, filters, taps, packed, edges, in_sems, one_sems, out_sems,
):
    rows, channels = key.shape
    share = filters.shape[0]
    chunks = out_sems.shape[0]
    span = channels // chunks
    near = span // LANES
    start = pl.multiple_of(group_ref[0] * share, share)
    whole = [
        pltpu.make_async_copy(taps_ref, taps, one_sems.at[0]),
        pltpu.make_async_copy(query_ref.at[pl.ds(rows - SUBLANES, SUBLANES)], query, one_sems.at[1]),
    ]

    def arrivals(chunk):
        columns = pl.ds(pl.multiple_of(chunk * span, span), span)
        return [
            pltpu.make_async_copy(key_ref.at[:, columns], key.at[:, columns], in_sems.at[0, chunk]),
            pltpu.make_async_copy(
                value_ref.at[:, columns], value.at[:, columns], in_sems.at[1, chunk]
            ),
            pltpu.make_async_copy(
                filter_ref.at[pl.ds(start, share), columns],
                filters.at[:, columns],
                in_sems.at[2, chunk],
            ),
        ]

    def departure(chunk):
        owners = pl.ds(chunk * near, near)
        return pltpu.make_async_copy(packed.at[owners], out_ref.at[owners], out_sems.at[chunk])

    for copy in whole:
        copy.start()
    for chunk in range(chunks):
        for copy in arrivals(chunk):
            copy.start()
    for copy in whole:
        copy.wait()
    row = lax.broadcasted_iota(jnp.int32, (SUBLANES, LANES), 0)

    @pl.loop(0, chunks)
    def _(chunk):
        for copy in arrivals(chunk):
            copy.wait()
        for part in range(near):
            span_here = pl.ds(pl.multiple_of(chunk * span + part * LANES, LANES), LANES)
            owner = chunk * near + part
            key_here = key[:, span_here].astype(jnp.float32)
            value_here = value[:, span_here].astype(jnp.float32)
            k_short = featurize_inside(key_here, taps[1, :, span_here])
            v_short = featurize_inside(value_here, taps[2, :, span_here])
            packed[owner, :rows] = (k_short * v_short).astype(packed.dtype)
            packed[owner, rows : rows + share] = filters[:, span_here]
            query_last = pltpu.roll(query[:, span_here].astype(jnp.float32), 4, 0)
            key_tile = jnp.where(
                row < 2,
                pltpu.roll(key_here[rows - SUBLANES :], 2, 0),
                pltpu.roll(key_here[:SUBLANES], 2, 0),
            )
            value_tile = jnp.where(
                row < 6,
                pltpu.roll(value_here[rows - SUBLANES :], 6, 0),
                pltpu.roll(value_here[:SUBLANES], 6, 0),
            )
            edge = jnp.where(row < 4, key_tile, value_tile)
            packed[owner, rows + share :] = edge.astype(packed.dtype)
            edge = jnp.where((row == 2) | (row == 3), query_last, edge)
            edges[:, span_here] = edge.astype(edges.dtype)
        departure(chunk).start()

    last = pltpu.make_async_copy(edges, edges_ref, one_sems.at[0])
    last.start()
    for chunk in range(chunks):
        departure(chunk).wait()
    last.wait()


def pack(query_in, key_in, value_in, long_filter, short_weight, group, owners, parts):
    rows, channels = key_in.shape
    chunks = max(1, channels // 1024)
    taps = short_weight.shape[1]
    share = rows // parts
    height = rows + share + SUBLANES
    here = pl.BlockSpec(memory_space=pltpu.HBM)
    return pl.pallas_call(
        pack_kernel,
        out_shape=(
            jax.ShapeDtypeStruct((owners, height, LANES), jnp.bfloat16),
            jax.ShapeDtypeStruct((SUBLANES, channels), jnp.bfloat16),
        ),
        in_specs=[pl.BlockSpec(memory_space=pltpu.SMEM)] + [here] * 5,
        out_specs=(here, here),
        scratch_shapes=[
            pltpu.VMEM((SUBLANES, channels), jnp.bfloat16),
            pltpu.VMEM((rows, channels), jnp.bfloat16),
            pltpu.VMEM((rows, channels), jnp.bfloat16),
            pltpu.VMEM((share, channels), jnp.bfloat16),
            pltpu.VMEM((3, taps, channels), jnp.float32),
            pltpu.VMEM((owners, height, LANES), jnp.bfloat16),
            pltpu.VMEM((SUBLANES, channels), jnp.bfloat16),
            pltpu.SemaphoreType.DMA((3, chunks)),
            pltpu.SemaphoreType.DMA((2,)),
            pltpu.SemaphoreType.DMA((chunks,)),
        ],
        cost_estimate=pl.CostEstimate(
            flops=12 * rows * channels, bytes_accessed=8 * rows * channels, transcendentals=0
        ),
    )(group.reshape(1), query_in, key_in, value_in, long_filter, short_weight)


def transform(table, values):
    both = jnp.dot(table, values, preferred_element_type=jnp.float32)
    half = table.shape[0] // 2
    return both[:half] + both[half:]


def over(count, body):
    if count <= UNROLLED:
        for step in range(count):
            body(step)
    else:

        @pl.loop(0, count)
        def _(step):
            body(step)


def filter_kernel(table_ref, filter_ref, out_ref):
    count, double, _ = out_ref.shape
    block = double // 2

    def body(step):
        start = step * block
        if not isinstance(step, int):
            start = pl.multiple_of(start, block)
        out_ref[step] = transform(table_ref[...], filter_ref[pl.ds(start, block), :])

    over(count, body)


def filter_spectra(long_filter, table):
    length, width = long_filter.shape
    block = table.shape[1]
    return pl.pallas_call(
        filter_kernel,
        out_shape=jax.ShapeDtypeStruct((length // block, 2 * block, width), jnp.float32),
        in_specs=[pl.BlockSpec(memory_space=pltpu.VMEM)] * 2,
        out_specs=pl.BlockSpec(memory_space=pltpu.VMEM),
        compiler_params=pltpu.CompilerParams(vmem_limit_bytes=40 * MIB),
        cost_estimate=pl.CostEstimate(
            flops=8 * length * block * width, bytes_accessed=10 * length * width, transcendentals=0
        ),
    )(table, long_filter)


def inverse(table_ref, values, block):
    high = values.astype(jnp.bfloat16)
    low = (values - high.astype(jnp.float32)).astype(jnp.bfloat16)
    return transform(table_ref[...], high) + jnp.dot(
        table_ref[:block], low, preferred_element_type=jnp.float32
    )


def conv_kernel(forward_ref, inverse_ref, product_ref, filter_ref, out_ref, data, mixed, last):
    count, double, width = filter_ref.shape
    block = double // 2
    lane_step = min(width, LANES)

    def piece(step):
        start = step * block
        return pl.ds(start if isinstance(step, int) else pl.multiple_of(start, block), block)

    def forward(step):
        data[step] = transform(forward_ref[...], product_ref[piece(step), :])

    over(count, forward)
    last[...] = jnp.zeros_like(last)

    @pl.loop(0, count)
    def _(total):
        for sign, base in ((1.0, 0), (-1.0, block // 2)):
            for column in range(0, width, lane_step):
                lanes = slice(column, column + lane_step)

                @pl.loop(0, block // 2 // SUBLANES)
                def _(index):
                    start = pl.multiple_of(base + index * SUBLANES, SUBLANES)
                    real = pl.ds(start, SUBLANES)
                    imag = pl.ds(pl.multiple_of(block + start, SUBLANES), SUBLANES)

                    def add(step, sums):
                        a, b = data[step, real, lanes], data[step, imag, lanes]
                        c = filter_ref[total - step, real, lanes]
                        d = filter_ref[total - step, imag, lanes]
                        return sums[0] + (a * c - b * d), sums[1] + (a * d + b * c)

                    zero = jnp.zeros((SUBLANES, lane_step), jnp.float32)
                    sum_real, sum_imag = lax.fori_loop(0, total + 1, add, (zero, zero))
                    mixed[real, lanes] = sum_real - sign * last[imag, lanes]
                    mixed[imag, lanes] = sum_imag + sign * last[real, lanes]
                    last[real, lanes] = sum_real
                    last[imag, lanes] = sum_imag

        out_ref[piece(total), :] = inverse(inverse_ref, mixed[...], block).astype(out_ref.dtype)


def convolve(product, spectra, forward_table, inverse_table):
    length, width = product.shape
    count, double, _ = spectra.shape
    return pl.pallas_call(
        conv_kernel,
        out_shape=jax.ShapeDtypeStruct((length, width), jnp.bfloat16),
        in_specs=[pl.BlockSpec(memory_space=pltpu.VMEM)] * 4,
        out_specs=pl.BlockSpec(memory_space=pltpu.VMEM),
        scratch_shapes=[
            pltpu.VMEM((count, double, width), jnp.float32),
            pltpu.VMEM((double, width), jnp.float32),
            pltpu.VMEM((double, width), jnp.float32),
        ],
        compiler_params=pltpu.CompilerParams(vmem_limit_bytes=56 * MIB),
        cost_estimate=pl.CostEstimate(
            flops=16 * length * double * width,
            bytes_accessed=12 * length * width,
            transcendentals=0,
        ),
    )(forward_table, inverse_table, product, spectra)


def whole_kernel(
    owner_ref, forward_ref, inverse_ref, taps_ref, arrived, ready,
    product, filters, data, known, mixed, partly,
):
    del owner_ref
    senders, rows, _ = ready.shape
    places = senders // 2
    share = rows // 2
    _, count, block, _ = data.shape
    half = block // 2
    near = block // rows
    tiles = half // SUBLANES // count
    row = lax.broadcasted_iota(jnp.int32, (SUBLANES, LANES), 0)
    weights = tap_tiles(taps_ref, slice(None))

    def forward(side, values):
        return transform(forward_ref[side], values)

    def backward(side, step):
        return inverse(inverse_ref.at[side], mixed[side, step], block)

    def multiply(side, tile):
        start = tile * SUBLANES
        real = slice(start, start + SUBLANES)
        imag = slice(half + start, half + start + SUBLANES)
        filter_parts = []
        for step in range(count):
            c, d = known[side, step, real], known[side, step, imag]
            filter_parts.append((c, d - c, c + d))
        for part in range(2):
            lanes = slice(part * LANES, (part + 1) * LANES)
            data_parts = []
            for step in range(count):
                a, b = data[side, step, real, lanes], data[side, step, imag, lanes]
                data_parts.append((a + b, a, b))
            before = None
            for total in range(count):
                sums = None
                for step in range(total + 1):
                    pairs = zip(data_parts[step], filter_parts[total - step])
                    terms = [x * y for x, y in pairs]
                    sums = terms if sums is None else [x + y for x, y in zip(sums, terms)]
                both = (sums[0] - sums[2], sums[0] + sums[1])
                if before is None:
                    out = both
                elif side == 0:
                    out = (both[0] - before[1], both[1] + before[0])
                else:
                    out = (both[0] + before[1], both[1] - before[0])
                mixed[side, total, real, lanes] = out[0]
                mixed[side, total, imag, lanes] = out[1]
                before = both

    behind = [jnp.zeros((SUBLANES, LANES), jnp.float32)] * 2
    for step in range(count):
        for part in range(2):
            lanes = slice(part * LANES, (part + 1) * LANES)
            for offset in range(near):
                sender = part * places + step * near + offset
                edge = arrived[sender, rows + share :].astype(jnp.float32)
                first = first_products(edge, behind[part], weights)
                behind[part] = edge
                values = arrived[sender, : 2 * SUBLANES].astype(jnp.float32)
                top = jnp.where(row < 2, first, values[:SUBLANES])
                values = jnp.concatenate([top, values[SUBLANES:]], axis=0)
                start = offset * rows
                product[step, start : start + 2 * SUBLANES, lanes] = values.astype(product.dtype)
                product[step, start + 2 * SUBLANES : start + rows, lanes] = arrived[
                    sender, 2 * SUBLANES : rows
                ]
                start = offset * rows + part * share
                place = (step % 2) * LANES
                filters[step // 2, start : start + share, place : place + LANES] = arrived[
                    sender, rows : rows + share
                ]
        data[0, step] = forward(0, product[step])
        if step % 2:
            for side in range(2):
                both = forward(side, filters[step // 2])
                known[side, step - 1] = both[:, :LANES]
                known[side, step] = both[:, LANES:]

    for step in range(count):
        for tile in range(tiles):
            multiply(0, step * tiles + tile)
        data[1, step] = forward(1, product[step])

    for step in range(count):
        for tile in range(tiles):
            multiply(1, step * tiles + tile)
        partly[step] = backward(0, step)

    for step in range(count):
        result = (partly[step] + backward(1, step)).astype(ready.dtype)
        for part in range(2):
            for offset in range(near):
                ready[part * places + step * near + offset] = result[
                    offset * rows : (offset + 1) * rows, part * LANES : (part + 1) * LANES
                ]


def convolve_whole(sent, short_weight, owner, rows, forward_table, inverse_table):
    senders, height, _ = sent.shape
    block = forward_table.shape[2]
    length = senders // 2 * rows
    count = length // block
    taps = short_weight.shape[1]
    return pl.pallas_call(
        whole_kernel,
        out_shape=jax.ShapeDtypeStruct((senders, rows, LANES), jnp.bfloat16),
        grid_spec=pltpu.PrefetchScalarGridSpec(
            num_scalar_prefetch=1,
            grid=(1,),
            in_specs=[
                pl.BlockSpec(memory_space=pltpu.VMEM),
                pl.BlockSpec(memory_space=pltpu.VMEM),
                pl.BlockSpec((3, taps, LANES), lambda i, owner: (0, 0, owner[0])),
                pl.BlockSpec(memory_space=pltpu.VMEM),
            ],
            out_specs=pl.BlockSpec(memory_space=pltpu.VMEM),
            scratch_shapes=[
                pltpu.VMEM((count, block, 2 * LANES), jnp.bfloat16),
                pltpu.VMEM((count // 2, block, 2 * LANES), jnp.bfloat16),
                pltpu.VMEM((2, count, block, 2 * LANES), jnp.float32),
                pltpu.VMEM((2, count, block, LANES), jnp.float32),
                pltpu.VMEM((2, count, block, 2 * LANES), jnp.float32),
                pltpu.VMEM((count, block, 2 * LANES), jnp.float32),
            ],
        ),
        compiler_params=pltpu.CompilerParams(vmem_limit_bytes=32 * MIB),
        cost_estimate=pl.CostEstimate(
            flops=40 * length * block * LANES,
            bytes_accessed=2 * senders * (height + rows) * LANES,
            transcendentals=0,
        ),
    )(owner.reshape(1), forward_table, inverse_table, short_weight, sent)


def exchange(value, axes):
    return lax.all_to_all(value, axes, split_axis=0, concat_axis=0, tiled=True)


def on_device(query_in, key_in, value_in, long_filter, short_weight, skip_gain):
    places = lax.axis_size("seq")
    parts = lax.axis_size("groups")
    group = lax.axis_index("groups").astype(jnp.int32)
    place = lax.axis_index("seq").astype(jnp.int32)
    rows, channels = key_in.shape
    length = places * rows
    block = BLOCK if length % BLOCK == 0 else rows
    rim = short_weight.shape[1] - 1
    owners = parts * places
    count = length // block
    aligned = (
        parts == 2
        and rim == 2
        and channels == owners * LANES
        and rows % 32 == 0
        and block % rows == 0
        and block == BLOCK
        and count in (2, 4, 8)
    )
    forward_table, inverse_table = half_tables(block) if aligned else transform_tables(block)
    forward_table = jnp.asarray(forward_table)
    inverse_table = jnp.asarray(inverse_table)
    if aligned:
        sent, edges = pack(
            query_in, key_in, value_in, long_filter, short_weight, group, owners, parts
        )
        received = exchange(sent, ("groups", "seq"))
        edges = from_behind(edges, "seq")
        prepared = prepare(sent, query_in, short_weight, skip_gain)
        received, edges, prepared = lax.optimization_barrier((received, edges, prepared))
        owner = group * places + place
        convolved = convolve_whole(
            received, short_weight, owner, rows, forward_table, inverse_table
        )
        convolved = exchange(convolved, ("groups", "seq"))
        return finish(
            convolved, prepared, sent, query_in, edges, short_weight, skip_gain
        )
    else:
        width = channels // places
        edges = jnp.stack([query_in[-rim:], key_in[-rim:], value_in[-rim:]])
        sent = long_filter.reshape(rows, places, width).transpose(1, 0, 2)
        spectra = filter_spectra(exchange(sent, "seq").reshape(length, width), forward_table)
        edges = from_behind(edges, "seq")
        product = products(key_in, value_in, edges, short_weight)
        sent = product.reshape(rows, places, width).transpose(1, 0, 2)
        received = exchange(sent, "seq").reshape(length, width)
        convolved = convolve(received, spectra, forward_table, inverse_table)
        convolved = exchange(convolved.reshape(places, rows, width), "seq")
        convolved = convolved.transpose(1, 0, 2).reshape(rows, channels // LANES, LANES)
        convolved = convolved.transpose(1, 0, 2)
        return gate(convolved, product, query_in, edges, short_weight, skip_gain)


def solution(mesh):
    placed = (
        P(("groups", "seq"), None),
        P(("groups", "seq"), None),
        P(("groups", "seq"), None),
        P("seq", None),
        P(),
        P(),
    )
    return jax.shard_map(
        on_device, mesh=mesh, in_specs=placed, out_specs=P(("groups", "seq"), None), check_vma=False
    )
```

```python
import functools

import jax
import jax.numpy as jnp
import ml_dtypes
import numpy as np
from jax import lax
from jax.experimental import pallas as pl
from jax.experimental.pallas import tpu as pltpu
from jax.sharding import PartitionSpec as P

LANES = 128
SUBLANES = 8
BLOCK = 256
UNROLLED = 8
MIB = 1 << 20


def from_behind(value, axis):
    count = lax.axis_size(axis)
    return lax.ppermute(value, axis, [(source, source + 1) for source in range(count - 1)])


def transform_tables(block):
    numbers = np.concatenate([np.arange(0, block, 2), np.arange(1, block, 2)])
    quarter = (2 * numbers[:, None] + 1) * np.arange(block)[None, :] % (4 * block)
    angle = quarter.astype(np.float64) * (2.0 * np.pi / (4 * block))
    table = np.concatenate([np.cos(angle), -np.sin(angle)], axis=0)

    def split(values):
        high = values.astype(ml_dtypes.bfloat16)
        low = (values - high.astype(np.float64)).astype(ml_dtypes.bfloat16)
        return np.concatenate([high, low], axis=0)

    return split(table), split(table.T / block)


def half_tables(block):
    forward, inverse = transform_tables(block)
    half = block // 2
    rows = np.arange(2 * block).reshape(2, 2, half).transpose(1, 0, 2).reshape(2, block)
    forward = forward.reshape(2, 2 * block, block)
    forward = np.stack([forward[:, rows[side]].reshape(2 * block, block) for side in range(2)])
    inverse = np.stack([inverse[:, rows[side]] for side in range(2)])
    return forward, inverse


def shifted(values, edge, steps):
    rolled = pltpu.roll(values, steps, 0)
    row = lax.broadcasted_iota(jnp.int32, values.shape, 0)
    for place in range(steps):
        source = edge[edge.shape[0] - steps + place : edge.shape[0] - steps + place + 1]
        rolled = jnp.where(row == place, jnp.broadcast_to(source, values.shape), rolled)
    return rolled


def featurize_inside(own, taps):
    result = taps[0:1] * own
    for offset in range(1, taps.shape[0]):
        result = result + taps[offset : offset + 1] * pltpu.roll(own, offset, 0)
    return result


def featurize(own, edge, taps):
    own = own.astype(jnp.float32)
    edge = edge.astype(jnp.float32)
    top = own[:SUBLANES]
    first = taps[0:1] * top
    for offset in range(1, taps.shape[0]):
        first = first + taps[offset : offset + 1] * shifted(top, edge, offset)
    return jnp.concatenate([first, featurize_inside(own, taps)[SUBLANES:]], axis=0)


def product_kernel(key_ref, value_ref, edge_ref, taps_ref, out_ref):
    for start in range(0, key_ref.shape[1], LANES):
        span = slice(start, start + LANES)
        k_short = featurize(key_ref[:, span], edge_ref[1, :, span], taps_ref[1, :, span])
        v_short = featurize(value_ref[:, span], edge_ref[2, :, span], taps_ref[2, :, span])
        out_ref[:, span] = (k_short * v_short).astype(out_ref.dtype)


def products(key_in, value_in, edges, short_weight):
    rows, channels = key_in.shape
    span = min(channels, 1024)
    taps = short_weight.shape[1]
    return pl.pallas_call(
        product_kernel,
        out_shape=jax.ShapeDtypeStruct((rows, channels), jnp.bfloat16),
        grid=(channels // span,),
        in_specs=[
            pl.BlockSpec((rows, span), lambda i: (0, i)),
            pl.BlockSpec((rows, span), lambda i: (0, i)),
            pl.BlockSpec((3, taps - 1, span), lambda i: (0, 0, i)),
            pl.BlockSpec((3, taps, span), lambda i: (0, 0, i)),
        ],
        out_specs=pl.BlockSpec((rows, span), lambda i: (0, i)),
        cost_estimate=pl.CostEstimate(
            flops=12 * rows * channels, bytes_accessed=6 * rows * channels, transcendentals=0
        ),
    )(key_in, value_in, edges, short_weight)


def gate_kernel(conv_ref, product_ref, query_ref, edge_ref, taps_ref, gain_ref, out_ref):
    for part in range(conv_ref.shape[0]):
        span = slice(part * LANES, (part + 1) * LANES)
        q_short = featurize(query_ref[:, span], edge_ref[0, :, span], taps_ref[0, :, span])
        mixed = conv_ref[part].astype(jnp.float32) + gain_ref[:, span] * product_ref[
            :, span
        ].astype(jnp.float32)
        out_ref[:, span] = (q_short * mixed).astype(out_ref.dtype)


def gate(convolved, product, query_in, edges, short_weight, skip_gain):
    rows, channels = query_in.shape
    span = min(channels, 1024)
    taps = short_weight.shape[1]
    across = pl.BlockSpec((rows, span), lambda i: (0, i))
    return pl.pallas_call(
        gate_kernel,
        out_shape=jax.ShapeDtypeStruct((rows, channels), jnp.bfloat16),
        grid=(channels // span,),
        in_specs=[
            pl.BlockSpec((span // LANES, rows, LANES), lambda i: (i, 0, 0)),
            across,
            across,
            pl.BlockSpec((3, taps - 1, span), lambda i: (0, 0, i)),
            pl.BlockSpec((3, taps, span), lambda i: (0, 0, i)),
            pl.BlockSpec((1, span), lambda i: (0, i)),
        ],
        out_specs=across,
        cost_estimate=pl.CostEstimate(
            flops=9 * rows * channels, bytes_accessed=8 * rows * channels, transcendentals=0
        ),
    )(convolved, product, query_in, edges, short_weight, skip_gain.reshape(1, channels))


def prepare_kernel(sent_ref, query_ref, taps_ref, gain_ref, short_ref, direct_ref):
    owners, rows, _ = short_ref.shape
    for owner in range(owners):
        lanes = slice(owner * LANES, (owner + 1) * LANES)
        q_short = featurize_inside(query_ref[:, lanes].astype(jnp.float32), taps_ref[0, :, lanes])
        product = sent_ref[owner, :rows].astype(jnp.float32)
        short_ref[owner] = q_short
        direct_ref[owner] = q_short * (gain_ref[:, lanes] * product)


def prepare(sent, query_in, short_weight, skip_gain):
    rows, channels = query_in.shape
    owners, height, _ = sent.shape
    near = min(owners, 8)
    span = near * LANES
    taps = short_weight.shape[1]
    out = pl.BlockSpec((near, rows, LANES), lambda i: (i, 0, 0))
    return pl.pallas_call(
        prepare_kernel,
        out_shape=(jax.ShapeDtypeStruct((owners, rows, LANES), jnp.float32),) * 2,
        grid=(owners // near,),
        in_specs=[
            pl.BlockSpec((near, height, LANES), lambda i: (i, 0, 0)),
            pl.BlockSpec((rows, span), lambda i: (0, i)),
            pl.BlockSpec((3, taps, span), lambda i: (0, 0, i)),
            pl.BlockSpec((1, span), lambda i: (0, i)),
        ],
        out_specs=(out, out),
        cost_estimate=pl.CostEstimate(
            flops=8 * rows * channels, bytes_accessed=12 * rows * channels, transcendentals=0
        ),
    )(sent, query_in, short_weight, skip_gain.reshape(1, channels))


def finish_kernel(
    conv_ref, short_ref, direct_ref, sent_ref, query_ref, edge_ref, taps_ref, gain_ref, out_ref,
    ready, sems,
):
    rows, channels = ready.shape
    tail = sent_ref.shape[1] - SUBLANES
    chunks = sems.shape[0]
    span = channels // chunks
    near = span // LANES
    row = lax.broadcasted_iota(jnp.int32, (SUBLANES, LANES), 0)

    def departure(chunk):
        columns = pl.ds(pl.multiple_of(chunk * span, span), span)
        return pltpu.make_async_copy(ready.at[:, columns], out_ref.at[:, columns], sems.at[chunk])

    @pl.loop(0, chunks)
    def _(chunk):
        for part in range(near):
            owner = chunk * near + part
            lanes = pl.ds(pl.multiple_of(owner * LANES, LANES), LANES)
            behind = edge_ref[:, lanes].astype(jnp.float32)
            own = sent_ref[owner, tail:].astype(jnp.float32)
            first = first_products(own, behind, tap_tiles(taps_ref, lanes))
            first = first.astype(jnp.bfloat16).astype(jnp.float32)
            product = sent_ref[owner, :SUBLANES].astype(jnp.float32)
            product = jnp.where(row < 2, first, product)

            weights = taps_ref[0, :, lanes]
            top = query_ref[:SUBLANES, lanes].astype(jnp.float32)
            one = jnp.where(row < 1, pltpu.roll(behind, 5, 0), pltpu.roll(top, 1, 0))
            two = jnp.where(row < 2, pltpu.roll(behind, 6, 0), pltpu.roll(top, 2, 0))
            top = weights[0:1] * top + weights[1:2] * one + weights[2:3] * two

            convolved = conv_ref[owner].astype(jnp.float32)
            top = top * convolved[:SUBLANES] + top * (gain_ref[:, lanes] * product)
            result = short_ref[owner] * convolved + direct_ref[owner]
            result = jnp.concatenate([top, result[SUBLANES:]], axis=0)
            ready[:, lanes] = result.astype(ready.dtype)
        departure(chunk).start()

    for chunk in range(chunks):
        departure(chunk).wait()


def finish(convolved, prepared, sent, query_in, edges, short_weight, skip_gain):
    rows, channels = query_in.shape
    chunks = max(1, channels // 512)
    here = pl.BlockSpec(memory_space=pltpu.VMEM)
    return pl.pallas_call(
        finish_kernel,
        out_shape=jax.ShapeDtypeStruct((rows, channels), jnp.bfloat16),
        in_specs=[here] * 8,
        out_specs=pl.BlockSpec(memory_space=pltpu.HBM),
        scratch_shapes=[
            pltpu.VMEM((rows, channels), jnp.bfloat16),
            pltpu.SemaphoreType.DMA((chunks,)),
        ],
        compiler_params=pltpu.CompilerParams(vmem_limit_bytes=8 * MIB),
        cost_estimate=pl.CostEstimate(
            flops=3 * rows * channels, bytes_accessed=12 * rows * channels, transcendentals=0
        ),
    )(
        convolved, *prepared, sent, query_in, edges, short_weight, skip_gain.reshape(1, channels)
    )


def tap_tiles(taps_ref, lanes):
    row = lax.broadcasted_iota(jnp.int32, (SUBLANES, LANES), 0)
    return [
        jnp.where(row < 4, taps_ref[1, tap : tap + 1, lanes], taps_ref[2, tap : tap + 1, lanes])
        for tap in range(taps_ref.shape[1])
    ]


def first_products(tile, behind, weights):
    row = lax.broadcasted_iota(jnp.int32, (SUBLANES, LANES), 0)
    joined = jnp.where(row % 4 >= 2, tile, behind)
    short = weights[0] * joined
    for tap in range(1, len(weights)):
        short = short + weights[tap] * pltpu.roll(joined, tap, 0)
    return pltpu.roll(short * pltpu.roll(short, 4, 0), 6, 0)


def pack_kernel(
    group_ref, query_ref, key_ref, value_ref, filter_ref, taps_ref, out_ref, edges_ref,
    query, key, value, filters, taps, packed, edges, in_sems, one_sems, out_sems,
):
    rows, channels = key.shape
    share = filters.shape[0]
    chunks = out_sems.shape[0]
    span = channels // chunks
    near = span // LANES
    start = pl.multiple_of(group_ref[0] * share, share)
    whole = [
        pltpu.make_async_copy(taps_ref, taps, one_sems.at[0]),
        pltpu.make_async_copy(query_ref.at[pl.ds(rows - SUBLANES, SUBLANES)], query, one_sems.at[1]),
    ]

    def arrivals(chunk):
        columns = pl.ds(pl.multiple_of(chunk * span, span), span)
        return [
            pltpu.make_async_copy(key_ref.at[:, columns], key.at[:, columns], in_sems.at[0, chunk]),
            pltpu.make_async_copy(
                value_ref.at[:, columns], value.at[:, columns], in_sems.at[1, chunk]
            ),
            pltpu.make_async_copy(
                filter_ref.at[pl.ds(start, share), columns],
                filters.at[:, columns],
                in_sems.at[2, chunk],
            ),
        ]

    def departure(chunk):
        owners = pl.ds(chunk * near, near)
        return pltpu.make_async_copy(packed.at[owners], out_ref.at[owners], out_sems.at[chunk])

    for copy in whole:
        copy.start()
    for chunk in range(chunks):
        for copy in arrivals(chunk):
            copy.start(priority=1)
    for copy in whole:
        copy.wait()
    row = lax.broadcasted_iota(jnp.int32, (SUBLANES, LANES), 0)

    @pl.loop(0, chunks)
    def _(chunk):
        for copy in arrivals(chunk):
            copy.wait()
        for part in range(near):
            span_here = pl.ds(pl.multiple_of(chunk * span + part * LANES, LANES), LANES)
            owner = chunk * near + part
            key_here = key[:, span_here].astype(jnp.float32)
            value_here = value[:, span_here].astype(jnp.float32)
            k_short = featurize_inside(key_here, taps[1, :, span_here])
            v_short = featurize_inside(value_here, taps[2, :, span_here])
            packed[owner, :rows] = (k_short * v_short).astype(packed.dtype)
            packed[owner, rows : rows + share] = filters[:, span_here]
            query_last = pltpu.roll(query[:, span_here].astype(jnp.float32), 4, 0)
            key_tile = jnp.where(
                row < 2,
                pltpu.roll(key_here[rows - SUBLANES :], 2, 0),
                pltpu.roll(key_here[:SUBLANES], 2, 0),
            )
            value_tile = jnp.where(
                row < 6,
                pltpu.roll(value_here[rows - SUBLANES :], 6, 0),
                pltpu.roll(value_here[:SUBLANES], 6, 0),
            )
            edge = jnp.where(row < 4, key_tile, value_tile)
            packed[owner, rows + share :] = edge.astype(packed.dtype)
            edge = jnp.where((row == 2) | (row == 3), query_last, edge)
            edges[:, span_here] = edge.astype(edges.dtype)
        departure(chunk).start()

    last = pltpu.make_async_copy(edges, edges_ref, one_sems.at[0])
    last.start()
    for chunk in range(chunks):
        departure(chunk).wait()
    last.wait()


def pack(query_in, key_in, value_in, long_filter, short_weight, group, owners, parts):
    rows, channels = key_in.shape
    chunks = max(1, channels // 1024)
    taps = short_weight.shape[1]
    share = rows // parts
    height = rows + share + SUBLANES
    here = pl.BlockSpec(memory_space=pltpu.HBM)
    return pl.pallas_call(
        pack_kernel,
        out_shape=(
            jax.ShapeDtypeStruct((owners, height, LANES), jnp.bfloat16),
            jax.ShapeDtypeStruct((SUBLANES, channels), jnp.bfloat16),
        ),
        in_specs=[pl.BlockSpec(memory_space=pltpu.SMEM)] + [here] * 5,
        out_specs=(here, here),
        scratch_shapes=[
            pltpu.VMEM((SUBLANES, channels), jnp.bfloat16),
            pltpu.VMEM((rows, channels), jnp.bfloat16),
            pltpu.VMEM((rows, channels), jnp.bfloat16),
            pltpu.VMEM((share, channels), jnp.bfloat16),
            pltpu.VMEM((3, taps, channels), jnp.float32),
            pltpu.VMEM((owners, height, LANES), jnp.bfloat16),
            pltpu.VMEM((SUBLANES, channels), jnp.bfloat16),
            pltpu.SemaphoreType.DMA((3, chunks)),
            pltpu.SemaphoreType.DMA((2,)),
            pltpu.SemaphoreType.DMA((chunks,)),
        ],
        cost_estimate=pl.CostEstimate(
            flops=12 * rows * channels, bytes_accessed=8 * rows * channels, transcendentals=0
        ),
    )(group.reshape(1), query_in, key_in, value_in, long_filter, short_weight)


def transform(table, values):
    both = jnp.dot(table, values, preferred_element_type=jnp.float32)
    half = table.shape[0] // 2
    return both[:half] + both[half:]


def over(count, body):
    if count <= UNROLLED:
        for step in range(count):
            body(step)
    else:

        @pl.loop(0, count)
        def _(step):
            body(step)


def filter_kernel(table_ref, filter_ref, out_ref):
    count, double, _ = out_ref.shape
    block = double // 2

    def body(step):
        start = step * block
        if not isinstance(step, int):
            start = pl.multiple_of(start, block)
        out_ref[step] = transform(table_ref[...], filter_ref[pl.ds(start, block), :])

    over(count, body)


def filter_spectra(long_filter, table):
    length, width = long_filter.shape
    block = table.shape[1]
    return pl.pallas_call(
        filter_kernel,
        out_shape=jax.ShapeDtypeStruct((length // block, 2 * block, width), jnp.float32),
        in_specs=[pl.BlockSpec(memory_space=pltpu.VMEM)] * 2,
        out_specs=pl.BlockSpec(memory_space=pltpu.VMEM),
        compiler_params=pltpu.CompilerParams(vmem_limit_bytes=40 * MIB),
        cost_estimate=pl.CostEstimate(
            flops=8 * length * block * width, bytes_accessed=10 * length * width, transcendentals=0
        ),
    )(table, long_filter)


def inverse(table_ref, values, block):
    high = values.astype(jnp.bfloat16)
    low = (values - high.astype(jnp.float32)).astype(jnp.bfloat16)
    return transform(table_ref[...], high) + jnp.dot(
        table_ref[:block], low, preferred_element_type=jnp.float32
    )


def conv_kernel(forward_ref, inverse_ref, product_ref, filter_ref, out_ref, data, mixed, last):
    count, double, width = filter_ref.shape
    block = double // 2
    lane_step = min(width, LANES)

    def piece(step):
        start = step * block
        return pl.ds(start if isinstance(step, int) else pl.multiple_of(start, block), block)

    def forward(step):
        data[step] = transform(forward_ref[...], product_ref[piece(step), :])

    over(count, forward)
    last[...] = jnp.zeros_like(last)

    @pl.loop(0, count)
    def _(total):
        for sign, base in ((1.0, 0), (-1.0, block // 2)):
            for column in range(0, width, lane_step):
                lanes = slice(column, column + lane_step)

                @pl.loop(0, block // 2 // SUBLANES)
                def _(index):
                    start = pl.multiple_of(base + index * SUBLANES, SUBLANES)
                    real = pl.ds(start, SUBLANES)
                    imag = pl.ds(pl.multiple_of(block + start, SUBLANES), SUBLANES)

                    def add(step, sums):
                        a, b = data[step, real, lanes], data[step, imag, lanes]
                        c = filter_ref[total - step, real, lanes]
                        d = filter_ref[total - step, imag, lanes]
                        return sums[0] + (a * c - b * d), sums[1] + (a * d + b * c)

                    zero = jnp.zeros((SUBLANES, lane_step), jnp.float32)
                    sum_real, sum_imag = lax.fori_loop(0, total + 1, add, (zero, zero))
                    mixed[real, lanes] = sum_real - sign * last[imag, lanes]
                    mixed[imag, lanes] = sum_imag + sign * last[real, lanes]
                    last[real, lanes] = sum_real
                    last[imag, lanes] = sum_imag

        out_ref[piece(total), :] = inverse(inverse_ref, mixed[...], block).astype(out_ref.dtype)


def convolve(product, spectra, forward_table, inverse_table):
    length, width = product.shape
    count, double, _ = spectra.shape
    return pl.pallas_call(
        conv_kernel,
        out_shape=jax.ShapeDtypeStruct((length, width), jnp.bfloat16),
        in_specs=[pl.BlockSpec(memory_space=pltpu.VMEM)] * 4,
        out_specs=pl.BlockSpec(memory_space=pltpu.VMEM),
        scratch_shapes=[
            pltpu.VMEM((count, double, width), jnp.float32),
            pltpu.VMEM((double, width), jnp.float32),
            pltpu.VMEM((double, width), jnp.float32),
        ],
        compiler_params=pltpu.CompilerParams(vmem_limit_bytes=56 * MIB),
        cost_estimate=pl.CostEstimate(
            flops=16 * length * double * width,
            bytes_accessed=12 * length * width,
            transcendentals=0,
        ),
    )(forward_table, inverse_table, product, spectra)


def whole_kernel(
    owner_ref, forward_ref, inverse_ref, taps_ref, arrived, ready,
    product, filters, data, known, mixed, partly,
):
    del owner_ref
    senders, rows, _ = ready.shape
    places = senders // 2
    share = rows // 2
    _, count, block, _ = data.shape
    half = block // 2
    near = block // rows
    tiles = half // SUBLANES // count
    row = lax.broadcasted_iota(jnp.int32, (SUBLANES, LANES), 0)
    weights = tap_tiles(taps_ref, slice(None))

    def forward(side, values):
        return transform(forward_ref[side], values)

    def backward(side, step):
        return inverse(inverse_ref.at[side], mixed[side, step], block)

    def multiply(side, tile):
        start = tile * SUBLANES
        real = slice(start, start + SUBLANES)
        imag = slice(half + start, half + start + SUBLANES)
        filter_parts = []
        for step in range(count):
            c, d = known[side, step, real], known[side, step, imag]
            filter_parts.append((c, d - c, c + d))
        for part in range(2):
            lanes = slice(part * LANES, (part + 1) * LANES)
            data_parts = []
            for step in range(count):
                a, b = data[side, step, real, lanes], data[side, step, imag, lanes]
                data_parts.append((a + b, a, b))
            before = None
            for total in range(count):
                sums = None
                for step in range(total + 1):
                    pairs = zip(data_parts[step], filter_parts[total - step])
                    terms = [x * y for x, y in pairs]
                    sums = terms if sums is None else [x + y for x, y in zip(sums, terms)]
                both = (sums[0] - sums[2], sums[0] + sums[1])
                if before is None:
                    out = both
                elif side == 0:
                    out = (both[0] - before[1], both[1] + before[0])
                else:
                    out = (both[0] + before[1], both[1] - before[0])
                mixed[side, total, real, lanes] = out[0]
                mixed[side, total, imag, lanes] = out[1]
                before = both

    behind = [jnp.zeros((SUBLANES, LANES), jnp.float32)] * 2
    for step in range(count):
        for part in range(2):
            lanes = slice(part * LANES, (part + 1) * LANES)
            for offset in range(near):
                sender = part * places + step * near + offset
                edge = arrived[sender, rows + share :].astype(jnp.float32)
                first = first_products(edge, behind[part], weights)
                behind[part] = edge
                values = arrived[sender, : 2 * SUBLANES].astype(jnp.float32)
                top = jnp.where(row < 2, first, values[:SUBLANES])
                values = jnp.concatenate([top, values[SUBLANES:]], axis=0)
                start = offset * rows
                product[step, start : start + 2 * SUBLANES, lanes] = values.astype(product.dtype)
                product[step, start + 2 * SUBLANES : start + rows, lanes] = arrived[
                    sender, 2 * SUBLANES : rows
                ]
                start = offset * rows + part * share
                place = (step % 2) * LANES
                filters[step // 2, start : start + share, place : place + LANES] = arrived[
                    sender, rows : rows + share
                ]
        data[0, step] = forward(0, product[step])
        if step % 2:
            for side in range(2):
                both = forward(side, filters[step // 2])
                known[side, step - 1] = both[:, :LANES]
                known[side, step] = both[:, LANES:]

    for step in range(count):
        for tile in range(tiles):
            multiply(0, step * tiles + tile)
        data[1, step] = forward(1, product[step])

    for step in range(count):
        for tile in range(tiles):
            multiply(1, step * tiles + tile)
        partly[step] = backward(0, step)

    for step in range(count):
        result = (partly[step] + backward(1, step)).astype(ready.dtype)
        for part in range(2):
            for offset in range(near):
                ready[part * places + step * near + offset] = result[
                    offset * rows : (offset + 1) * rows, part * LANES : (part + 1) * LANES
                ]


def convolve_whole(sent, short_weight, owner, rows, forward_table, inverse_table):
    senders, height, _ = sent.shape
    block = forward_table.shape[2]
    length = senders // 2 * rows
    count = length // block
    taps = short_weight.shape[1]
    return pl.pallas_call(
        whole_kernel,
        out_shape=jax.ShapeDtypeStruct((senders, rows, LANES), jnp.bfloat16),
        grid_spec=pltpu.PrefetchScalarGridSpec(
            num_scalar_prefetch=1,
            grid=(1,),
            in_specs=[
                pl.BlockSpec(memory_space=pltpu.VMEM),
                pl.BlockSpec(memory_space=pltpu.VMEM),
                pl.BlockSpec((3, taps, LANES), lambda i, owner: (0, 0, owner[0])),
                pl.BlockSpec(memory_space=pltpu.VMEM),
            ],
            out_specs=pl.BlockSpec(memory_space=pltpu.VMEM),
            scratch_shapes=[
                pltpu.VMEM((count, block, 2 * LANES), jnp.bfloat16),
                pltpu.VMEM((count // 2, block, 2 * LANES), jnp.bfloat16),
                pltpu.VMEM((2, count, block, 2 * LANES), jnp.float32),
                pltpu.VMEM((2, count, block, LANES), jnp.float32),
                pltpu.VMEM((2, count, block, 2 * LANES), jnp.float32),
                pltpu.VMEM((count, block, 2 * LANES), jnp.float32),
            ],
        ),
        compiler_params=pltpu.CompilerParams(vmem_limit_bytes=32 * MIB),
        cost_estimate=pl.CostEstimate(
            flops=40 * length * block * LANES,
            bytes_accessed=2 * senders * (height + rows) * LANES,
            transcendentals=0,
        ),
    )(owner.reshape(1), forward_table, inverse_table, short_weight, sent)


def exchange(value, axes):
    return lax.all_to_all(value, axes, split_axis=0, concat_axis=0, tiled=True)


def on_device(query_in, key_in, value_in, long_filter, short_weight, skip_gain):
    places = lax.axis_size("seq")
    parts = lax.axis_size("groups")
    group = lax.axis_index("groups").astype(jnp.int32)
    place = lax.axis_index("seq").astype(jnp.int32)
    rows, channels = key_in.shape
    length = places * rows
    block = BLOCK if length % BLOCK == 0 else rows
    rim = short_weight.shape[1] - 1
    owners = parts * places
    count = length // block
    aligned = (
        parts == 2
        and rim == 2
        and channels == owners * LANES
        and rows % 32 == 0
        and block % rows == 0
        and block == BLOCK
        and count in (2, 4, 8)
    )
    forward_table, inverse_table = half_tables(block) if aligned else transform_tables(block)
    forward_table = jnp.asarray(forward_table)
    inverse_table = jnp.asarray(inverse_table)
    if aligned:
        sent, edges = pack(
            query_in, key_in, value_in, long_filter, short_weight, group, owners, parts
        )
        received = exchange(sent, ("groups", "seq"))
        edges = from_behind(edges, "seq")
        prepared = prepare(sent, query_in, short_weight, skip_gain)
        received, edges, prepared = lax.optimization_barrier((received, edges, prepared))
        owner = group * places + place
        convolved = convolve_whole(
            received, short_weight, owner, rows, forward_table, inverse_table
        )
        convolved = exchange(convolved, ("groups", "seq"))
        return finish(
            convolved, prepared, sent, query_in, edges, short_weight, skip_gain
        )
    else:
        width = channels // places
        edges = jnp.stack([query_in[-rim:], key_in[-rim:], value_in[-rim:]])
        sent = long_filter.reshape(rows, places, width).transpose(1, 0, 2)
        spectra = filter_spectra(exchange(sent, "seq").reshape(length, width), forward_table)
        edges = from_behind(edges, "seq")
        product = products(key_in, value_in, edges, short_weight)
        sent = product.reshape(rows, places, width).transpose(1, 0, 2)
        received = exchange(sent, "seq").reshape(length, width)
        convolved = convolve(received, spectra, forward_table, inverse_table)
        convolved = exchange(convolved.reshape(places, rows, width), "seq")
        convolved = convolved.transpose(1, 0, 2).reshape(rows, channels // LANES, LANES)
        convolved = convolved.transpose(1, 0, 2)
        return gate(convolved, product, query_in, edges, short_weight, skip_gain)


def solution(mesh):
    placed = (
        P(("groups", "seq"), None),
        P(("groups", "seq"), None),
        P(("groups", "seq"), None),
        P("seq", None),
        P(),
        P(),
    )
    return jax.shard_map(
        on_device, mesh=mesh, in_specs=placed, out_specs=P(("groups", "seq"), None), check_vma=False
    )
```

```python
import functools

import jax
import jax.numpy as jnp
import ml_dtypes
import numpy as np
from jax import lax
from jax.experimental import pallas as pl
from jax.experimental.pallas import tpu as pltpu
from jax.sharding import PartitionSpec as P

LANES = 128
SUBLANES = 8
BLOCK = 256
UNROLLED = 8
MIB = 1 << 20


def from_behind(value, axis):
    count = lax.axis_size(axis)
    return lax.ppermute(value, axis, [(source, source + 1) for source in range(count - 1)])


def transform_tables(block):
    numbers = np.concatenate([np.arange(0, block, 2), np.arange(1, block, 2)])
    quarter = (2 * numbers[:, None] + 1) * np.arange(block)[None, :] % (4 * block)
    angle = quarter.astype(np.float64) * (2.0 * np.pi / (4 * block))
    table = np.concatenate([np.cos(angle), -np.sin(angle)], axis=0)

    def split(values):
        high = values.astype(ml_dtypes.bfloat16)
        low = (values - high.astype(np.float64)).astype(ml_dtypes.bfloat16)
        return np.concatenate([high, low], axis=0)

    return split(table), split(table.T / block)


def half_tables(block):
    forward, inverse = transform_tables(block)
    half = block // 2
    rows = np.arange(2 * block).reshape(2, 2, half).transpose(1, 0, 2).reshape(2, block)
    forward = forward.reshape(2, 2 * block, block)
    forward = np.stack([forward[:, rows[side]].reshape(2 * block, block) for side in range(2)])
    inverse = np.stack([inverse[:, rows[side]] for side in range(2)])
    return forward, inverse


def shifted(values, edge, steps):
    rolled = pltpu.roll(values, steps, 0)
    row = lax.broadcasted_iota(jnp.int32, values.shape, 0)
    for place in range(steps):
        source = edge[edge.shape[0] - steps + place : edge.shape[0] - steps + place + 1]
        rolled = jnp.where(row == place, jnp.broadcast_to(source, values.shape), rolled)
    return rolled


def featurize_inside(own, taps):
    result = taps[0:1] * own
    for offset in range(1, taps.shape[0]):
        result = result + taps[offset : offset + 1] * pltpu.roll(own, offset, 0)
    return result


def featurize(own, edge, taps):
    own = own.astype(jnp.float32)
    edge = edge.astype(jnp.float32)
    top = own[:SUBLANES]
    first = taps[0:1] * top
    for offset in range(1, taps.shape[0]):
        first = first + taps[offset : offset + 1] * shifted(top, edge, offset)
    return jnp.concatenate([first, featurize_inside(own, taps)[SUBLANES:]], axis=0)


def product_kernel(key_ref, value_ref, edge_ref, taps_ref, out_ref):
    for start in range(0, key_ref.shape[1], LANES):
        span = slice(start, start + LANES)
        k_short = featurize(key_ref[:, span], edge_ref[1, :, span], taps_ref[1, :, span])
        v_short = featurize(value_ref[:, span], edge_ref[2, :, span], taps_ref[2, :, span])
        out_ref[:, span] = (k_short * v_short).astype(out_ref.dtype)


def products(key_in, value_in, edges, short_weight):
    rows, channels = key_in.shape
    span = min(channels, 1024)
    taps = short_weight.shape[1]
    return pl.pallas_call(
        product_kernel,
        out_shape=jax.ShapeDtypeStruct((rows, channels), jnp.bfloat16),
        grid=(channels // span,),
        in_specs=[
            pl.BlockSpec((rows, span), lambda i: (0, i)),
            pl.BlockSpec((rows, span), lambda i: (0, i)),
            pl.BlockSpec((3, taps - 1, span), lambda i: (0, 0, i)),
            pl.BlockSpec((3, taps, span), lambda i: (0, 0, i)),
        ],
        out_specs=pl.BlockSpec((rows, span), lambda i: (0, i)),
        cost_estimate=pl.CostEstimate(
            flops=12 * rows * channels, bytes_accessed=6 * rows * channels, transcendentals=0
        ),
    )(key_in, value_in, edges, short_weight)


def gate_kernel(conv_ref, product_ref, query_ref, edge_ref, taps_ref, gain_ref, out_ref):
    for part in range(conv_ref.shape[0]):
        span = slice(part * LANES, (part + 1) * LANES)
        q_short = featurize(query_ref[:, span], edge_ref[0, :, span], taps_ref[0, :, span])
        mixed = conv_ref[part].astype(jnp.float32) + gain_ref[:, span] * product_ref[
            :, span
        ].astype(jnp.float32)
        out_ref[:, span] = (q_short * mixed).astype(out_ref.dtype)


def gate(convolved, product, query_in, edges, short_weight, skip_gain):
    rows, channels = query_in.shape
    span = min(channels, 1024)
    taps = short_weight.shape[1]
    across = pl.BlockSpec((rows, span), lambda i: (0, i))
    return pl.pallas_call(
        gate_kernel,
        out_shape=jax.ShapeDtypeStruct((rows, channels), jnp.bfloat16),
        grid=(channels // span,),
        in_specs=[
            pl.BlockSpec((span // LANES, rows, LANES), lambda i: (i, 0, 0)),
            across,
            across,
            pl.BlockSpec((3, taps - 1, span), lambda i: (0, 0, i)),
            pl.BlockSpec((3, taps, span), lambda i: (0, 0, i)),
            pl.BlockSpec((1, span), lambda i: (0, i)),
        ],
        out_specs=across,
        cost_estimate=pl.CostEstimate(
            flops=9 * rows * channels, bytes_accessed=8 * rows * channels, transcendentals=0
        ),
    )(convolved, product, query_in, edges, short_weight, skip_gain.reshape(1, channels))


def prepare_kernel(sent_ref, query_ref, taps_ref, gain_ref, short_ref, direct_ref):
    owners, rows, _ = short_ref.shape
    for owner in range(owners):
        lanes = slice(owner * LANES, (owner + 1) * LANES)
        q_short = featurize_inside(query_ref[:, lanes].astype(jnp.float32), taps_ref[0, :, lanes])
        product = sent_ref[owner, :rows].astype(jnp.float32)
        short_ref[owner] = q_short
        direct_ref[owner] = q_short * (gain_ref[:, lanes] * product)


def prepare(sent, query_in, short_weight, skip_gain):
    rows, channels = query_in.shape
    owners, height, _ = sent.shape
    near = min(owners, 8)
    span = near * LANES
    taps = short_weight.shape[1]
    out = pl.BlockSpec((near, rows, LANES), lambda i: (i, 0, 0))
    return pl.pallas_call(
        prepare_kernel,
        out_shape=(jax.ShapeDtypeStruct((owners, rows, LANES), jnp.float32),) * 2,
        grid=(owners // near,),
        in_specs=[
            pl.BlockSpec((near, height, LANES), lambda i: (i, 0, 0)),
            pl.BlockSpec((rows, span), lambda i: (0, i)),
            pl.BlockSpec((3, taps, span), lambda i: (0, 0, i)),
            pl.BlockSpec((1, span), lambda i: (0, i)),
        ],
        out_specs=(out, out),
        cost_estimate=pl.CostEstimate(
            flops=8 * rows * channels, bytes_accessed=12 * rows * channels, transcendentals=0
        ),
    )(sent, query_in, short_weight, skip_gain.reshape(1, channels))


def finish_kernel(
    conv_ref, short_ref, direct_ref, sent_ref, query_ref, edge_ref, taps_ref, gain_ref, out_ref,
    ready, sems,
):
    rows, channels = ready.shape
    tail = sent_ref.shape[1] - SUBLANES
    chunks = sems.shape[0]
    span = channels // chunks
    near = span // LANES
    row = lax.broadcasted_iota(jnp.int32, (SUBLANES, LANES), 0)

    def departure(chunk):
        columns = pl.ds(pl.multiple_of(chunk * span, span), span)
        return pltpu.make_async_copy(ready.at[:, columns], out_ref.at[:, columns], sems.at[chunk])

    @pl.loop(0, chunks)
    def _(chunk):
        for part in range(near):
            owner = chunk * near + part
            lanes = pl.ds(pl.multiple_of(owner * LANES, LANES), LANES)
            behind = edge_ref[:, lanes].astype(jnp.float32)
            own = sent_ref[owner, tail:].astype(jnp.float32)
            first = first_products(own, behind, tap_tiles(taps_ref, lanes))
            first = first.astype(jnp.bfloat16).astype(jnp.float32)
            product = sent_ref[owner, :SUBLANES].astype(jnp.float32)
            product = jnp.where(row < 2, first, product)

            weights = taps_ref[0, :, lanes]
            top = query_ref[:SUBLANES, lanes].astype(jnp.float32)
            one = jnp.where(row < 1, pltpu.roll(behind, 5, 0), pltpu.roll(top, 1, 0))
            two = jnp.where(row < 2, pltpu.roll(behind, 6, 0), pltpu.roll(top, 2, 0))
            top = weights[0:1] * top + weights[1:2] * one + weights[2:3] * two

            convolved = conv_ref[owner].astype(jnp.float32)
            top = top * convolved[:SUBLANES] + top * (gain_ref[:, lanes] * product)
            result = short_ref[owner] * convolved + direct_ref[owner]
            result = jnp.concatenate([top, result[SUBLANES:]], axis=0)
            ready[:, lanes] = result.astype(ready.dtype)
        departure(chunk).start()

    for chunk in range(chunks):
        departure(chunk).wait()


def finish(convolved, prepared, sent, query_in, edges, short_weight, skip_gain):
    rows, channels = query_in.shape
    chunks = max(1, channels // 512)
    here = pl.BlockSpec(memory_space=pltpu.VMEM)
    return pl.pallas_call(
        finish_kernel,
        out_shape=jax.ShapeDtypeStruct((rows, channels), jnp.bfloat16),
        in_specs=[here] * 8,
        out_specs=pl.BlockSpec(memory_space=pltpu.HBM),
        scratch_shapes=[
            pltpu.VMEM((rows, channels), jnp.bfloat16),
            pltpu.SemaphoreType.DMA((chunks,)),
        ],
        compiler_params=pltpu.CompilerParams(vmem_limit_bytes=8 * MIB),
        cost_estimate=pl.CostEstimate(
            flops=3 * rows * channels, bytes_accessed=12 * rows * channels, transcendentals=0
        ),
    )(
        convolved, *prepared, sent, query_in, edges, short_weight, skip_gain.reshape(1, channels)
    )


def tap_tiles(taps_ref, lanes):
    row = lax.broadcasted_iota(jnp.int32, (SUBLANES, LANES), 0)
    return [
        jnp.where(row < 4, taps_ref[1, tap : tap + 1, lanes], taps_ref[2, tap : tap + 1, lanes])
        for tap in range(taps_ref.shape[1])
    ]


def first_products(tile, behind, weights):
    row = lax.broadcasted_iota(jnp.int32, (SUBLANES, LANES), 0)
    joined = jnp.where(row % 4 >= 2, tile, behind)
    short = weights[0] * joined
    for tap in range(1, len(weights)):
        short = short + weights[tap] * pltpu.roll(joined, tap, 0)
    return pltpu.roll(short * pltpu.roll(short, 4, 0), 6, 0)


def pack_kernel(
    group_ref, query_ref, key_ref, value_ref, filter_ref, taps_ref, out_ref, edges_ref,
    query, key, value, filters, taps, packed, edges, in_sems, one_sems, out_sems,
):
    rows, channels = key.shape
    share = filters.shape[0]
    chunks = out_sems.shape[0]
    span = channels // chunks
    near = span // LANES
    start = pl.multiple_of(group_ref[0] * share, share)
    whole = [
        pltpu.make_async_copy(taps_ref, taps, one_sems.at[0]),
        pltpu.make_async_copy(query_ref.at[pl.ds(rows - SUBLANES, SUBLANES)], query, one_sems.at[1]),
    ]

    def arrivals(chunk):
        columns = pl.ds(pl.multiple_of(chunk * span, span), span)
        return [
            pltpu.make_async_copy(key_ref.at[:, columns], key.at[:, columns], in_sems.at[0, chunk]),
            pltpu.make_async_copy(
                value_ref.at[:, columns], value.at[:, columns], in_sems.at[1, chunk]
            ),
            pltpu.make_async_copy(
                filter_ref.at[pl.ds(start, share), columns],
                filters.at[:, columns],
                in_sems.at[2, chunk],
            ),
        ]

    def departure(chunk):
        owners = pl.ds(chunk * near, near)
        return pltpu.make_async_copy(packed.at[owners], out_ref.at[owners], out_sems.at[chunk])

    for copy in whole:
        copy.start()
    for chunk in range(chunks):
        for copy in arrivals(chunk):
            copy.start(priority=1)
    for copy in whole:
        copy.wait()
    row = lax.broadcasted_iota(jnp.int32, (SUBLANES, LANES), 0)

    @pl.loop(0, chunks)
    def _(chunk):
        for copy in arrivals(chunk):
            copy.wait()
        for part in range(near):
            span_here = pl.ds(pl.multiple_of(chunk * span + part * LANES, LANES), LANES)
            owner = chunk * near + part
            key_here = key[:, span_here].astype(jnp.float32)
            value_here = value[:, span_here].astype(jnp.float32)
            k_short = featurize_inside(key_here, taps[1, :, span_here])
            v_short = featurize_inside(value_here, taps[2, :, span_here])
            packed[owner, :rows] = (k_short * v_short).astype(packed.dtype)
            packed[owner, rows : rows + share] = filters[:, span_here]
            query_last = pltpu.roll(query[:, span_here].astype(jnp.float32), 4, 0)
            key_tile = jnp.where(
                row < 2,
                pltpu.roll(key_here[rows - SUBLANES :], 2, 0),
                pltpu.roll(key_here[:SUBLANES], 2, 0),
            )
            value_tile = jnp.where(
                row < 6,
                pltpu.roll(value_here[rows - SUBLANES :], 6, 0),
                pltpu.roll(value_here[:SUBLANES], 6, 0),
            )
            edge = jnp.where(row < 4, key_tile, value_tile)
            packed[owner, rows + share :] = edge.astype(packed.dtype)
            edge = jnp.where((row == 2) | (row == 3), query_last, edge)
            edges[:, span_here] = edge.astype(edges.dtype)
        departure(chunk).start()

    last = pltpu.make_async_copy(edges, edges_ref, one_sems.at[0])
    last.start()
    for chunk in range(chunks):
        departure(chunk).wait()
    last.wait()


def pack(query_in, key_in, value_in, long_filter, short_weight, group, owners, parts):
    rows, channels = key_in.shape
    chunks = max(1, channels // 1024)
    taps = short_weight.shape[1]
    share = rows // parts
    height = rows + share + SUBLANES
    here = pl.BlockSpec(memory_space=pltpu.HBM)
    return pl.pallas_call(
        pack_kernel,
        out_shape=(
            jax.ShapeDtypeStruct((owners, height, LANES), jnp.bfloat16),
            jax.ShapeDtypeStruct((SUBLANES, channels), jnp.bfloat16),
        ),
        in_specs=[pl.BlockSpec(memory_space=pltpu.SMEM)] + [here] * 5,
        out_specs=(here, here),
        scratch_shapes=[
            pltpu.VMEM((SUBLANES, channels), jnp.bfloat16),
            pltpu.VMEM((rows, channels), jnp.bfloat16),
            pltpu.VMEM((rows, channels), jnp.bfloat16),
            pltpu.VMEM((share, channels), jnp.bfloat16),
            pltpu.VMEM((3, taps, channels), jnp.float32),
            pltpu.VMEM((owners, height, LANES), jnp.bfloat16),
            pltpu.VMEM((SUBLANES, channels), jnp.bfloat16),
            pltpu.SemaphoreType.DMA((3, chunks)),
            pltpu.SemaphoreType.DMA((2,)),
            pltpu.SemaphoreType.DMA((chunks,)),
        ],
        cost_estimate=pl.CostEstimate(
            flops=12 * rows * channels, bytes_accessed=8 * rows * channels, transcendentals=0
        ),
    )(group.reshape(1), query_in, key_in, value_in, long_filter, short_weight)


def transform(table, values):
    both = jnp.dot(table, values, preferred_element_type=jnp.float32)
    half = table.shape[0] // 2
    return both[:half] + both[half:]


def over(count, body):
    if count <= UNROLLED:
        for step in range(count):
            body(step)
    else:

        @pl.loop(0, count)
        def _(step):
            body(step)


def filter_kernel(table_ref, filter_ref, out_ref):
    count, double, _ = out_ref.shape
    block = double // 2

    def body(step):
        start = step * block
        if not isinstance(step, int):
            start = pl.multiple_of(start, block)
        out_ref[step] = transform(table_ref[...], filter_ref[pl.ds(start, block), :])

    over(count, body)


def filter_spectra(long_filter, table):
    length, width = long_filter.shape
    block = table.shape[1]
    return pl.pallas_call(
        filter_kernel,
        out_shape=jax.ShapeDtypeStruct((length // block, 2 * block, width), jnp.float32),
        in_specs=[pl.BlockSpec(memory_space=pltpu.VMEM)] * 2,
        out_specs=pl.BlockSpec(memory_space=pltpu.VMEM),
        compiler_params=pltpu.CompilerParams(vmem_limit_bytes=40 * MIB),
        cost_estimate=pl.CostEstimate(
            flops=8 * length * block * width, bytes_accessed=10 * length * width, transcendentals=0
        ),
    )(table, long_filter)


def inverse(table_ref, values, block):
    high = values.astype(jnp.bfloat16)
    low = (values - high.astype(jnp.float32)).astype(jnp.bfloat16)
    return transform(table_ref[...], high) + jnp.dot(
        table_ref[:block], low, preferred_element_type=jnp.float32
    )


def conv_kernel(forward_ref, inverse_ref, product_ref, filter_ref, out_ref, data, mixed, last):
    count, double, width = filter_ref.shape
    block = double // 2
    lane_step = min(width, LANES)

    def piece(step):
        start = step * block
        return pl.ds(start if isinstance(step, int) else pl.multiple_of(start, block), block)

    def forward(step):
        data[step] = transform(forward_ref[...], product_ref[piece(step), :])

    over(count, forward)
    last[...] = jnp.zeros_like(last)

    @pl.loop(0, count)
    def _(total):
        for sign, base in ((1.0, 0), (-1.0, block // 2)):
            for column in range(0, width, lane_step):
                lanes = slice(column, column + lane_step)

                @pl.loop(0, block // 2 // SUBLANES)
                def _(index):
                    start = pl.multiple_of(base + index * SUBLANES, SUBLANES)
                    real = pl.ds(start, SUBLANES)
                    imag = pl.ds(pl.multiple_of(block + start, SUBLANES), SUBLANES)

                    def add(step, sums):
                        a, b = data[step, real, lanes], data[step, imag, lanes]
                        c = filter_ref[total - step, real, lanes]
                        d = filter_ref[total - step, imag, lanes]
                        return sums[0] + (a * c - b * d), sums[1] + (a * d + b * c)

                    zero = jnp.zeros((SUBLANES, lane_step), jnp.float32)
                    sum_real, sum_imag = lax.fori_loop(0, total + 1, add, (zero, zero))
                    mixed[real, lanes] = sum_real - sign * last[imag, lanes]
                    mixed[imag, lanes] = sum_imag + sign * last[real, lanes]
                    last[real, lanes] = sum_real
                    last[imag, lanes] = sum_imag

        out_ref[piece(total), :] = inverse(inverse_ref, mixed[...], block).astype(out_ref.dtype)


def convolve(product, spectra, forward_table, inverse_table):
    length, width = product.shape
    count, double, _ = spectra.shape
    return pl.pallas_call(
        conv_kernel,
        out_shape=jax.ShapeDtypeStruct((length, width), jnp.bfloat16),
        in_specs=[pl.BlockSpec(memory_space=pltpu.VMEM)] * 4,
        out_specs=pl.BlockSpec(memory_space=pltpu.VMEM),
        scratch_shapes=[
            pltpu.VMEM((count, double, width), jnp.float32),
            pltpu.VMEM((double, width), jnp.float32),
            pltpu.VMEM((double, width), jnp.float32),
        ],
        compiler_params=pltpu.CompilerParams(vmem_limit_bytes=56 * MIB),
        cost_estimate=pl.CostEstimate(
            flops=16 * length * double * width,
            bytes_accessed=12 * length * width,
            transcendentals=0,
        ),
    )(forward_table, inverse_table, product, spectra)


def whole_kernel(
    owner_ref, forward_ref, inverse_ref, taps_ref, arrived, ready,
    product, filters, data, known, mixed, partly,
):
    senders, rows, _ = ready.shape
    places = senders // 2
    share = rows // 2
    _, count, block, _ = data.shape
    half = block // 2
    near = block // rows
    tiles = half // SUBLANES // count
    row = lax.broadcasted_iota(jnp.int32, (SUBLANES, LANES), 0)
    own = pl.multiple_of(owner_ref[0] * LANES, LANES)
    weights = tap_tiles(taps_ref, pl.ds(own, LANES))

    def forward(side, values):
        return transform(forward_ref[side], values)

    def backward(side, step):
        return inverse(inverse_ref.at[side], mixed[side, step], block)

    def multiply(side, tile):
        start = tile * SUBLANES
        real = slice(start, start + SUBLANES)
        imag = slice(half + start, half + start + SUBLANES)
        filter_parts = []
        for step in range(count):
            c, d = known[side, step, real], known[side, step, imag]
            filter_parts.append((c, d - c, c + d))
        for part in range(2):
            lanes = slice(part * LANES, (part + 1) * LANES)
            data_parts = []
            for step in range(count):
                a, b = data[side, step, real, lanes], data[side, step, imag, lanes]
                data_parts.append((a + b, a, b))
            before = None
            for total in range(count):
                sums = None
                for step in range(total + 1):
                    pairs = zip(data_parts[step], filter_parts[total - step])
                    terms = [x * y for x, y in pairs]
                    sums = terms if sums is None else [x + y for x, y in zip(sums, terms)]
                both = (sums[0] - sums[2], sums[0] + sums[1])
                if before is None:
                    out = both
                elif side == 0:
                    out = (both[0] - before[1], both[1] + before[0])
                else:
                    out = (both[0] + before[1], both[1] - before[0])
                mixed[side, total, real, lanes] = out[0]
                mixed[side, total, imag, lanes] = out[1]
                before = both

    behind = [jnp.zeros((SUBLANES, LANES), jnp.float32)] * 2
    for step in range(count):
        for part in range(2):
            lanes = slice(part * LANES, (part + 1) * LANES)
            for offset in range(near):
                sender = part * places + step * near + offset
                edge = arrived[sender, rows + share :].astype(jnp.float32)
                first = first_products(edge, behind[part], weights)
                behind[part] = edge
                values = arrived[sender, : 2 * SUBLANES].astype(jnp.float32)
                top = jnp.where(row < 2, first, values[:SUBLANES])
                values = jnp.concatenate([top, values[SUBLANES:]], axis=0)
                start = offset * rows
                product[step, start : start + 2 * SUBLANES, lanes] = values.astype(product.dtype)
                product[step, start + 2 * SUBLANES : start + rows, lanes] = arrived[
                    sender, 2 * SUBLANES : rows
                ]
                start = offset * rows + part * share
                place = (step % 2) * LANES
                filters[step // 2, start : start + share, place : place + LANES] = arrived[
                    sender, rows : rows + share
                ]
        data[0, step] = forward(0, product[step])
        if step % 2:
            for side in range(2):
                both = forward(side, filters[step // 2])
                known[side, step - 1] = both[:, :LANES]
                known[side, step] = both[:, LANES:]

    for step in range(count):
        for tile in range(tiles):
            multiply(0, step * tiles + tile)
        data[1, step] = forward(1, product[step])

    for step in range(count):
        for tile in range(tiles):
            multiply(1, step * tiles + tile)
        partly[step] = backward(0, step)

    for step in range(count):
        result = (partly[step] + backward(1, step)).astype(ready.dtype)
        for part in range(2):
            for offset in range(near):
                ready[part * places + step * near + offset] = result[
                    offset * rows : (offset + 1) * rows, part * LANES : (part + 1) * LANES
                ]


def convolve_whole(sent, short_weight, owner, rows, forward_table, inverse_table):
    senders, height, _ = sent.shape
    block = forward_table.shape[2]
    length = senders // 2 * rows
    count = length // block
    return pl.pallas_call(
        whole_kernel,
        out_shape=jax.ShapeDtypeStruct((senders, rows, LANES), jnp.bfloat16),
        in_specs=[pl.BlockSpec(memory_space=pltpu.SMEM)]
        + [pl.BlockSpec(memory_space=pltpu.VMEM)] * 4,
        out_specs=pl.BlockSpec(memory_space=pltpu.VMEM),
        scratch_shapes=[
            pltpu.VMEM((count, block, 2 * LANES), jnp.bfloat16),
            pltpu.VMEM((count // 2, block, 2 * LANES), jnp.bfloat16),
            pltpu.VMEM((2, count, block, 2 * LANES), jnp.float32),
            pltpu.VMEM((2, count, block, LANES), jnp.float32),
            pltpu.VMEM((2, count, block, 2 * LANES), jnp.float32),
            pltpu.VMEM((count, block, 2 * LANES), jnp.float32),
        ],
        compiler_params=pltpu.CompilerParams(vmem_limit_bytes=32 * MIB),
        cost_estimate=pl.CostEstimate(
            flops=40 * length * block * LANES,
            bytes_accessed=2 * senders * (height + rows) * LANES,
            transcendentals=0,
        ),
    )(owner.reshape(1), forward_table, inverse_table, short_weight, sent)


def exchange(value, axes):
    return lax.all_to_all(value, axes, split_axis=0, concat_axis=0, tiled=True)


def on_device(query_in, key_in, value_in, long_filter, short_weight, skip_gain):
    places = lax.axis_size("seq")
    parts = lax.axis_size("groups")
    group = lax.axis_index("groups").astype(jnp.int32)
    place = lax.axis_index("seq").astype(jnp.int32)
    rows, channels = key_in.shape
    length = places * rows
    block = BLOCK if length % BLOCK == 0 else rows
    rim = short_weight.shape[1] - 1
    owners = parts * places
    count = length // block
    aligned = (
        parts == 2
        and rim == 2
        and channels == owners * LANES
        and rows % 32 == 0
        and block % rows == 0
        and block == BLOCK
        and count in (2, 4, 8)
    )
    forward_table, inverse_table = half_tables(block) if aligned else transform_tables(block)
    forward_table = jnp.asarray(forward_table)
    inverse_table = jnp.asarray(inverse_table)
    if aligned:
        sent, edges = pack(
            query_in, key_in, value_in, long_filter, short_weight, group, owners, parts
        )
        received = exchange(sent, ("groups", "seq"))
        edges = from_behind(edges, "seq")
        prepared = prepare(sent, query_in, short_weight, skip_gain)
        received, edges, prepared = lax.optimization_barrier((received, edges, prepared))
        owner = group * places + place
        convolved = convolve_whole(
            received, short_weight, owner, rows, forward_table, inverse_table
        )
        convolved = exchange(convolved, ("groups", "seq"))
        return finish(
            convolved, prepared, sent, query_in, edges, short_weight, skip_gain
        )
    else:
        width = channels // places
        edges = jnp.stack([query_in[-rim:], key_in[-rim:], value_in[-rim:]])
        sent = long_filter.reshape(rows, places, width).transpose(1, 0, 2)
        spectra = filter_spectra(exchange(sent, "seq").reshape(length, width), forward_table)
        edges = from_behind(edges, "seq")
        product = products(key_in, value_in, edges, short_weight)
        sent = product.reshape(rows, places, width).transpose(1, 0, 2)
        received = exchange(sent, "seq").reshape(length, width)
        convolved = convolve(received, spectra, forward_table, inverse_table)
        convolved = exchange(convolved.reshape(places, rows, width), "seq")
        convolved = convolved.transpose(1, 0, 2).reshape(rows, channels // LANES, LANES)
        convolved = convolved.transpose(1, 0, 2)
        return gate(convolved, product, query_in, edges, short_weight, skip_gain)


def solution(mesh):
    placed = (
        P(("groups", "seq"), None),
        P(("groups", "seq"), None),
        P(("groups", "seq"), None),
        P("seq", None),
        P(),
        P(),
    )
    return jax.shard_map(
        on_device, mesh=mesh, in_specs=placed, out_specs=P(("groups", "seq"), None), check_vma=False
    )
```

```python
import functools

import jax
import jax.numpy as jnp
import ml_dtypes
import numpy as np
from jax import lax
from jax.experimental import pallas as pl
from jax.experimental.pallas import tpu as pltpu
from jax.sharding import PartitionSpec as P

LANES = 128
SUBLANES = 8
BLOCK = 256
UNROLLED = 8
MIB = 1 << 20


def from_behind(value, axis):
    count = lax.axis_size(axis)
    return lax.ppermute(value, axis, [(source, source + 1) for source in range(count - 1)])


def transform_tables(block):
    numbers = np.concatenate([np.arange(0, block, 2), np.arange(1, block, 2)])
    quarter = (2 * numbers[:, None] + 1) * np.arange(block)[None, :] % (4 * block)
    angle = quarter.astype(np.float64) * (2.0 * np.pi / (4 * block))
    table = np.concatenate([np.cos(angle), -np.sin(angle)], axis=0)

    def split(values):
        high = values.astype(ml_dtypes.bfloat16)
        low = (values - high.astype(np.float64)).astype(ml_dtypes.bfloat16)
        return np.concatenate([high, low], axis=0)

    return split(table), split(table.T / block)


def half_tables(block):
    forward, inverse = transform_tables(block)
    half = block // 2
    rows = np.arange(2 * block).reshape(2, 2, half).transpose(1, 0, 2).reshape(2, block)
    forward = forward.reshape(2, 2 * block, block)
    forward = np.stack([forward[:, rows[side]].reshape(2 * block, block) for side in range(2)])
    inverse = np.stack([inverse[:, rows[side]] for side in range(2)])
    return forward, inverse


def shifted(values, edge, steps):
    rolled = pltpu.roll(values, steps, 0)
    row = lax.broadcasted_iota(jnp.int32, values.shape, 0)
    for place in range(steps):
        source = edge[edge.shape[0] - steps + place : edge.shape[0] - steps + place + 1]
        rolled = jnp.where(row == place, jnp.broadcast_to(source, values.shape), rolled)
    return rolled


def featurize_inside(own, taps):
    result = taps[0:1] * own
    for offset in range(1, taps.shape[0]):
        result = result + taps[offset : offset + 1] * pltpu.roll(own, offset, 0)
    return result


def featurize(own, edge, taps):
    own = own.astype(jnp.float32)
    edge = edge.astype(jnp.float32)
    top = own[:SUBLANES]
    first = taps[0:1] * top
    for offset in range(1, taps.shape[0]):
        first = first + taps[offset : offset + 1] * shifted(top, edge, offset)
    return jnp.concatenate([first, featurize_inside(own, taps)[SUBLANES:]], axis=0)


def product_kernel(key_ref, value_ref, edge_ref, taps_ref, out_ref):
    for start in range(0, key_ref.shape[1], LANES):
        span = slice(start, start + LANES)
        k_short = featurize(key_ref[:, span], edge_ref[1, :, span], taps_ref[1, :, span])
        v_short = featurize(value_ref[:, span], edge_ref[2, :, span], taps_ref[2, :, span])
        out_ref[:, span] = (k_short * v_short).astype(out_ref.dtype)


def products(key_in, value_in, edges, short_weight):
    rows, channels = key_in.shape
    span = min(channels, 1024)
    taps = short_weight.shape[1]
    return pl.pallas_call(
        product_kernel,
        out_shape=jax.ShapeDtypeStruct((rows, channels), jnp.bfloat16),
        grid=(channels // span,),
        in_specs=[
            pl.BlockSpec((rows, span), lambda i: (0, i)),
            pl.BlockSpec((rows, span), lambda i: (0, i)),
            pl.BlockSpec((3, taps - 1, span), lambda i: (0, 0, i)),
            pl.BlockSpec((3, taps, span), lambda i: (0, 0, i)),
        ],
        out_specs=pl.BlockSpec((rows, span), lambda i: (0, i)),
        cost_estimate=pl.CostEstimate(
            flops=12 * rows * channels, bytes_accessed=6 * rows * channels, transcendentals=0
        ),
    )(key_in, value_in, edges, short_weight)


def gate_kernel(conv_ref, product_ref, query_ref, edge_ref, taps_ref, gain_ref, out_ref):
    for part in range(conv_ref.shape[0]):
        span = slice(part * LANES, (part + 1) * LANES)
        q_short = featurize(query_ref[:, span], edge_ref[0, :, span], taps_ref[0, :, span])
        mixed = conv_ref[part].astype(jnp.float32) + gain_ref[:, span] * product_ref[
            :, span
        ].astype(jnp.float32)
        out_ref[:, span] = (q_short * mixed).astype(out_ref.dtype)


def gate(convolved, product, query_in, edges, short_weight, skip_gain):
    rows, channels = query_in.shape
    span = min(channels, 1024)
    taps = short_weight.shape[1]
    across = pl.BlockSpec((rows, span), lambda i: (0, i))
    return pl.pallas_call(
        gate_kernel,
        out_shape=jax.ShapeDtypeStruct((rows, channels), jnp.bfloat16),
        grid=(channels // span,),
        in_specs=[
            pl.BlockSpec((span // LANES, rows, LANES), lambda i: (i, 0, 0)),
            across,
            across,
            pl.BlockSpec((3, taps - 1, span), lambda i: (0, 0, i)),
            pl.BlockSpec((3, taps, span), lambda i: (0, 0, i)),
            pl.BlockSpec((1, span), lambda i: (0, i)),
        ],
        out_specs=across,
        cost_estimate=pl.CostEstimate(
            flops=9 * rows * channels, bytes_accessed=8 * rows * channels, transcendentals=0
        ),
    )(convolved, product, query_in, edges, short_weight, skip_gain.reshape(1, channels))


def prepare_kernel(sent_ref, query_ref, taps_ref, gain_ref, short_ref, direct_ref):
    owners, rows, _ = short_ref.shape
    for owner in range(owners):
        lanes = slice(owner * LANES, (owner + 1) * LANES)
        q_short = featurize_inside(query_ref[:, lanes].astype(jnp.float32), taps_ref[0, :, lanes])
        product = sent_ref[owner, :rows].astype(jnp.float32)
        short_ref[owner] = q_short
        direct_ref[owner] = q_short * (gain_ref[:, lanes] * product)


def prepare(sent, query_in, short_weight, skip_gain):
    rows, channels = query_in.shape
    owners, height, _ = sent.shape
    near = min(owners, 8)
    span = near * LANES
    taps = short_weight.shape[1]
    out = pl.BlockSpec((near, rows, LANES), lambda i: (i, 0, 0))
    return pl.pallas_call(
        prepare_kernel,
        out_shape=(jax.ShapeDtypeStruct((owners, rows, LANES), jnp.float32),) * 2,
        grid=(owners // near,),
        in_specs=[
            pl.BlockSpec((near, height, LANES), lambda i: (i, 0, 0)),
            pl.BlockSpec((rows, span), lambda i: (0, i)),
            pl.BlockSpec((3, taps, span), lambda i: (0, 0, i)),
            pl.BlockSpec((1, span), lambda i: (0, i)),
        ],
        out_specs=(out, out),
        cost_estimate=pl.CostEstimate(
            flops=8 * rows * channels, bytes_accessed=12 * rows * channels, transcendentals=0
        ),
    )(sent, query_in, short_weight, skip_gain.reshape(1, channels))


def finish_kernel(
    places, conv_ref, short_ref, direct_ref, sent_ref, query_ref, edge_ref, taps_ref, gain_ref, out_ref,
    ready, sems,
):
    rows, channels = ready.shape
    tail = sent_ref.shape[1] - SUBLANES
    chunks = sems.shape[0]
    span = channels // chunks
    near = span // LANES
    row = lax.broadcasted_iota(jnp.int32, (SUBLANES, LANES), 0)

    def departure(chunk):
        columns = pl.ds(pl.multiple_of(chunk * span, span), span)
        return pltpu.make_async_copy(ready.at[:, columns], out_ref.at[:, columns], sems.at[chunk])

    @pl.loop(0, chunks)
    def _(chunk):
        for part in range(near):
            owner = chunk * near + part
            lanes = pl.ds(pl.multiple_of(owner * LANES, LANES), LANES)
            behind = edge_ref[:, lanes].astype(jnp.float32)
            own = sent_ref[owner, tail:].astype(jnp.float32)
            first = first_products(own, behind, tap_tiles(taps_ref, lanes))
            first = first.astype(jnp.bfloat16).astype(jnp.float32)
            product = sent_ref[owner, :SUBLANES].astype(jnp.float32)
            product = jnp.where(row < 2, first, product)

            weights = taps_ref[0, :, lanes]
            top = query_ref[:SUBLANES, lanes].astype(jnp.float32)
            one = jnp.where(row < 1, pltpu.roll(behind, 5, 0), pltpu.roll(top, 1, 0))
            two = jnp.where(row < 2, pltpu.roll(behind, 6, 0), pltpu.roll(top, 2, 0))
            top = weights[0:1] * top + weights[1:2] * one + weights[2:3] * two

            source = 2 * lax.rem(owner, places) + lax.div(owner, places)
            convolved = conv_ref[source].astype(jnp.float32)
            top = top * convolved[:SUBLANES] + top * (gain_ref[:, lanes] * product)
            result = short_ref[owner] * convolved + direct_ref[owner]
            result = jnp.concatenate([top, result[SUBLANES:]], axis=0)
            ready[:, lanes] = result.astype(ready.dtype)
        departure(chunk).start()

    for chunk in range(chunks):
        departure(chunk).wait()


def finish(convolved, prepared, sent, query_in, edges, short_weight, skip_gain):
    rows, channels = query_in.shape
    chunks = max(1, channels // 512)
    here = pl.BlockSpec(memory_space=pltpu.VMEM)
    return pl.pallas_call(
        functools.partial(finish_kernel, sent.shape[0] // 2),
        out_shape=jax.ShapeDtypeStruct((rows, channels), jnp.bfloat16),
        in_specs=[here] * 8,
        out_specs=pl.BlockSpec(memory_space=pltpu.HBM),
        scratch_shapes=[
            pltpu.VMEM((rows, channels), jnp.bfloat16),
            pltpu.SemaphoreType.DMA((chunks,)),
        ],
        compiler_params=pltpu.CompilerParams(vmem_limit_bytes=8 * MIB),
        cost_estimate=pl.CostEstimate(
            flops=3 * rows * channels, bytes_accessed=12 * rows * channels, transcendentals=0
        ),
    )(
        convolved, *prepared, sent, query_in, edges, short_weight, skip_gain.reshape(1, channels)
    )


def tap_tiles(taps_ref, lanes):
    row = lax.broadcasted_iota(jnp.int32, (SUBLANES, LANES), 0)
    return [
        jnp.where(row < 4, taps_ref[1, tap : tap + 1, lanes], taps_ref[2, tap : tap + 1, lanes])
        for tap in range(taps_ref.shape[1])
    ]


def first_products(tile, behind, weights):
    row = lax.broadcasted_iota(jnp.int32, (SUBLANES, LANES), 0)
    joined = jnp.where(row % 4 >= 2, tile, behind)
    short = weights[0] * joined
    for tap in range(1, len(weights)):
        short = short + weights[tap] * pltpu.roll(joined, tap, 0)
    return pltpu.roll(short * pltpu.roll(short, 4, 0), 6, 0)


def pack_kernel(
    group_ref, query_ref, key_ref, value_ref, filter_ref, taps_ref, out_ref, edges_ref,
    query, key, value, filters, taps, packed, edges, in_sems, one_sems, out_sems,
):
    rows, channels = key.shape
    share = filters.shape[0]
    chunks = out_sems.shape[0]
    span = channels // chunks
    near = span // LANES
    start = pl.multiple_of(group_ref[0] * share, share)
    whole = [
        pltpu.make_async_copy(taps_ref, taps, one_sems.at[0]),
        pltpu.make_async_copy(query_ref.at[pl.ds(rows - SUBLANES, SUBLANES)], query, one_sems.at[1]),
    ]

    def arrivals(chunk):
        columns = pl.ds(pl.multiple_of(chunk * span, span), span)
        return [
            pltpu.make_async_copy(key_ref.at[:, columns], key.at[:, columns], in_sems.at[0, chunk]),
            pltpu.make_async_copy(
                value_ref.at[:, columns], value.at[:, columns], in_sems.at[1, chunk]
            ),
            pltpu.make_async_copy(
                filter_ref.at[pl.ds(start, share), columns],
                filters.at[:, columns],
                in_sems.at[2, chunk],
            ),
        ]

    def departure(chunk):
        owners = pl.ds(chunk * near, near)
        return pltpu.make_async_copy(packed.at[owners], out_ref.at[owners], out_sems.at[chunk])

    for copy in whole:
        copy.start()
    for chunk in range(chunks):
        for copy in arrivals(chunk):
            copy.start(priority=1)
    for copy in whole:
        copy.wait()
    row = lax.broadcasted_iota(jnp.int32, (SUBLANES, LANES), 0)

    @pl.loop(0, chunks)
    def _(chunk):
        for copy in arrivals(chunk):
            copy.wait()
        for part in range(near):
            span_here = pl.ds(pl.multiple_of(chunk * span + part * LANES, LANES), LANES)
            owner = chunk * near + part
            key_here = key[:, span_here].astype(jnp.float32)
            value_here = value[:, span_here].astype(jnp.float32)
            k_short = featurize_inside(key_here, taps[1, :, span_here])
            v_short = featurize_inside(value_here, taps[2, :, span_here])
            packed[owner, :rows] = (k_short * v_short).astype(packed.dtype)
            packed[owner, rows : rows + share] = filters[:, span_here]
            query_last = pltpu.roll(query[:, span_here].astype(jnp.float32), 4, 0)
            key_tile = jnp.where(
                row < 2,
                pltpu.roll(key_here[rows - SUBLANES :], 2, 0),
                pltpu.roll(key_here[:SUBLANES], 2, 0),
            )
            value_tile = jnp.where(
                row < 6,
                pltpu.roll(value_here[rows - SUBLANES :], 6, 0),
                pltpu.roll(value_here[:SUBLANES], 6, 0),
            )
            edge = jnp.where(row < 4, key_tile, value_tile)
            packed[owner, rows + share :] = edge.astype(packed.dtype)
            edge = jnp.where((row == 2) | (row == 3), query_last, edge)
            edges[:, span_here] = edge.astype(edges.dtype)
        departure(chunk).start()

    last = pltpu.make_async_copy(edges, edges_ref, one_sems.at[0])
    last.start()
    for chunk in range(chunks):
        departure(chunk).wait()
    last.wait()


def pack(query_in, key_in, value_in, long_filter, short_weight, group, owners, parts):
    rows, channels = key_in.shape
    chunks = max(1, channels // 1024)
    taps = short_weight.shape[1]
    share = rows // parts
    height = rows + share + SUBLANES
    here = pl.BlockSpec(memory_space=pltpu.HBM)
    return pl.pallas_call(
        pack_kernel,
        out_shape=(
            jax.ShapeDtypeStruct((owners, height, LANES), jnp.bfloat16),
            jax.ShapeDtypeStruct((SUBLANES, channels), jnp.bfloat16),
        ),
        in_specs=[pl.BlockSpec(memory_space=pltpu.SMEM)] + [here] * 5,
        out_specs=(here, here),
        scratch_shapes=[
            pltpu.VMEM((SUBLANES, channels), jnp.bfloat16),
            pltpu.VMEM((rows, channels), jnp.bfloat16),
            pltpu.VMEM((rows, channels), jnp.bfloat16),
            pltpu.VMEM((share, channels), jnp.bfloat16),
            pltpu.VMEM((3, taps, channels), jnp.float32),
            pltpu.VMEM((owners, height, LANES), jnp.bfloat16),
            pltpu.VMEM((SUBLANES, channels), jnp.bfloat16),
            pltpu.SemaphoreType.DMA((3, chunks)),
            pltpu.SemaphoreType.DMA((2,)),
            pltpu.SemaphoreType.DMA((chunks,)),
        ],
        cost_estimate=pl.CostEstimate(
            flops=12 * rows * channels, bytes_accessed=8 * rows * channels, transcendentals=0
        ),
    )(group.reshape(1), query_in, key_in, value_in, long_filter, short_weight)


def transform(table, values):
    both = jnp.dot(table, values, preferred_element_type=jnp.float32)
    half = table.shape[0] // 2
    return both[:half] + both[half:]


def over(count, body):
    if count <= UNROLLED:
        for step in range(count):
            body(step)
    else:

        @pl.loop(0, count)
        def _(step):
            body(step)


def filter_kernel(table_ref, filter_ref, out_ref):
    count, double, _ = out_ref.shape
    block = double // 2

    def body(step):
        start = step * block
        if not isinstance(step, int):
            start = pl.multiple_of(start, block)
        out_ref[step] = transform(table_ref[...], filter_ref[pl.ds(start, block), :])

    over(count, body)


def filter_spectra(long_filter, table):
    length, width = long_filter.shape
    block = table.shape[1]
    return pl.pallas_call(
        filter_kernel,
        out_shape=jax.ShapeDtypeStruct((length // block, 2 * block, width), jnp.float32),
        in_specs=[pl.BlockSpec(memory_space=pltpu.VMEM)] * 2,
        out_specs=pl.BlockSpec(memory_space=pltpu.VMEM),
        compiler_params=pltpu.CompilerParams(vmem_limit_bytes=40 * MIB),
        cost_estimate=pl.CostEstimate(
            flops=8 * length * block * width, bytes_accessed=10 * length * width, transcendentals=0
        ),
    )(table, long_filter)


def inverse(table_ref, values, block):
    high = values.astype(jnp.bfloat16)
    low = (values - high.astype(jnp.float32)).astype(jnp.bfloat16)
    return transform(table_ref[...], high) + jnp.dot(
        table_ref[:block], low, preferred_element_type=jnp.float32
    )


def conv_kernel(forward_ref, inverse_ref, product_ref, filter_ref, out_ref, data, mixed, last):
    count, double, width = filter_ref.shape
    block = double // 2
    lane_step = min(width, LANES)

    def piece(step):
        start = step * block
        return pl.ds(start if isinstance(step, int) else pl.multiple_of(start, block), block)

    def forward(step):
        data[step] = transform(forward_ref[...], product_ref[piece(step), :])

    over(count, forward)
    last[...] = jnp.zeros_like(last)

    @pl.loop(0, count)
    def _(total):
        for sign, base in ((1.0, 0), (-1.0, block // 2)):
            for column in range(0, width, lane_step):
                lanes = slice(column, column + lane_step)

                @pl.loop(0, block // 2 // SUBLANES)
                def _(index):
                    start = pl.multiple_of(base + index * SUBLANES, SUBLANES)
                    real = pl.ds(start, SUBLANES)
                    imag = pl.ds(pl.multiple_of(block + start, SUBLANES), SUBLANES)

                    def add(step, sums):
                        a, b = data[step, real, lanes], data[step, imag, lanes]
                        c = filter_ref[total - step, real, lanes]
                        d = filter_ref[total - step, imag, lanes]
                        return sums[0] + (a * c - b * d), sums[1] + (a * d + b * c)

                    zero = jnp.zeros((SUBLANES, lane_step), jnp.float32)
                    sum_real, sum_imag = lax.fori_loop(0, total + 1, add, (zero, zero))
                    mixed[real, lanes] = sum_real - sign * last[imag, lanes]
                    mixed[imag, lanes] = sum_imag + sign * last[real, lanes]
                    last[real, lanes] = sum_real
                    last[imag, lanes] = sum_imag

        out_ref[piece(total), :] = inverse(inverse_ref, mixed[...], block).astype(out_ref.dtype)


def convolve(product, spectra, forward_table, inverse_table):
    length, width = product.shape
    count, double, _ = spectra.shape
    return pl.pallas_call(
        conv_kernel,
        out_shape=jax.ShapeDtypeStruct((length, width), jnp.bfloat16),
        in_specs=[pl.BlockSpec(memory_space=pltpu.VMEM)] * 4,
        out_specs=pl.BlockSpec(memory_space=pltpu.VMEM),
        scratch_shapes=[
            pltpu.VMEM((count, double, width), jnp.float32),
            pltpu.VMEM((double, width), jnp.float32),
            pltpu.VMEM((double, width), jnp.float32),
        ],
        compiler_params=pltpu.CompilerParams(vmem_limit_bytes=56 * MIB),
        cost_estimate=pl.CostEstimate(
            flops=16 * length * double * width,
            bytes_accessed=12 * length * width,
            transcendentals=0,
        ),
    )(forward_table, inverse_table, product, spectra)


def whole_kernel(
    owner_ref, forward_ref, inverse_ref, taps_ref, arrived, ready,
    product, filters, data, known, mixed, partly,
):
    del owner_ref
    senders, rows, _ = ready.shape
    places = senders // 2
    share = rows // 2
    _, count, block, _ = data.shape
    half = block // 2
    near = block // rows
    tiles = half // SUBLANES // count
    row = lax.broadcasted_iota(jnp.int32, (SUBLANES, LANES), 0)
    weights = tap_tiles(taps_ref, slice(None))

    def forward(side, values):
        return transform(forward_ref[side], values)

    def backward(side, step):
        return inverse(inverse_ref.at[side], mixed[side, step], block)

    def multiply(side, tile):
        start = tile * SUBLANES
        real = slice(start, start + SUBLANES)
        imag = slice(half + start, half + start + SUBLANES)
        filter_parts = []
        for step in range(count):
            c, d = known[side, step, real], known[side, step, imag]
            filter_parts.append((c, d - c, c + d))
        for part in range(2):
            lanes = slice(part * LANES, (part + 1) * LANES)
            data_parts = []
            for step in range(count):
                a, b = data[side, step, real, lanes], data[side, step, imag, lanes]
                data_parts.append((a + b, a, b))
            before = None
            for total in range(count):
                sums = None
                for step in range(total + 1):
                    pairs = zip(data_parts[step], filter_parts[total - step])
                    terms = [x * y for x, y in pairs]
                    sums = terms if sums is None else [x + y for x, y in zip(sums, terms)]
                both = (sums[0] - sums[2], sums[0] + sums[1])
                if before is None:
                    out = both
                elif side == 0:
                    out = (both[0] - before[1], both[1] + before[0])
                else:
                    out = (both[0] + before[1], both[1] - before[0])
                mixed[side, total, real, lanes] = out[0]
                mixed[side, total, imag, lanes] = out[1]
                before = both

    behind = [jnp.zeros((SUBLANES, LANES), jnp.float32)] * 2
    for step in range(count):
        for part in range(2):
            lanes = slice(part * LANES, (part + 1) * LANES)
            for offset in range(near):
                sender = part * places + step * near + offset
                edge = arrived[sender, rows + share :].astype(jnp.float32)
                first = first_products(edge, behind[part], weights)
                behind[part] = edge
                values = arrived[sender, : 2 * SUBLANES].astype(jnp.float32)
                top = jnp.where(row < 2, first, values[:SUBLANES])
                values = jnp.concatenate([top, values[SUBLANES:]], axis=0)
                start = offset * rows
                product[step, start : start + 2 * SUBLANES, lanes] = values.astype(product.dtype)
                product[step, start + 2 * SUBLANES : start + rows, lanes] = arrived[
                    sender, 2 * SUBLANES : rows
                ]
                start = offset * rows + part * share
                place = (step % 2) * LANES
                filters[step // 2, start : start + share, place : place + LANES] = arrived[
                    sender, rows : rows + share
                ]
        data[0, step] = forward(0, product[step])
        if step % 2:
            for side in range(2):
                both = forward(side, filters[step // 2])
                known[side, step - 1] = both[:, :LANES]
                known[side, step] = both[:, LANES:]

    for step in range(count):
        for tile in range(tiles):
            multiply(0, step * tiles + tile)
        data[1, step] = forward(1, product[step])

    for step in range(count):
        for tile in range(tiles):
            multiply(1, step * tiles + tile)
        partly[step] = backward(0, step)

    for step in range(count):
        result = (partly[step] + backward(1, step)).astype(ready.dtype)
        for part in range(2):
            for offset in range(near):
                ready[2 * (step * near + offset) + part] = result[
                    offset * rows : (offset + 1) * rows, part * LANES : (part + 1) * LANES
                ]


def convolve_whole(sent, short_weight, owner, rows, forward_table, inverse_table):
    senders, height, _ = sent.shape
    block = forward_table.shape[2]
    length = senders // 2 * rows
    count = length // block
    taps = short_weight.shape[1]
    return pl.pallas_call(
        whole_kernel,
        out_shape=jax.ShapeDtypeStruct((senders, rows, LANES), jnp.bfloat16),
        grid_spec=pltpu.PrefetchScalarGridSpec(
            num_scalar_prefetch=1,
            grid=(1,),
            in_specs=[
                pl.BlockSpec(memory_space=pltpu.VMEM),
                pl.BlockSpec(memory_space=pltpu.VMEM),
                pl.BlockSpec((3, taps, LANES), lambda i, owner: (0, 0, owner[0])),
                pl.BlockSpec(memory_space=pltpu.VMEM),
            ],
            out_specs=pl.BlockSpec(memory_space=pltpu.VMEM),
            scratch_shapes=[
                pltpu.VMEM((count, block, 2 * LANES), jnp.bfloat16),
                pltpu.VMEM((count // 2, block, 2 * LANES), jnp.bfloat16),
                pltpu.VMEM((2, count, block, 2 * LANES), jnp.float32),
                pltpu.VMEM((2, count, block, LANES), jnp.float32),
                pltpu.VMEM((2, count, block, 2 * LANES), jnp.float32),
                pltpu.VMEM((count, block, 2 * LANES), jnp.float32),
            ],
        ),
        compiler_params=pltpu.CompilerParams(vmem_limit_bytes=32 * MIB),
        cost_estimate=pl.CostEstimate(
            flops=40 * length * block * LANES,
            bytes_accessed=2 * senders * (height + rows) * LANES,
            transcendentals=0,
        ),
    )(owner.reshape(1), forward_table, inverse_table, short_weight, sent)


def exchange(value, axes):
    return lax.all_to_all(value, axes, split_axis=0, concat_axis=0, tiled=True)


def on_device(query_in, key_in, value_in, long_filter, short_weight, skip_gain):
    places = lax.axis_size("seq")
    parts = lax.axis_size("groups")
    group = lax.axis_index("groups").astype(jnp.int32)
    place = lax.axis_index("seq").astype(jnp.int32)
    rows, channels = key_in.shape
    length = places * rows
    block = BLOCK if length % BLOCK == 0 else rows
    rim = short_weight.shape[1] - 1
    owners = parts * places
    count = length // block
    aligned = (
        parts == 2
        and rim == 2
        and channels == owners * LANES
        and rows % 32 == 0
        and block % rows == 0
        and block == BLOCK
        and count in (2, 4, 8)
    )
    forward_table, inverse_table = half_tables(block) if aligned else transform_tables(block)
    forward_table = jnp.asarray(forward_table)
    inverse_table = jnp.asarray(inverse_table)
    if aligned:
        sent, edges = pack(
            query_in, key_in, value_in, long_filter, short_weight, group, owners, parts
        )
        received = exchange(sent, ("groups", "seq"))
        edges = from_behind(edges, "seq")
        prepared = prepare(sent, query_in, short_weight, skip_gain)
        received, edges, prepared = lax.optimization_barrier((received, edges, prepared))
        owner = group * places + place
        convolved = convolve_whole(
            received, short_weight, owner, rows, forward_table, inverse_table
        )
        convolved = exchange(convolved, ("seq", "groups"))
        return finish(
            convolved, prepared, sent, query_in, edges, short_weight, skip_gain
        )
    else:
        width = channels // places
        edges = jnp.stack([query_in[-rim:], key_in[-rim:], value_in[-rim:]])
        sent = long_filter.reshape(rows, places, width).transpose(1, 0, 2)
        spectra = filter_spectra(exchange(sent, "seq").reshape(length, width), forward_table)
        edges = from_behind(edges, "seq")
        product = products(key_in, value_in, edges, short_weight)
        sent = product.reshape(rows, places, width).transpose(1, 0, 2)
        received = exchange(sent, "seq").reshape(length, width)
        convolved = convolve(received, spectra, forward_table, inverse_table)
        convolved = exchange(convolved.reshape(places, rows, width), "seq")
        convolved = convolved.transpose(1, 0, 2).reshape(rows, channels // LANES, LANES)
        convolved = convolved.transpose(1, 0, 2)
        return gate(convolved, product, query_in, edges, short_weight, skip_gain)


def solution(mesh):
    placed = (
        P(("groups", "seq"), None),
        P(("groups", "seq"), None),
        P(("groups", "seq"), None),
        P("seq", None),
        P(),
        P(),
    )
    return jax.shard_map(
        on_device, mesh=mesh, in_specs=placed, out_specs=P(("groups", "seq"), None), check_vma=False
    )
```

```python
import functools

import jax
import jax.numpy as jnp
import ml_dtypes
import numpy as np
from jax import lax
from jax.experimental import pallas as pl
from jax.experimental.pallas import tpu as pltpu
from jax.sharding import PartitionSpec as P

LANES = 128
SUBLANES = 8
BLOCK = 256
UNROLLED = 8
MIB = 1 << 20


def from_behind(value, axis):
    count = lax.axis_size(axis)
    return lax.ppermute(value, axis, [(source, source + 1) for source in range(count - 1)])


def transform_tables(block):
    numbers = np.concatenate([np.arange(0, block, 2), np.arange(1, block, 2)])
    quarter = (2 * numbers[:, None] + 1) * np.arange(block)[None, :] % (4 * block)
    angle = quarter.astype(np.float64) * (2.0 * np.pi / (4 * block))
    table = np.concatenate([np.cos(angle), -np.sin(angle)], axis=0)

    def split(values):
        high = values.astype(ml_dtypes.bfloat16)
        low = (values - high.astype(np.float64)).astype(ml_dtypes.bfloat16)
        return np.concatenate([high, low], axis=0)

    return split(table), split(table.T / block)


def half_tables(block):
    forward, inverse = transform_tables(block)
    half = block // 2
    rows = np.arange(2 * block).reshape(2, 2, half).transpose(1, 0, 2).reshape(2, block)
    forward = forward.reshape(2, 2 * block, block)
    forward = np.stack([forward[:, rows[side]].reshape(2 * block, block) for side in range(2)])
    inverse = np.stack([inverse[:, rows[side]] for side in range(2)])
    return forward, inverse


def shifted(values, edge, steps):
    rolled = pltpu.roll(values, steps, 0)
    row = lax.broadcasted_iota(jnp.int32, values.shape, 0)
    for place in range(steps):
        source = edge[edge.shape[0] - steps + place : edge.shape[0] - steps + place + 1]
        rolled = jnp.where(row == place, jnp.broadcast_to(source, values.shape), rolled)
    return rolled


def featurize_inside(own, taps):
    result = taps[0:1] * own
    for offset in range(1, taps.shape[0]):
        result = result + taps[offset : offset + 1] * pltpu.roll(own, offset, 0)
    return result


def featurize(own, edge, taps):
    own = own.astype(jnp.float32)
    edge = edge.astype(jnp.float32)
    top = own[:SUBLANES]
    first = taps[0:1] * top
    for offset in range(1, taps.shape[0]):
        first = first + taps[offset : offset + 1] * shifted(top, edge, offset)
    return jnp.concatenate([first, featurize_inside(own, taps)[SUBLANES:]], axis=0)


def product_kernel(key_ref, value_ref, edge_ref, taps_ref, out_ref):
    for start in range(0, key_ref.shape[1], LANES):
        span = slice(start, start + LANES)
        k_short = featurize(key_ref[:, span], edge_ref[1, :, span], taps_ref[1, :, span])
        v_short = featurize(value_ref[:, span], edge_ref[2, :, span], taps_ref[2, :, span])
        out_ref[:, span] = (k_short * v_short).astype(out_ref.dtype)


def products(key_in, value_in, edges, short_weight):
    rows, channels = key_in.shape
    span = min(channels, 1024)
    taps = short_weight.shape[1]
    return pl.pallas_call(
        product_kernel,
        out_shape=jax.ShapeDtypeStruct((rows, channels), jnp.bfloat16),
        grid=(channels // span,),
        in_specs=[
            pl.BlockSpec((rows, span), lambda i: (0, i)),
            pl.BlockSpec((rows, span), lambda i: (0, i)),
            pl.BlockSpec((3, taps - 1, span), lambda i: (0, 0, i)),
            pl.BlockSpec((3, taps, span), lambda i: (0, 0, i)),
        ],
        out_specs=pl.BlockSpec((rows, span), lambda i: (0, i)),
        cost_estimate=pl.CostEstimate(
            flops=12 * rows * channels, bytes_accessed=6 * rows * channels, transcendentals=0
        ),
    )(key_in, value_in, edges, short_weight)


def gate_kernel(conv_ref, product_ref, query_ref, edge_ref, taps_ref, gain_ref, out_ref):
    for part in range(conv_ref.shape[0]):
        span = slice(part * LANES, (part + 1) * LANES)
        q_short = featurize(query_ref[:, span], edge_ref[0, :, span], taps_ref[0, :, span])
        mixed = conv_ref[part].astype(jnp.float32) + gain_ref[:, span] * product_ref[
            :, span
        ].astype(jnp.float32)
        out_ref[:, span] = (q_short * mixed).astype(out_ref.dtype)


def gate(convolved, product, query_in, edges, short_weight, skip_gain):
    rows, channels = query_in.shape
    span = min(channels, 1024)
    taps = short_weight.shape[1]
    across = pl.BlockSpec((rows, span), lambda i: (0, i))
    return pl.pallas_call(
        gate_kernel,
        out_shape=jax.ShapeDtypeStruct((rows, channels), jnp.bfloat16),
        grid=(channels // span,),
        in_specs=[
            pl.BlockSpec((span // LANES, rows, LANES), lambda i: (i, 0, 0)),
            across,
            across,
            pl.BlockSpec((3, taps - 1, span), lambda i: (0, 0, i)),
            pl.BlockSpec((3, taps, span), lambda i: (0, 0, i)),
            pl.BlockSpec((1, span), lambda i: (0, i)),
        ],
        out_specs=across,
        cost_estimate=pl.CostEstimate(
            flops=9 * rows * channels, bytes_accessed=8 * rows * channels, transcendentals=0
        ),
    )(convolved, product, query_in, edges, short_weight, skip_gain.reshape(1, channels))


def prepare_kernel(sent_ref, query_ref, taps_ref, gain_ref, short_ref, direct_ref):
    owners, rows, _ = short_ref.shape
    for owner in range(owners):
        lanes = slice(owner * LANES, (owner + 1) * LANES)
        q_short = featurize_inside(query_ref[:, lanes].astype(jnp.float32), taps_ref[0, :, lanes])
        product = sent_ref[owner, :rows].astype(jnp.float32)
        short_ref[owner] = q_short
        direct_ref[owner] = q_short * (gain_ref[:, lanes] * product)


def prepare(sent, query_in, short_weight, skip_gain):
    rows, channels = query_in.shape
    owners, height, _ = sent.shape
    near = min(owners, 8)
    span = near * LANES
    taps = short_weight.shape[1]
    out = pl.BlockSpec((near, rows, LANES), lambda i: (i, 0, 0))
    return pl.pallas_call(
        prepare_kernel,
        out_shape=(jax.ShapeDtypeStruct((owners, rows, LANES), jnp.float32),) * 2,
        grid=(owners // near,),
        in_specs=[
            pl.BlockSpec((near, height, LANES), lambda i: (i, 0, 0)),
            pl.BlockSpec((rows, span), lambda i: (0, i)),
            pl.BlockSpec((3, taps, span), lambda i: (0, 0, i)),
            pl.BlockSpec((1, span), lambda i: (0, i)),
        ],
        out_specs=(out, out),
        cost_estimate=pl.CostEstimate(
            flops=8 * rows * channels, bytes_accessed=12 * rows * channels, transcendentals=0
        ),
    )(sent, query_in, short_weight, skip_gain.reshape(1, channels))


def finish_kernel(
    places, conv_ref, short_ref, direct_ref, sent_ref, query_ref, edge_ref, taps_ref, gain_ref, out_ref,
    ready, sems,
):
    rows, channels = ready.shape
    tail = sent_ref.shape[1] - SUBLANES
    chunks = sems.shape[0]
    span = channels // chunks
    near = span // LANES
    row = lax.broadcasted_iota(jnp.int32, (SUBLANES, LANES), 0)

    def departure(chunk):
        columns = pl.ds(pl.multiple_of(chunk * span, span), span)
        return pltpu.make_async_copy(ready.at[:, columns], out_ref.at[:, columns], sems.at[chunk])

    @pl.loop(0, chunks)
    def _(chunk):
        for part in range(near):
            owner = chunk * near + part
            lanes = pl.ds(pl.multiple_of(owner * LANES, LANES), LANES)
            behind = edge_ref[:, lanes].astype(jnp.float32)
            own = sent_ref[owner, tail:].astype(jnp.float32)
            first = first_products(own, behind, tap_tiles(taps_ref, lanes))
            first = first.astype(jnp.bfloat16).astype(jnp.float32)
            product = sent_ref[owner, :SUBLANES].astype(jnp.float32)
            product = jnp.where(row < 2, first, product)

            weights = taps_ref[0, :, lanes]
            top = query_ref[:SUBLANES, lanes].astype(jnp.float32)
            one = jnp.where(row < 1, pltpu.roll(behind, 5, 0), pltpu.roll(top, 1, 0))
            two = jnp.where(row < 2, pltpu.roll(behind, 6, 0), pltpu.roll(top, 2, 0))
            top = weights[0:1] * top + weights[1:2] * one + weights[2:3] * two

            source = 2 * owner - jnp.where(owner >= places, 2 * places - 1, 0)
            convolved = conv_ref[source].astype(jnp.float32)
            top = top * convolved[:SUBLANES] + top * (gain_ref[:, lanes] * product)
            result = short_ref[owner] * convolved + direct_ref[owner]
            result = jnp.concatenate([top, result[SUBLANES:]], axis=0)
            ready[:, lanes] = result.astype(ready.dtype)
        departure(chunk).start()

    for chunk in range(chunks):
        departure(chunk).wait()


def finish(convolved, prepared, sent, query_in, edges, short_weight, skip_gain):
    rows, channels = query_in.shape
    chunks = max(1, channels // 512)
    here = pl.BlockSpec(memory_space=pltpu.VMEM)
    return pl.pallas_call(
        functools.partial(finish_kernel, sent.shape[0] // 2),
        out_shape=jax.ShapeDtypeStruct((rows, channels), jnp.bfloat16),
        in_specs=[here] * 8,
        out_specs=pl.BlockSpec(memory_space=pltpu.HBM),
        scratch_shapes=[
            pltpu.VMEM((rows, channels), jnp.bfloat16),
            pltpu.SemaphoreType.DMA((chunks,)),
        ],
        compiler_params=pltpu.CompilerParams(vmem_limit_bytes=8 * MIB),
        cost_estimate=pl.CostEstimate(
            flops=3 * rows * channels, bytes_accessed=12 * rows * channels, transcendentals=0
        ),
    )(
        convolved, *prepared, sent, query_in, edges, short_weight, skip_gain.reshape(1, channels)
    )


def tap_tiles(taps_ref, lanes):
    row = lax.broadcasted_iota(jnp.int32, (SUBLANES, LANES), 0)
    return [
        jnp.where(row < 4, taps_ref[1, tap : tap + 1, lanes], taps_ref[2, tap : tap + 1, lanes])
        for tap in range(taps_ref.shape[1])
    ]


def first_products(tile, behind, weights):
    row = lax.broadcasted_iota(jnp.int32, (SUBLANES, LANES), 0)
    joined = jnp.where(row % 4 >= 2, tile, behind)
    short = weights[0] * joined
    for tap in range(1, len(weights)):
        short = short + weights[tap] * pltpu.roll(joined, tap, 0)
    return pltpu.roll(short * pltpu.roll(short, 4, 0), 6, 0)


def pack_kernel(
    group_ref, query_ref, key_ref, value_ref, filter_ref, taps_ref, out_ref, edges_ref,
    query, key, value, filters, taps, packed, edges, in_sems, one_sems, out_sems,
):
    rows, channels = key.shape
    share = filters.shape[0]
    chunks = out_sems.shape[0]
    span = channels // chunks
    near = span // LANES
    start = pl.multiple_of(group_ref[0] * share, share)
    whole = [
        pltpu.make_async_copy(taps_ref, taps, one_sems.at[0]),
        pltpu.make_async_copy(query_ref.at[pl.ds(rows - SUBLANES, SUBLANES)], query, one_sems.at[1]),
    ]

    def arrivals(chunk):
        columns = pl.ds(pl.multiple_of(chunk * span, span), span)
        return [
            pltpu.make_async_copy(key_ref.at[:, columns], key.at[:, columns], in_sems.at[0, chunk]),
            pltpu.make_async_copy(
                value_ref.at[:, columns], value.at[:, columns], in_sems.at[1, chunk]
            ),
            pltpu.make_async_copy(
                filter_ref.at[pl.ds(start, share), columns],
                filters.at[:, columns],
                in_sems.at[2, chunk],
            ),
        ]

    def departure(chunk):
        owners = pl.ds(chunk * near, near)
        return pltpu.make_async_copy(packed.at[owners], out_ref.at[owners], out_sems.at[chunk])

    for copy in whole:
        copy.start()
    for chunk in range(chunks):
        for copy in arrivals(chunk):
            copy.start(priority=1)
    for copy in whole:
        copy.wait()
    row = lax.broadcasted_iota(jnp.int32, (SUBLANES, LANES), 0)

    @pl.loop(0, chunks)
    def _(chunk):
        for copy in arrivals(chunk):
            copy.wait()
        for part in range(near):
            span_here = pl.ds(pl.multiple_of(chunk * span + part * LANES, LANES), LANES)
            owner = chunk * near + part
            key_here = key[:, span_here].astype(jnp.float32)
            value_here = value[:, span_here].astype(jnp.float32)
            k_short = featurize_inside(key_here, taps[1, :, span_here])
            v_short = featurize_inside(value_here, taps[2, :, span_here])
            packed[owner, :rows] = (k_short * v_short).astype(packed.dtype)
            packed[owner, rows : rows + share] = filters[:, span_here]
            query_last = pltpu.roll(query[:, span_here].astype(jnp.float32), 4, 0)
            key_tile = jnp.where(
                row < 2,
                pltpu.roll(key_here[rows - SUBLANES :], 2, 0),
                pltpu.roll(key_here[:SUBLANES], 2, 0),
            )
            value_tile = jnp.where(
                row < 6,
                pltpu.roll(value_here[rows - SUBLANES :], 6, 0),
                pltpu.roll(value_here[:SUBLANES], 6, 0),
            )
            edge = jnp.where(row < 4, key_tile, value_tile)
            packed[owner, rows + share :] = edge.astype(packed.dtype)
            edge = jnp.where((row == 2) | (row == 3), query_last, edge)
            edges[:, span_here] = edge.astype(edges.dtype)
        departure(chunk).start()

    last = pltpu.make_async_copy(edges, edges_ref, one_sems.at[0])
    last.start()
    for chunk in range(chunks):
        departure(chunk).wait()
    last.wait()


def pack(query_in, key_in, value_in, long_filter, short_weight, group, owners, parts):
    rows, channels = key_in.shape
    chunks = max(1, channels // 1024)
    taps = short_weight.shape[1]
    share = rows // parts
    height = rows + share + SUBLANES
    here = pl.BlockSpec(memory_space=pltpu.HBM)
    return pl.pallas_call(
        pack_kernel,
        out_shape=(
            jax.ShapeDtypeStruct((owners, height, LANES), jnp.bfloat16),
            jax.ShapeDtypeStruct((SUBLANES, channels), jnp.bfloat16),
        ),
        in_specs=[pl.BlockSpec(memory_space=pltpu.SMEM)] + [here] * 5,
        out_specs=(here, here),
        scratch_shapes=[
            pltpu.VMEM((SUBLANES, channels), jnp.bfloat16),
            pltpu.VMEM((rows, channels), jnp.bfloat16),
            pltpu.VMEM((rows, channels), jnp.bfloat16),
            pltpu.VMEM((share, channels), jnp.bfloat16),
            pltpu.VMEM((3, taps, channels), jnp.float32),
            pltpu.VMEM((owners, height, LANES), jnp.bfloat16),
            pltpu.VMEM((SUBLANES, channels), jnp.bfloat16),
            pltpu.SemaphoreType.DMA((3, chunks)),
            pltpu.SemaphoreType.DMA((2,)),
            pltpu.SemaphoreType.DMA((chunks,)),
        ],
        cost_estimate=pl.CostEstimate(
            flops=12 * rows * channels, bytes_accessed=8 * rows * channels, transcendentals=0
        ),
    )(group.reshape(1), query_in, key_in, value_in, long_filter, short_weight)


def transform(table, values):
    both = jnp.dot(table, values, preferred_element_type=jnp.float32)
    half = table.shape[0] // 2
    return both[:half] + both[half:]


def over(count, body):
    if count <= UNROLLED:
        for step in range(count):
            body(step)
    else:

        @pl.loop(0, count)
        def _(step):
            body(step)


def filter_kernel(table_ref, filter_ref, out_ref):
    count, double, _ = out_ref.shape
    block = double // 2

    def body(step):
        start = step * block
        if not isinstance(step, int):
            start = pl.multiple_of(start, block)
        out_ref[step] = transform(table_ref[...], filter_ref[pl.ds(start, block), :])

    over(count, body)


def filter_spectra(long_filter, table):
    length, width = long_filter.shape
    block = table.shape[1]
    return pl.pallas_call(
        filter_kernel,
        out_shape=jax.ShapeDtypeStruct((length // block, 2 * block, width), jnp.float32),
        in_specs=[pl.BlockSpec(memory_space=pltpu.VMEM)] * 2,
        out_specs=pl.BlockSpec(memory_space=pltpu.VMEM),
        compiler_params=pltpu.CompilerParams(vmem_limit_bytes=40 * MIB),
        cost_estimate=pl.CostEstimate(
            flops=8 * length * block * width, bytes_accessed=10 * length * width, transcendentals=0
        ),
    )(table, long_filter)


def inverse(table_ref, values, block):
    high = values.astype(jnp.bfloat16)
    low = (values - high.astype(jnp.float32)).astype(jnp.bfloat16)
    return transform(table_ref[...], high) + jnp.dot(
        table_ref[:block], low, preferred_element_type=jnp.float32
    )


def conv_kernel(forward_ref, inverse_ref, product_ref, filter_ref, out_ref, data, mixed, last):
    count, double, width = filter_ref.shape
    block = double // 2
    lane_step = min(width, LANES)

    def piece(step):
        start = step * block
        return pl.ds(start if isinstance(step, int) else pl.multiple_of(start, block), block)

    def forward(step):
        data[step] = transform(forward_ref[...], product_ref[piece(step), :])

    over(count, forward)
    last[...] = jnp.zeros_like(last)

    @pl.loop(0, count)
    def _(total):
        for sign, base in ((1.0, 0), (-1.0, block // 2)):
            for column in range(0, width, lane_step):
                lanes = slice(column, column + lane_step)

                @pl.loop(0, block // 2 // SUBLANES)
                def _(index):
                    start = pl.multiple_of(base + index * SUBLANES, SUBLANES)
                    real = pl.ds(start, SUBLANES)
                    imag = pl.ds(pl.multiple_of(block + start, SUBLANES), SUBLANES)

                    def add(step, sums):
                        a, b = data[step, real, lanes], data[step, imag, lanes]
                        c = filter_ref[total - step, real, lanes]
                        d = filter_ref[total - step, imag, lanes]
                        return sums[0] + (a * c - b * d), sums[1] + (a * d + b * c)

                    zero = jnp.zeros((SUBLANES, lane_step), jnp.float32)
                    sum_real, sum_imag = lax.fori_loop(0, total + 1, add, (zero, zero))
                    mixed[real, lanes] = sum_real - sign * last[imag, lanes]
                    mixed[imag, lanes] = sum_imag + sign * last[real, lanes]
                    last[real, lanes] = sum_real
                    last[imag, lanes] = sum_imag

        out_ref[piece(total), :] = inverse(inverse_ref, mixed[...], block).astype(out_ref.dtype)


def convolve(product, spectra, forward_table, inverse_table):
    length, width = product.shape
    count, double, _ = spectra.shape
    return pl.pallas_call(
        conv_kernel,
        out_shape=jax.ShapeDtypeStruct((length, width), jnp.bfloat16),
        in_specs=[pl.BlockSpec(memory_space=pltpu.VMEM)] * 4,
        out_specs=pl.BlockSpec(memory_space=pltpu.VMEM),
        scratch_shapes=[
            pltpu.VMEM((count, double, width), jnp.float32),
            pltpu.VMEM((double, width), jnp.float32),
            pltpu.VMEM((double, width), jnp.float32),
        ],
        compiler_params=pltpu.CompilerParams(vmem_limit_bytes=56 * MIB),
        cost_estimate=pl.CostEstimate(
            flops=16 * length * double * width,
            bytes_accessed=12 * length * width,
            transcendentals=0,
        ),
    )(forward_table, inverse_table, product, spectra)


def whole_kernel(
    owner_ref, forward_ref, inverse_ref, taps_ref, arrived, ready,
    product, filters, data, known, mixed, partly,
):
    del owner_ref
    senders, rows, _ = ready.shape
    places = senders // 2
    share = rows // 2
    _, count, block, _ = data.shape
    half = block // 2
    near = block // rows
    tiles = half // SUBLANES // count
    row = lax.broadcasted_iota(jnp.int32, (SUBLANES, LANES), 0)
    weights = tap_tiles(taps_ref, slice(None))

    def forward(side, values):
        return transform(forward_ref[side], values)

    def backward(side, step):
        return inverse(inverse_ref.at[side], mixed[side, step], block)

    def multiply(side, tile):
        start = tile * SUBLANES
        real = slice(start, start + SUBLANES)
        imag = slice(half + start, half + start + SUBLANES)
        filter_parts = []
        for step in range(count):
            c, d = known[side, step, real], known[side, step, imag]
            filter_parts.append((c, d - c, c + d))
        for part in range(2):
            lanes = slice(part * LANES, (part + 1) * LANES)
            data_parts = []
            for step in range(count):
                a, b = data[side, step, real, lanes], data[side, step, imag, lanes]
                data_parts.append((a + b, a, b))
            before = None
            for total in range(count):
                sums = None
                for step in range(total + 1):
                    pairs = zip(data_parts[step], filter_parts[total - step])
                    terms = [x * y for x, y in pairs]
                    sums = terms if sums is None else [x + y for x, y in zip(sums, terms)]
                both = (sums[0] - sums[2], sums[0] + sums[1])
                if before is None:
                    out = both
                elif side == 0:
                    out = (both[0] - before[1], both[1] + before[0])
                else:
                    out = (both[0] + before[1], both[1] - before[0])
                mixed[side, total, real, lanes] = out[0]
                mixed[side, total, imag, lanes] = out[1]
                before = both

    behind = [jnp.zeros((SUBLANES, LANES), jnp.float32)] * 2
    for step in range(count):
        for part in range(2):
            lanes = slice(part * LANES, (part + 1) * LANES)
            for offset in range(near):
                sender = part * places + step * near + offset
                edge = arrived[sender, rows + share :].astype(jnp.float32)
                first = first_products(edge, behind[part], weights)
                behind[part] = edge
                values = arrived[sender, : 2 * SUBLANES].astype(jnp.float32)
                top = jnp.where(row < 2, first, values[:SUBLANES])
                values = jnp.concatenate([top, values[SUBLANES:]], axis=0)
                start = offset * rows
                product[step, start : start + 2 * SUBLANES, lanes] = values.astype(product.dtype)
                product[step, start + 2 * SUBLANES : start + rows, lanes] = arrived[
                    sender, 2 * SUBLANES : rows
                ]
                start = offset * rows + part * share
                place = (step % 2) * LANES
                filters[step // 2, start : start + share, place : place + LANES] = arrived[
                    sender, rows : rows + share
                ]
        data[0, step] = forward(0, product[step])
        if step % 2:
            for side in range(2):
                both = forward(side, filters[step // 2])
                known[side, step - 1] = both[:, :LANES]
                known[side, step] = both[:, LANES:]

    for step in range(count):
        for tile in range(tiles):
            multiply(0, step * tiles + tile)
        data[1, step] = forward(1, product[step])

    for step in range(count):
        for tile in range(tiles):
            multiply(1, step * tiles + tile)
        partly[step] = backward(0, step)

    for step in range(count):
        result = (partly[step] + backward(1, step)).astype(ready.dtype)
        for part in range(2):
            for offset in range(near):
                ready[2 * (step * near + offset) + part] = result[
                    offset * rows : (offset + 1) * rows, part * LANES : (part + 1) * LANES
                ]


def convolve_whole(sent, short_weight, owner, rows, forward_table, inverse_table):
    senders, height, _ = sent.shape
    block = forward_table.shape[2]
    length = senders // 2 * rows
    count = length // block
    taps = short_weight.shape[1]
    return pl.pallas_call(
        whole_kernel,
        out_shape=jax.ShapeDtypeStruct((senders, rows, LANES), jnp.bfloat16),
        grid_spec=pltpu.PrefetchScalarGridSpec(
            num_scalar_prefetch=1,
            grid=(1,),
            in_specs=[
                pl.BlockSpec(memory_space=pltpu.VMEM),
                pl.BlockSpec(memory_space=pltpu.VMEM),
                pl.BlockSpec((3, taps, LANES), lambda i, owner: (0, 0, owner[0])),
                pl.BlockSpec(memory_space=pltpu.VMEM),
            ],
            out_specs=pl.BlockSpec(memory_space=pltpu.VMEM),
            scratch_shapes=[
                pltpu.VMEM((count, block, 2 * LANES), jnp.bfloat16),
                pltpu.VMEM((count // 2, block, 2 * LANES), jnp.bfloat16),
                pltpu.VMEM((2, count, block, 2 * LANES), jnp.float32),
                pltpu.VMEM((2, count, block, LANES), jnp.float32),
                pltpu.VMEM((2, count, block, 2 * LANES), jnp.float32),
                pltpu.VMEM((count, block, 2 * LANES), jnp.float32),
            ],
        ),
        compiler_params=pltpu.CompilerParams(vmem_limit_bytes=32 * MIB),
        cost_estimate=pl.CostEstimate(
            flops=40 * length * block * LANES,
            bytes_accessed=2 * senders * (height + rows) * LANES,
            transcendentals=0,
        ),
    )(owner.reshape(1), forward_table, inverse_table, short_weight, sent)


def exchange(value, axes):
    return lax.all_to_all(value, axes, split_axis=0, concat_axis=0, tiled=True)


def on_device(query_in, key_in, value_in, long_filter, short_weight, skip_gain):
    places = lax.axis_size("seq")
    parts = lax.axis_size("groups")
    group = lax.axis_index("groups").astype(jnp.int32)
    place = lax.axis_index("seq").astype(jnp.int32)
    rows, channels = key_in.shape
    length = places * rows
    block = BLOCK if length % BLOCK == 0 else rows
    rim = short_weight.shape[1] - 1
    owners = parts * places
    count = length // block
    aligned = (
        parts == 2
        and rim == 2
        and channels == owners * LANES
        and rows % 32 == 0
        and block % rows == 0
        and block == BLOCK
        and count in (2, 4, 8)
    )
    forward_table, inverse_table = half_tables(block) if aligned else transform_tables(block)
    forward_table = jnp.asarray(forward_table)
    inverse_table = jnp.asarray(inverse_table)
    if aligned:
        sent, edges = pack(
            query_in, key_in, value_in, long_filter, short_weight, group, owners, parts
        )
        received = exchange(sent, ("groups", "seq"))
        edges = from_behind(edges, "seq")
        prepared = prepare(sent, query_in, short_weight, skip_gain)
        received, edges, prepared = lax.optimization_barrier((received, edges, prepared))
        owner = group * places + place
        convolved = convolve_whole(
            received, short_weight, owner, rows, forward_table, inverse_table
        )
        convolved = exchange(convolved, ("seq", "groups"))
        return finish(
            convolved, prepared, sent, query_in, edges, short_weight, skip_gain
        )
    else:
        width = channels // places
        edges = jnp.stack([query_in[-rim:], key_in[-rim:], value_in[-rim:]])
        sent = long_filter.reshape(rows, places, width).transpose(1, 0, 2)
        spectra = filter_spectra(exchange(sent, "seq").reshape(length, width), forward_table)
        edges = from_behind(edges, "seq")
        product = products(key_in, value_in, edges, short_weight)
        sent = product.reshape(rows, places, width).transpose(1, 0, 2)
        received = exchange(sent, "seq").reshape(length, width)
        convolved = convolve(received, spectra, forward_table, inverse_table)
        convolved = exchange(convolved.reshape(places, rows, width), "seq")
        convolved = convolved.transpose(1, 0, 2).reshape(rows, channels // LANES, LANES)
        convolved = convolved.transpose(1, 0, 2)
        return gate(convolved, product, query_in, edges, short_weight, skip_gain)


def solution(mesh):
    placed = (
        P(("groups", "seq"), None),
        P(("groups", "seq"), None),
        P(("groups", "seq"), None),
        P("seq", None),
        P(),
        P(),
    )
    return jax.shard_map(
        on_device, mesh=mesh, in_specs=placed, out_specs=P(("groups", "seq"), None), check_vma=False
    )
```

```python
import functools

import jax
import jax.numpy as jnp
import ml_dtypes
import numpy as np
from jax import lax
from jax.experimental import pallas as pl
from jax.experimental.pallas import tpu as pltpu
from jax.sharding import PartitionSpec as P

LANES = 128
SUBLANES = 8
BLOCK = 256
UNROLLED = 8
MIB = 1 << 20


def from_behind(value, axis):
    count = lax.axis_size(axis)
    return lax.ppermute(value, axis, [(source, source + 1) for source in range(count - 1)])


def transform_tables(block):
    numbers = np.concatenate([np.arange(0, block, 2), np.arange(1, block, 2)])
    quarter = (2 * numbers[:, None] + 1) * np.arange(block)[None, :] % (4 * block)
    angle = quarter.astype(np.float64) * (2.0 * np.pi / (4 * block))
    table = np.concatenate([np.cos(angle), -np.sin(angle)], axis=0)

    def split(values):
        high = values.astype(ml_dtypes.bfloat16)
        low = (values - high.astype(np.float64)).astype(ml_dtypes.bfloat16)
        return np.concatenate([high, low], axis=0)

    return split(table), split(table.T / block)


def half_tables(block):
    forward, inverse = transform_tables(block)
    half = block // 2
    rows = np.arange(2 * block).reshape(2, 2, half).transpose(1, 0, 2).reshape(2, block)
    forward = forward.reshape(2, 2 * block, block)
    forward = np.stack([forward[:, rows[side]].reshape(2 * block, block) for side in range(2)])
    inverse = np.stack([inverse[:, rows[side]] for side in range(2)])
    return forward, inverse


def shifted(values, edge, steps):
    rolled = pltpu.roll(values, steps, 0)
    row = lax.broadcasted_iota(jnp.int32, values.shape, 0)
    for place in range(steps):
        source = edge[edge.shape[0] - steps + place : edge.shape[0] - steps + place + 1]
        rolled = jnp.where(row == place, jnp.broadcast_to(source, values.shape), rolled)
    return rolled


def featurize_inside(own, taps):
    result = taps[0:1] * own
    for offset in range(1, taps.shape[0]):
        result = result + taps[offset : offset + 1] * pltpu.roll(own, offset, 0)
    return result


def featurize(own, edge, taps):
    own = own.astype(jnp.float32)
    edge = edge.astype(jnp.float32)
    top = own[:SUBLANES]
    first = taps[0:1] * top
    for offset in range(1, taps.shape[0]):
        first = first + taps[offset : offset + 1] * shifted(top, edge, offset)
    return jnp.concatenate([first, featurize_inside(own, taps)[SUBLANES:]], axis=0)


def product_kernel(key_ref, value_ref, edge_ref, taps_ref, out_ref):
    for start in range(0, key_ref.shape[1], LANES):
        span = slice(start, start + LANES)
        k_short = featurize(key_ref[:, span], edge_ref[1, :, span], taps_ref[1, :, span])
        v_short = featurize(value_ref[:, span], edge_ref[2, :, span], taps_ref[2, :, span])
        out_ref[:, span] = (k_short * v_short).astype(out_ref.dtype)


def products(key_in, value_in, edges, short_weight):
    rows, channels = key_in.shape
    span = min(channels, 1024)
    taps = short_weight.shape[1]
    return pl.pallas_call(
        product_kernel,
        out_shape=jax.ShapeDtypeStruct((rows, channels), jnp.bfloat16),
        grid=(channels // span,),
        in_specs=[
            pl.BlockSpec((rows, span), lambda i: (0, i)),
            pl.BlockSpec((rows, span), lambda i: (0, i)),
            pl.BlockSpec((3, taps - 1, span), lambda i: (0, 0, i)),
            pl.BlockSpec((3, taps, span), lambda i: (0, 0, i)),
        ],
        out_specs=pl.BlockSpec((rows, span), lambda i: (0, i)),
        cost_estimate=pl.CostEstimate(
            flops=12 * rows * channels, bytes_accessed=6 * rows * channels, transcendentals=0
        ),
    )(key_in, value_in, edges, short_weight)


def gate_kernel(conv_ref, product_ref, query_ref, edge_ref, taps_ref, gain_ref, out_ref):
    for part in range(conv_ref.shape[0]):
        span = slice(part * LANES, (part + 1) * LANES)
        q_short = featurize(query_ref[:, span], edge_ref[0, :, span], taps_ref[0, :, span])
        mixed = conv_ref[part].astype(jnp.float32) + gain_ref[:, span] * product_ref[
            :, span
        ].astype(jnp.float32)
        out_ref[:, span] = (q_short * mixed).astype(out_ref.dtype)


def gate(convolved, product, query_in, edges, short_weight, skip_gain):
    rows, channels = query_in.shape
    span = min(channels, 1024)
    taps = short_weight.shape[1]
    across = pl.BlockSpec((rows, span), lambda i: (0, i))
    return pl.pallas_call(
        gate_kernel,
        out_shape=jax.ShapeDtypeStruct((rows, channels), jnp.bfloat16),
        grid=(channels // span,),
        in_specs=[
            pl.BlockSpec((span // LANES, rows, LANES), lambda i: (i, 0, 0)),
            across,
            across,
            pl.BlockSpec((3, taps - 1, span), lambda i: (0, 0, i)),
            pl.BlockSpec((3, taps, span), lambda i: (0, 0, i)),
            pl.BlockSpec((1, span), lambda i: (0, i)),
        ],
        out_specs=across,
        cost_estimate=pl.CostEstimate(
            flops=9 * rows * channels, bytes_accessed=8 * rows * channels, transcendentals=0
        ),
    )(convolved, product, query_in, edges, short_weight, skip_gain.reshape(1, channels))


def prepare_kernel(sent_ref, query_ref, taps_ref, gain_ref, short_ref, direct_ref):
    owners, rows, _ = short_ref.shape
    for owner in range(owners):
        lanes = slice(owner * LANES, (owner + 1) * LANES)
        q_short = featurize_inside(query_ref[:, lanes].astype(jnp.float32), taps_ref[0, :, lanes])
        product = sent_ref[owner, :rows].astype(jnp.float32)
        short_ref[owner] = q_short
        direct_ref[owner] = q_short * (gain_ref[:, lanes] * product)


def prepare(sent, query_in, short_weight, skip_gain):
    rows, channels = query_in.shape
    owners, height, _ = sent.shape
    near = min(owners, 8)
    span = near * LANES
    taps = short_weight.shape[1]
    out = pl.BlockSpec((near, rows, LANES), lambda i: (i, 0, 0))
    return pl.pallas_call(
        prepare_kernel,
        out_shape=(jax.ShapeDtypeStruct((owners, rows, LANES), jnp.float32),) * 2,
        grid=(owners // near,),
        in_specs=[
            pl.BlockSpec((near, height, LANES), lambda i: (i, 0, 0)),
            pl.BlockSpec((rows, span), lambda i: (0, i)),
            pl.BlockSpec((3, taps, span), lambda i: (0, 0, i)),
            pl.BlockSpec((1, span), lambda i: (0, i)),
        ],
        out_specs=(out, out),
        cost_estimate=pl.CostEstimate(
            flops=8 * rows * channels, bytes_accessed=12 * rows * channels, transcendentals=0
        ),
    )(sent, query_in, short_weight, skip_gain.reshape(1, channels))


def finish_kernel(
    places, conv_ref, short_ref, direct_ref, sent_ref, query_ref, edge_ref, taps_ref, gain_ref, out_ref,
    ready, sems,
):
    rows, channels = ready.shape
    tail = sent_ref.shape[1] - SUBLANES
    chunks = sems.shape[0]
    span = channels // chunks
    near = span // LANES
    row = lax.broadcasted_iota(jnp.int32, (SUBLANES, LANES), 0)

    def departure(chunk):
        columns = pl.ds(pl.multiple_of(chunk * span, span), span)
        return pltpu.make_async_copy(ready.at[:, columns], out_ref.at[:, columns], sems.at[chunk])

    @pl.loop(0, chunks)
    def _(chunk):
        for part in range(near):
            owner = chunk * near + part
            lanes = pl.ds(pl.multiple_of(owner * LANES, LANES), LANES)
            behind = edge_ref[:, lanes].astype(jnp.float32)
            own = sent_ref[owner, tail:].astype(jnp.float32)
            first = first_products(own, behind, tap_tiles(taps_ref, lanes))
            first = first.astype(jnp.bfloat16).astype(jnp.float32)
            product = sent_ref[owner, :SUBLANES].astype(jnp.float32)
            product = jnp.where(row < 2, first, product)

            weights = taps_ref[0, :, lanes]
            top = query_ref[:SUBLANES, lanes].astype(jnp.float32)
            one = jnp.where(row < 1, pltpu.roll(behind, 5, 0), pltpu.roll(top, 1, 0))
            two = jnp.where(row < 2, pltpu.roll(behind, 6, 0), pltpu.roll(top, 2, 0))
            top = weights[0:1] * top + weights[1:2] * one + weights[2:3] * two

            source = 2 * owner - jnp.where(owner >= places, 2 * places - 1, 0)
            convolved = conv_ref[source].astype(jnp.float32)
            top = top * convolved[:SUBLANES] + top * (gain_ref[:, lanes] * product)
            result = short_ref[owner] * convolved + direct_ref[owner]
            result = jnp.concatenate([top, result[SUBLANES:]], axis=0)
            ready[:, lanes] = result.astype(ready.dtype)
        departure(chunk).start()

    for chunk in range(chunks):
        departure(chunk).wait()


def finish(convolved, prepared, sent, query_in, edges, short_weight, skip_gain):
    rows, channels = query_in.shape
    chunks = max(1, channels // 512)
    here = pl.BlockSpec(memory_space=pltpu.VMEM)
    return pl.pallas_call(
        functools.partial(finish_kernel, sent.shape[0] // 2),
        out_shape=jax.ShapeDtypeStruct((rows, channels), jnp.bfloat16),
        in_specs=[here] * 8,
        out_specs=pl.BlockSpec(memory_space=pltpu.HBM),
        scratch_shapes=[
            pltpu.VMEM((rows, channels), jnp.bfloat16),
            pltpu.SemaphoreType.DMA((chunks,)),
        ],
        compiler_params=pltpu.CompilerParams(vmem_limit_bytes=8 * MIB),
        cost_estimate=pl.CostEstimate(
            flops=3 * rows * channels, bytes_accessed=12 * rows * channels, transcendentals=0
        ),
    )(
        convolved, *prepared, sent, query_in, edges, short_weight, skip_gain.reshape(1, channels)
    )


def tap_tiles(taps_ref, lanes):
    row = lax.broadcasted_iota(jnp.int32, (SUBLANES, LANES), 0)
    return [
        jnp.where(row < 4, taps_ref[1, tap : tap + 1, lanes], taps_ref[2, tap : tap + 1, lanes])
        for tap in range(taps_ref.shape[1])
    ]


def first_products(tile, behind, weights):
    row = lax.broadcasted_iota(jnp.int32, (SUBLANES, LANES), 0)
    joined = jnp.where(row % 4 >= 2, tile, behind)
    short = weights[0] * joined
    for tap in range(1, len(weights)):
        short = short + weights[tap] * pltpu.roll(joined, tap, 0)
    return pltpu.roll(short * pltpu.roll(short, 4, 0), 6, 0)


def pack_kernel(
    group_ref, query_ref, key_ref, value_ref, filter_ref, taps_ref, out_ref, edges_ref,
    query, key, value, filters, taps, packed, edges, in_sems, one_sems, out_sems,
):
    rows, channels = key.shape
    share = filters.shape[0]
    chunks = out_sems.shape[0]
    span = channels // chunks
    near = span // LANES
    start = pl.multiple_of(group_ref[0] * share, share)
    whole = [
        pltpu.make_async_copy(taps_ref, taps, one_sems.at[0]),
        pltpu.make_async_copy(query_ref.at[pl.ds(rows - SUBLANES, SUBLANES)], query, one_sems.at[1]),
    ]

    def arrivals(chunk):
        columns = pl.ds(pl.multiple_of(chunk * span, span), span)
        return [
            pltpu.make_async_copy(key_ref.at[:, columns], key.at[:, columns], in_sems.at[0, chunk]),
            pltpu.make_async_copy(
                value_ref.at[:, columns], value.at[:, columns], in_sems.at[1, chunk]
            ),
            pltpu.make_async_copy(
                filter_ref.at[pl.ds(start, share), columns],
                filters.at[:, columns],
                in_sems.at[2, chunk],
            ),
        ]

    def departure(chunk):
        owners = pl.ds(chunk * near, near)
        return pltpu.make_async_copy(packed.at[owners], out_ref.at[owners], out_sems.at[chunk])

    for copy in whole:
        copy.start()
    for chunk in range(chunks):
        for copy in arrivals(chunk):
            copy.start(priority=1 if chunk else 0)
    for copy in whole:
        copy.wait()
    row = lax.broadcasted_iota(jnp.int32, (SUBLANES, LANES), 0)

    @pl.loop(0, chunks)
    def _(chunk):
        for copy in arrivals(chunk):
            copy.wait()
        for part in range(near):
            span_here = pl.ds(pl.multiple_of(chunk * span + part * LANES, LANES), LANES)
            owner = chunk * near + part
            key_here = key[:, span_here].astype(jnp.float32)
            value_here = value[:, span_here].astype(jnp.float32)
            k_short = featurize_inside(key_here, taps[1, :, span_here])
            v_short = featurize_inside(value_here, taps[2, :, span_here])
            packed[owner, :rows] = (k_short * v_short).astype(packed.dtype)
            packed[owner, rows : rows + share] = filters[:, span_here]
            query_last = pltpu.roll(query[:, span_here].astype(jnp.float32), 4, 0)
            key_tile = jnp.where(
                row < 2,
                pltpu.roll(key_here[rows - SUBLANES :], 2, 0),
                pltpu.roll(key_here[:SUBLANES], 2, 0),
            )
            value_tile = jnp.where(
                row < 6,
                pltpu.roll(value_here[rows - SUBLANES :], 6, 0),
                pltpu.roll(value_here[:SUBLANES], 6, 0),
            )
            edge = jnp.where(row < 4, key_tile, value_tile)
            packed[owner, rows + share :] = edge.astype(packed.dtype)
            edge = jnp.where((row == 2) | (row == 3), query_last, edge)
            edges[:, span_here] = edge.astype(edges.dtype)
        departure(chunk).start()

    last = pltpu.make_async_copy(edges, edges_ref, one_sems.at[0])
    last.start()
    for chunk in range(chunks):
        departure(chunk).wait()
    last.wait()


def pack(query_in, key_in, value_in, long_filter, short_weight, group, owners, parts):
    rows, channels = key_in.shape
    chunks = max(1, channels // 1024)
    taps = short_weight.shape[1]
    share = rows // parts
    height = rows + share + SUBLANES
    here = pl.BlockSpec(memory_space=pltpu.HBM)
    return pl.pallas_call(
        pack_kernel,
        out_shape=(
            jax.ShapeDtypeStruct((owners, height, LANES), jnp.bfloat16),
            jax.ShapeDtypeStruct((SUBLANES, channels), jnp.bfloat16),
        ),
        in_specs=[pl.BlockSpec(memory_space=pltpu.SMEM)] + [here] * 5,
        out_specs=(here, here),
        scratch_shapes=[
            pltpu.VMEM((SUBLANES, channels), jnp.bfloat16),
            pltpu.VMEM((rows, channels), jnp.bfloat16),
            pltpu.VMEM((rows, channels), jnp.bfloat16),
            pltpu.VMEM((share, channels), jnp.bfloat16),
            pltpu.VMEM((3, taps, channels), jnp.float32),
            pltpu.VMEM((owners, height, LANES), jnp.bfloat16),
            pltpu.VMEM((SUBLANES, channels), jnp.bfloat16),
            pltpu.SemaphoreType.DMA((3, chunks)),
            pltpu.SemaphoreType.DMA((2,)),
            pltpu.SemaphoreType.DMA((chunks,)),
        ],
        cost_estimate=pl.CostEstimate(
            flops=12 * rows * channels, bytes_accessed=8 * rows * channels, transcendentals=0
        ),
    )(group.reshape(1), query_in, key_in, value_in, long_filter, short_weight)


def transform(table, values):
    both = jnp.dot(table, values, preferred_element_type=jnp.float32)
    half = table.shape[0] // 2
    return both[:half] + both[half:]


def over(count, body):
    if count <= UNROLLED:
        for step in range(count):
            body(step)
    else:

        @pl.loop(0, count)
        def _(step):
            body(step)


def filter_kernel(table_ref, filter_ref, out_ref):
    count, double, _ = out_ref.shape
    block = double // 2

    def body(step):
        start = step * block
        if not isinstance(step, int):
            start = pl.multiple_of(start, block)
        out_ref[step] = transform(table_ref[...], filter_ref[pl.ds(start, block), :])

    over(count, body)


def filter_spectra(long_filter, table):
    length, width = long_filter.shape
    block = table.shape[1]
    return pl.pallas_call(
        filter_kernel,
        out_shape=jax.ShapeDtypeStruct((length // block, 2 * block, width), jnp.float32),
        in_specs=[pl.BlockSpec(memory_space=pltpu.VMEM)] * 2,
        out_specs=pl.BlockSpec(memory_space=pltpu.VMEM),
        compiler_params=pltpu.CompilerParams(vmem_limit_bytes=40 * MIB),
        cost_estimate=pl.CostEstimate(
            flops=8 * length * block * width, bytes_accessed=10 * length * width, transcendentals=0
        ),
    )(table, long_filter)


def inverse(table_ref, values, block):
    high = values.astype(jnp.bfloat16)
    low = (values - high.astype(jnp.float32)).astype(jnp.bfloat16)
    return transform(table_ref[...], high) + jnp.dot(
        table_ref[:block], low, preferred_element_type=jnp.float32
    )


def conv_kernel(forward_ref, inverse_ref, product_ref, filter_ref, out_ref, data, mixed, last):
    count, double, width = filter_ref.shape
    block = double // 2
    lane_step = min(width, LANES)

    def piece(step):
        start = step * block
        return pl.ds(start if isinstance(step, int) else pl.multiple_of(start, block), block)

    def forward(step):
        data[step] = transform(forward_ref[...], product_ref[piece(step), :])

    over(count, forward)
    last[...] = jnp.zeros_like(last)

    @pl.loop(0, count)
    def _(total):
        for sign, base in ((1.0, 0), (-1.0, block // 2)):
            for column in range(0, width, lane_step):
                lanes = slice(column, column + lane_step)

                @pl.loop(0, block // 2 // SUBLANES)
                def _(index):
                    start = pl.multiple_of(base + index * SUBLANES, SUBLANES)
                    real = pl.ds(start, SUBLANES)
                    imag = pl.ds(pl.multiple_of(block + start, SUBLANES), SUBLANES)

                    def add(step, sums):
                        a, b = data[step, real, lanes], data[step, imag, lanes]
                        c = filter_ref[total - step, real, lanes]
                        d = filter_ref[total - step, imag, lanes]
                        return sums[0] + (a * c - b * d), sums[1] + (a * d + b * c)

                    zero = jnp.zeros((SUBLANES, lane_step), jnp.float32)
                    sum_real, sum_imag = lax.fori_loop(0, total + 1, add, (zero, zero))
                    mixed[real, lanes] = sum_real - sign * last[imag, lanes]
                    mixed[imag, lanes] = sum_imag + sign * last[real, lanes]
                    last[real, lanes] = sum_real
                    last[imag, lanes] = sum_imag

        out_ref[piece(total), :] = inverse(inverse_ref, mixed[...], block).astype(out_ref.dtype)


def convolve(product, spectra, forward_table, inverse_table):
    length, width = product.shape
    count, double, _ = spectra.shape
    return pl.pallas_call(
        conv_kernel,
        out_shape=jax.ShapeDtypeStruct((length, width), jnp.bfloat16),
        in_specs=[pl.BlockSpec(memory_space=pltpu.VMEM)] * 4,
        out_specs=pl.BlockSpec(memory_space=pltpu.VMEM),
        scratch_shapes=[
            pltpu.VMEM((count, double, width), jnp.float32),
            pltpu.VMEM((double, width), jnp.float32),
            pltpu.VMEM((double, width), jnp.float32),
        ],
        compiler_params=pltpu.CompilerParams(vmem_limit_bytes=56 * MIB),
        cost_estimate=pl.CostEstimate(
            flops=16 * length * double * width,
            bytes_accessed=12 * length * width,
            transcendentals=0,
        ),
    )(forward_table, inverse_table, product, spectra)


def whole_kernel(
    owner_ref, forward_ref, inverse_ref, taps_ref, arrived, ready,
    product, filters, data, known, mixed, partly,
):
    del owner_ref
    senders, rows, _ = ready.shape
    places = senders // 2
    share = rows // 2
    _, count, block, _ = data.shape
    half = block // 2
    near = block // rows
    tiles = half // SUBLANES // count
    row = lax.broadcasted_iota(jnp.int32, (SUBLANES, LANES), 0)
    weights = tap_tiles(taps_ref, slice(None))

    def forward(side, values):
        return transform(forward_ref[side], values)

    def backward(side, step):
        return inverse(inverse_ref.at[side], mixed[side, step], block)

    def multiply(side, tile):
        start = tile * SUBLANES
        real = slice(start, start + SUBLANES)
        imag = slice(half + start, half + start + SUBLANES)
        filter_parts = []
        for step in range(count):
            c, d = known[side, step, real], known[side, step, imag]
            filter_parts.append((c, d - c, c + d))
        for part in range(2):
            lanes = slice(part * LANES, (part + 1) * LANES)
            data_parts = []
            for step in range(count):
                a, b = data[side, step, real, lanes], data[side, step, imag, lanes]
                data_parts.append((a + b, a, b))
            before = None
            for total in range(count):
                sums = None
                for step in range(total + 1):
                    pairs = zip(data_parts[step], filter_parts[total - step])
                    terms = [x * y for x, y in pairs]
                    sums = terms if sums is None else [x + y for x, y in zip(sums, terms)]
                both = (sums[0] - sums[2], sums[0] + sums[1])
                if before is None:
                    out = both
                elif side == 0:
                    out = (both[0] - before[1], both[1] + before[0])
                else:
                    out = (both[0] + before[1], both[1] - before[0])
                mixed[side, total, real, lanes] = out[0]
                mixed[side, total, imag, lanes] = out[1]
                before = both

    behind = [jnp.zeros((SUBLANES, LANES), jnp.float32)] * 2
    for step in range(count):
        for part in range(2):
            lanes = slice(part * LANES, (part + 1) * LANES)
            for offset in range(near):
                sender = part * places + step * near + offset
                edge = arrived[sender, rows + share :].astype(jnp.float32)
                first = first_products(edge, behind[part], weights)
                behind[part] = edge
                values = arrived[sender, : 2 * SUBLANES].astype(jnp.float32)
                top = jnp.where(row < 2, first, values[:SUBLANES])
                values = jnp.concatenate([top, values[SUBLANES:]], axis=0)
                start = offset * rows
                product[step, start : start + 2 * SUBLANES, lanes] = values.astype(product.dtype)
                product[step, start + 2 * SUBLANES : start + rows, lanes] = arrived[
                    sender, 2 * SUBLANES : rows
                ]
                start = offset * rows + part * share
                place = (step % 2) * LANES
                filters[step // 2, start : start + share, place : place + LANES] = arrived[
                    sender, rows : rows + share
                ]
        data[0, step] = forward(0, product[step])
        if step % 2:
            for side in range(2):
                both = forward(side, filters[step // 2])
                known[side, step - 1] = both[:, :LANES]
                known[side, step] = both[:, LANES:]

    for step in range(count):
        for tile in range(tiles):
            multiply(0, step * tiles + tile)
        data[1, step] = forward(1, product[step])

    for step in range(count):
        for tile in range(tiles):
            multiply(1, step * tiles + tile)
        partly[step] = backward(0, step)

    for step in range(count):
        result = (partly[step] + backward(1, step)).astype(ready.dtype)
        for part in range(2):
            for offset in range(near):
                ready[2 * (step * near + offset) + part] = result[
                    offset * rows : (offset + 1) * rows, part * LANES : (part + 1) * LANES
                ]


def convolve_whole(sent, short_weight, owner, rows, forward_table, inverse_table):
    senders, height, _ = sent.shape
    block = forward_table.shape[2]
    length = senders // 2 * rows
    count = length // block
    taps = short_weight.shape[1]
    return pl.pallas_call(
        whole_kernel,
        out_shape=jax.ShapeDtypeStruct((senders, rows, LANES), jnp.bfloat16),
        grid_spec=pltpu.PrefetchScalarGridSpec(
            num_scalar_prefetch=1,
            grid=(1,),
            in_specs=[
                pl.BlockSpec(memory_space=pltpu.VMEM),
                pl.BlockSpec(memory_space=pltpu.VMEM),
                pl.BlockSpec((3, taps, LANES), lambda i, owner: (0, 0, owner[0])),
                pl.BlockSpec(memory_space=pltpu.VMEM),
            ],
            out_specs=pl.BlockSpec(memory_space=pltpu.VMEM),
            scratch_shapes=[
                pltpu.VMEM((count, block, 2 * LANES), jnp.bfloat16),
                pltpu.VMEM((count // 2, block, 2 * LANES), jnp.bfloat16),
                pltpu.VMEM((2, count, block, 2 * LANES), jnp.float32),
                pltpu.VMEM((2, count, block, LANES), jnp.float32),
                pltpu.VMEM((2, count, block, 2 * LANES), jnp.float32),
                pltpu.VMEM((count, block, 2 * LANES), jnp.float32),
            ],
        ),
        compiler_params=pltpu.CompilerParams(vmem_limit_bytes=32 * MIB),
        cost_estimate=pl.CostEstimate(
            flops=40 * length * block * LANES,
            bytes_accessed=2 * senders * (height + rows) * LANES,
            transcendentals=0,
        ),
    )(owner.reshape(1), forward_table, inverse_table, short_weight, sent)


def exchange(value, axes):
    return lax.all_to_all(value, axes, split_axis=0, concat_axis=0, tiled=True)


def on_device(query_in, key_in, value_in, long_filter, short_weight, skip_gain):
    places = lax.axis_size("seq")
    parts = lax.axis_size("groups")
    group = lax.axis_index("groups").astype(jnp.int32)
    place = lax.axis_index("seq").astype(jnp.int32)
    rows, channels = key_in.shape
    length = places * rows
    block = BLOCK if length % BLOCK == 0 else rows
    rim = short_weight.shape[1] - 1
    owners = parts * places
    count = length // block
    aligned = (
        parts == 2
        and rim == 2
        and channels == owners * LANES
        and rows % 32 == 0
        and block % rows == 0
        and block == BLOCK
        and count in (2, 4, 8)
    )
    forward_table, inverse_table = half_tables(block) if aligned else transform_tables(block)
    forward_table = jnp.asarray(forward_table)
    inverse_table = jnp.asarray(inverse_table)
    if aligned:
        sent, edges = pack(
            query_in, key_in, value_in, long_filter, short_weight, group, owners, parts
        )
        received = exchange(sent, ("groups", "seq"))
        edges = from_behind(edges, "seq")
        prepared = prepare(sent, query_in, short_weight, skip_gain)
        received, edges, prepared = lax.optimization_barrier((received, edges, prepared))
        owner = group * places + place
        convolved = convolve_whole(
            received, short_weight, owner, rows, forward_table, inverse_table
        )
        convolved = exchange(convolved, ("seq", "groups"))
        return finish(
            convolved, prepared, sent, query_in, edges, short_weight, skip_gain
        )
    else:
        width = channels // places
        edges = jnp.stack([query_in[-rim:], key_in[-rim:], value_in[-rim:]])
        sent = long_filter.reshape(rows, places, width).transpose(1, 0, 2)
        spectra = filter_spectra(exchange(sent, "seq").reshape(length, width), forward_table)
        edges = from_behind(edges, "seq")
        product = products(key_in, value_in, edges, short_weight)
        sent = product.reshape(rows, places, width).transpose(1, 0, 2)
        received = exchange(sent, "seq").reshape(length, width)
        convolved = convolve(received, spectra, forward_table, inverse_table)
        convolved = exchange(convolved.reshape(places, rows, width), "seq")
        convolved = convolved.transpose(1, 0, 2).reshape(rows, channels // LANES, LANES)
        convolved = convolved.transpose(1, 0, 2)
        return gate(convolved, product, query_in, edges, short_weight, skip_gain)


def solution(mesh):
    placed = (
        P(("groups", "seq"), None),
        P(("groups", "seq"), None),
        P(("groups", "seq"), None),
        P("seq", None),
        P(),
        P(),
    )
    return jax.shard_map(
        on_device, mesh=mesh, in_specs=placed, out_specs=P(("groups", "seq"), None), check_vma=False
    )
```
